32 devices in a mesh: tower: 2 (over x), dp: 16 (over z, y, core).
Axes of the slice: x: 2, y: 2, z: 4, core: 2. Of those that a mesh axis runs over, the one named last changes fastest.
Arguments:
- states: bfloat16 [2, 2, 8192, 768], P('tower', None, 'dp'), may hold values from -6 to 6
- segment_ids: int32 [2, 2, 8192], P('tower', None, 'dp'), may hold values from 0 to 8, as said below
- lengths: int32 [2, 2, 128], P('tower', None, 'dp'), may hold values from 16 to 96, as said below
- positives: int32 [2, 128], replicated, may hold values from 0 to 127
- w_query: bfloat16 [768, 768], replicated, may hold values from -0.078125 to 0.078125
- w_key: bfloat16 [768, 768], replicated, may hold values from -0.078125 to 0.078125
- w_value: bfloat16 [768, 768], replicated, may hold values from -0.21875 to 0.21875
- w_out: bfloat16 [768, 768], replicated, may hold values from -1.25 to 1.25
- w_in: bfloat16 [768, 3072], replicated, may hold values from -0.21875 to 0.21875
- w_ffout: bfloat16 [3072, 768], replicated, may hold values from -0.15625 to 0.15625
- w_proj: bfloat16 [768, 768], replicated, may hold values from -0.21875 to 0.21875
- gain_attn: float32 [768], replicated, may hold values from 0.5 to 1.5
- gain_ffn: float32 [768], replicated, may hold values from 0.5 to 1.5
- gain_final: float32 [768], replicated, may hold values from 0.5 to 1.5
- rel_bias: float32 [32, 12], replicated, may hold values from -6 to 6
Outputs:
- loss: float32 [], replicated
- embeddings: float32 [2, 2, 128, 768], P('tower', None, 'dp')
- d_states: float32 [2, 2, 8192, 768], P('tower', None, 'dp')
- grad_query: float32 [768, 768], replicated
- grad_key: float32 [768, 768], replicated
- grad_value: float32 [768, 768], replicated
- grad_out: float32 [768, 768], replicated
- grad_in: float32 [768, 3072], replicated
- grad_ffout: float32 [3072, 768], replicated
- grad_proj: float32 [768, 768], replicated
- grad_gain_attn: float32 [768], replicated
- grad_gain_ffn: float32 [768], replicated
- grad_gain_final: float32 [768], replicated
- grad_rel_bias: float32 [32, 12], replicated
The draws below stay inside these ranges and needn't reach their ends.
Inputs may be any that keep to these rules, and one draw needn't show every extreme that they name: `segment_ids`: in each device's row of 512 tokens: on tower index 0, query c (c < 8) holds the first lengths-many positions of slot c * 64 to (c + 1) * 64 - 1 and the rest of the slot has id 8; on tower index 1 passages 0 to 7 lie end to end in order and fill the row. Every item's count of positions equals its lengths entry. `lengths`: queries hold 16 to 64 tokens, query 0 of every row exactly 64; passages hold 32 to 96 tokens and sum to 512 in each row, passage 0 of every row exactly 96.
All inputs are finite; a program needn't handle non-finite values.
Results may differ from the reference program's by a relative error of at most 0.034.
The reference program's roundings to bfloat16 on the way count: a program that leaves them out, or rounds other values in their place, can miss the bound.
Values sent between devices are 32-bit elements; how exact they have to be, the bound alone decides.
No kernel may reach another device: no remote copies, remote signals or barrier semaphores. Data moves between devices by JAX's collectives and lax.ppermute only.
A program may use at most 256 MiB of HBM per device.

```python
import jax
import jax.numpy as jnp
from jax import lax

D = 768
HEADS = 12
HEAD = 64
FF = 3072
BUCKETS = 32
SEQ = 512
QLEN = 64
MB = 2
ITEMS = 8
ROWS = 128
TOKENS = 8192
N_TOWER = 2


def packing(key):
    blocks = ROWS // ITEMS
    base_key = jax.random.fold_in(key, 7177)
    query_key, passage_key = jax.random.split(base_key)
    query_len = jax.random.randint(query_key, (MB, blocks, ITEMS), QLEN // 4, QLEN + 1)
    query_len = query_len.at[:, :, 0].set(QLEN)
    half_len = QLEN // 2
    shifts = jax.random.randint(passage_key, (MB, blocks, ITEMS // 2), 0, half_len + 1)
    shifts = shifts.at[:, :, 0].set(half_len)
    passage_len = jnp.stack([QLEN + shifts, QLEN - shifts], axis=-1).reshape(MB, blocks, ITEMS)
    slot_start = jnp.broadcast_to(jnp.arange(ITEMS, dtype=jnp.int32) * QLEN, (MB, blocks, ITEMS))
    packed_start = jnp.cumsum(passage_len, axis=-1) - passage_len
    starts = jnp.stack([slot_start, packed_start], axis=0).astype(jnp.int32)
    counts = jnp.stack([query_len, passage_len], axis=0).astype(jnp.int32)
    where_at = jnp.arange(SEQ, dtype=jnp.int32)[None, None, None, :, None]
    inside = (where_at >= starts[:, :, :, None, :]) & (where_at < (starts + counts)[:, :, :, None, :])
    weights_id = (ITEMS - jnp.arange(ITEMS, dtype=jnp.int32))[None, None, None, None, :]
    segment = ITEMS - jnp.sum(inside.astype(jnp.int32) * weights_id, axis=-1)
    return (segment.reshape(2, MB, blocks * SEQ).astype(jnp.int32), counts.reshape(2, MB, blocks * ITEMS))


def draw_segment_ids(key, part):
    segment, counts = packing(key)
    return segment


def draw_lengths(key, part):
    segment, counts = packing(key)
    return counts


def set_ends(entries, rng, low, top_value):
    longest = entries.shape.index(max(entries.shape))
    spots = []
    for shift in (0, 1):
        where = [jax.random.randint(jax.random.fold_in(rng, axis), (), 0, length) for axis, length in enumerate(entries.shape)]
        where[longest] = (where[longest] + shift) % entries.shape[longest]
        spots.append(tuple(where))
    return entries.at[spots[0]].set(low).at[spots[1]].set(top_value)


def levels(own_key, shape, pieces, smallest, high):
    gain, own = 1.0, jax.random.fold_in(own_key, 6)
    for dim, blocks in pieces:
        steps = jnp.exp(jax.random.uniform(jax.random.fold_in(own, dim), (blocks,), jnp.float32, smallest / len(pieces), high / len(pieces)))
        gain = gain * jnp.repeat(steps, shape[dim] // blocks).reshape([-1 if axis == dim else 1 for axis in range(len(shape))])
    return gain


def bell_draw(stream_key, shape, spread, most, pieces=(), held_as=jnp.bfloat16):
    drawn = spread * jax.random.normal(stream_key, shape, jnp.float32)
    if pieces:
        drawn = drawn * levels(stream_key, shape, pieces, -0.22, 0.18)
    return jnp.clip(drawn, -most, most).astype(held_as)


def setup_inputs(seed: int = 0) -> dict:
    arg_keys = jax.random.split(jax.random.key(seed), 16)
    states = bell_draw(arg_keys[0], (N_TOWER, MB, TOKENS, D), 1.0, 6.0, ((0, 2), (2, 16)))
    segment_ids = draw_segment_ids(jax.random.fold_in(arg_keys[15], 71), 0)
    lengths = draw_lengths(jax.random.fold_in(arg_keys[15], 71), 0)
    positives = set_ends(jax.random.randint(arg_keys[3], (MB, ROWS), 0, ROWS), jax.random.fold_in(arg_keys[3], 1), 0, ROWS - 1).astype(jnp.int32)
    w_query = bell_draw(arg_keys[4], (D, D), (8 * D) ** -0.5, 0.078125)
    w_key = bell_draw(arg_keys[5], (D, D), (8 * D) ** -0.5, 0.078125)
    w_value = bell_draw(arg_keys[6], (D, D), D ** -0.5, 0.21875)
    w_out = bell_draw(arg_keys[7], (D, D), (D // 32) ** -0.5, 1.25)
    w_in = bell_draw(arg_keys[8], (D, FF), D ** -0.5, 0.21875)
    w_ffout = bell_draw(arg_keys[9], (FF, D), (FF // 2) ** -0.5, 0.15625)
    w_proj = bell_draw(arg_keys[10], (D, D), D ** -0.5, 0.21875)
    gain_attn = jnp.clip(1.0 + 0.1 * jax.random.normal(arg_keys[11], (D,), jnp.float32), 0.5, 1.5)
    gain_ffn = jnp.clip(1.0 + 0.1 * jax.random.normal(arg_keys[12], (D,), jnp.float32), 0.5, 1.5)
    gain_final = jnp.clip(1.0 + 0.1 * jax.random.normal(arg_keys[13], (D,), jnp.float32), 0.5, 1.5)
    rel_bias = bell_draw(arg_keys[14], (BUCKETS, HEADS), 1.0, 6.0, (), jnp.float32)
    return dict(states=states, segment_ids=segment_ids, lengths=lengths, positives=positives, w_query=w_query, w_key=w_key, w_value=w_value, w_out=w_out, w_in=w_in, w_ffout=w_ffout, w_proj=w_proj, gain_attn=gain_attn, gain_ffn=gain_ffn, gain_final=gain_final, rel_bias=rel_bias)


@jax.custom_vjp
def low(v):
    return lax.optimization_barrier(v.astype(jnp.bfloat16)).astype(jnp.float32)

@jax.custom_vjp
def low_back(v):
    return v

def low_keep(v):
    return (low(v), None)

def low_pass(kept, grad):
    return (grad,)

def back_keep(v):
    return (v, None)

def back_low(kept, grad):
    return (low(grad),)
low.defvjp(low_keep, low_pass)
low_back.defvjp(back_keep, back_low)
highest = lax.Precision.HIGHEST
norm_epsilon = 1e-06
logit_scale = 50.0
bucket_edges = (12, 16, 23, 32, 46, 64, 91)

def bucket_table(length):
    where_at = jnp.arange(length, dtype=jnp.int32)
    offset = where_at[None, :] - where_at[:, None]
    distance = jnp.abs(offset)
    far_bucket = jnp.full_like(distance, 8)
    for edge_value in bucket_edges:
        far_bucket = far_bucket + (distance >= edge_value).astype(jnp.int32)
    near_far = jnp.where(distance < 8, distance, far_bucket)
    return (near_far + jnp.where(offset > 0, 16, 0)).astype(jnp.int32)

def rms_scale(values, gain_vec):
    return values * lax.rsqrt(lax.optimization_barrier(jnp.mean(values * values, axis=-1, keepdims=True)) + norm_epsilon) * gain_vec

def unit_rows(values):
    return values * lax.rsqrt(lax.optimization_barrier(jnp.sum(values * values, axis=-1, keepdims=True)) + norm_epsilon)

def block_forward(params, block_inputs):
    w_query, w_key, w_value, w_out, w_in, w_ffout, w_proj, gain_attn, gain_ffn, gain_final, rel_bias = params
    states_blk, segment, counts = block_inputs
    length = states_blk.shape[0]
    normed = low(rms_scale(states_blk, gain_attn))

    def project(weight):
        return low(low_back(jnp.dot(normed, weight, precision=highest))).reshape(length, HEADS, HEAD)
    query_h = project(w_query)
    key_h = project(w_key)
    value_h = project(w_value)
    bucket = bucket_table(length)
    bias_map = jnp.transpose(rel_bias[bucket], (2, 0, 1))
    scores = jnp.einsum('qhd,khd->hqk', query_h, key_h, precision=highest) + bias_map
    scores = low_back(scores)
    same_seg = segment[:, None] == segment[None, :]
    scores = jnp.where(same_seg[None], scores, -1000000000.0)
    maxima = lax.optimization_barrier(jnp.max(scores, axis=-1, keepdims=True))
    expo_vals = jnp.exp(scores - maxima)
    probs_full = expo_vals / lax.optimization_barrier(jnp.sum(expo_vals, axis=-1, keepdims=True))
    mixed = jnp.einsum('hqk,khd->qhd', low(probs_full), value_h, precision=highest).reshape(length, D)
    mixed = low(low_back(mixed))
    hidden = states_blk + low_back(jnp.dot(mixed, w_out, precision=highest))
    normed_two = low(rms_scale(hidden, gain_ffn))
    inner = low_back(jnp.dot(normed_two, w_in, precision=highest))
    activ = low(jnp.maximum(inner, 0.0))
    output = hidden + low_back(jnp.dot(activ, w_ffout, precision=highest))
    final_norm = rms_scale(output, gain_final)
    member = (segment[:, None] == jnp.arange(ITEMS, dtype=jnp.int32)[None, :]).astype(jnp.float32)
    pooled = jnp.dot(member.T, final_norm, precision=highest) / counts.astype(jnp.float32)[:, None]
    embed = low_back(jnp.dot(low(pooled), w_proj, precision=highest))
    return unit_rows(embed)

def contrast(embeds, targets):
    logits = logit_scale * jnp.dot(embeds[0], embeds[1].T, precision=highest)
    maxima = lax.optimization_barrier(jnp.max(logits, axis=1, keepdims=True))
    log_total = maxima[:, 0] + jnp.log(lax.optimization_barrier(jnp.sum(jnp.exp(logits - maxima), axis=1)))
    picked = jnp.take_along_axis(logits, targets[:, None].astype(jnp.int32), axis=1)[:, 0]
    return jnp.sum(log_total - picked)

def reference(states, segment_ids, lengths, positives, w_query, w_key, w_value, w_out, w_in, w_ffout, w_proj, gain_attn, gain_ffn, gain_final, rel_bias):
    blocks = ROWS // ITEMS
    states_f = states.astype(jnp.float32).reshape(2, MB, blocks, SEQ, D)
    states_f = jnp.transpose(states_f, (1, 0, 2, 3, 4)).reshape(MB, 2 * blocks, SEQ, D)
    segment_all = jnp.transpose(segment_ids.reshape(2, MB, blocks, SEQ), (1, 0, 2, 3)).reshape(MB, 2 * blocks, SEQ)
    counts_all = jnp.transpose(lengths.reshape(2, MB, blocks, ITEMS), (1, 0, 2, 3)).reshape(MB, 2 * blocks, ITEMS)
    params = (w_query.astype(jnp.float32), w_key.astype(jnp.float32), w_value.astype(jnp.float32), w_out.astype(jnp.float32), w_in.astype(jnp.float32), w_ffout.astype(jnp.float32), w_proj.astype(jnp.float32), gain_attn, gain_ffn, gain_final, rel_bias)

    def total(states_in, params_in):

        def one_block(block_inputs):
            return block_forward(params_in, block_inputs)
        checked = jax.checkpoint(one_block)

        def micro_step(carry, micro_inputs):
            states_mb, segment_mb, counts_mb, targets = micro_inputs
            embeds = lax.map(checked, (states_mb, segment_mb, counts_mb)).reshape(2, ROWS, D)
            return (carry + contrast(embeds, targets), embeds)
        loss_sum, embeds_all = lax.scan(micro_step, jnp.zeros((), jnp.float32), (states_in, segment_all, counts_all, positives))
        return (loss_sum, embeds_all)
    loss_sum, pullback, embeds_all = jax.vjp(total, states_f, params, has_aux=True)
    grad_states, grad_params = pullback(jnp.ones((), jnp.float32))
    loss = loss_sum / (MB * ROWS)
    embeddings = jnp.transpose(embeds_all, (1, 0, 2, 3))
    d_states = jnp.transpose(grad_states.reshape(MB, 2, blocks, SEQ, D), (1, 0, 2, 3, 4)).reshape(2, MB, blocks * SEQ, D)
    return (loss, embeddings, d_states, grad_params[0], grad_params[1], grad_params[2], grad_params[3], grad_params[4], grad_params[5], grad_params[6], grad_params[7], grad_params[8], grad_params[9], grad_params[10])
```

```python
import jax
import jax.numpy as jnp
from jax import lax
from jax.sharding import PartitionSpec as P

highest = lax.Precision.HIGHEST
norm_epsilon = 1e-06
logit_scale = 50.0
bucket_edges = (12, 16, 23, 32, 46, 64, 91)
AXES = ("tower", "dp")


def bucket_table(length):
    where_at = jnp.arange(length, dtype=jnp.int32)
    offset = where_at[None, :] - where_at[:, None]
    distance = jnp.abs(offset)
    far_bucket = jnp.full_like(distance, 8)
    for edge_value in bucket_edges:
        far_bucket = far_bucket + (distance >= edge_value).astype(jnp.int32)
    near_far = jnp.where(distance < 8, distance, far_bucket)
    return near_far + jnp.where(offset > 0, 16, 0)


def rms_scale(values, gain_vec):
    return (
        values
        * lax.rsqrt(jnp.mean(values * values, axis=-1, keepdims=True) + norm_epsilon)
        * gain_vec
    )


def unit_rows(values):
    return values * lax.rsqrt(jnp.sum(values * values, axis=-1, keepdims=True) + norm_epsilon)


def softmax_terms(logits, target_hot):
    maxima = jnp.max(logits, axis=1, keepdims=True)
    log_total = maxima + jnp.log(jnp.sum(jnp.exp(logits - maxima), axis=1, keepdims=True))
    loss_part = jnp.sum(log_total[:, 0] - jnp.sum(logits * target_hot, axis=1))
    return (loss_part, jnp.exp(logits - log_total) - target_hot)


def mm(a, b):
    return jnp.dot(a, b, preferred_element_type=jnp.float32)


def mm_t(a, b):
    return lax.dot_general(a, b, (((1,), (1,)), ((), ())), preferred_element_type=jnp.float32)


def t_mm(a, b):
    return lax.dot_general(a, b, (((0,), (0,)), ((), ())), preferred_element_type=jnp.float32)


class Net:
    def __init__(self):
        self.dp = lax.axis_size("dp")
        self.size = self.dp * lax.axis_size("tower")
        self.index = lax.axis_index("tower") * self.dp + lax.axis_index("dp")

    def bit(self, b):
        return (self.index >> b) & 1

    def swap(self, value, b):
        return lax.ppermute(value, AXES, [(i, i ^ (1 << b)) for i in range(self.size)])


def join(own, other, bit):
    first = jnp.where(bit == 0, own, other)
    second = jnp.where(bit == 0, other, own)
    return jnp.concatenate([first, second], axis=0)


def half_of(value, which):
    rows = value.shape[0] // 2
    return lax.dynamic_slice_in_dim(value, which * rows, rows, 0)


def scatter_sum(net, sent, kept, order):
    got = net.swap(sent, order[0])
    for b in order[1:]:
        bit = net.bit(b)
        sent = half_of(kept, 1 - bit) + half_of(got, 1 - bit)
        kept = half_of(kept, bit) + half_of(got, bit)
        got = net.swap(sent, b)
    return kept + got


def gather_all(net, piece, order):
    for b in reversed(order):
        piece = join(piece, net.swap(piece, b), net.bit(b))
    return piece


def sum_small(net, value, order):
    for b in order:
        value = value + net.swap(value, b)
    return value


def local(
    states,
    segment_ids,
    lengths,
    positives,
    w_query,
    w_key,
    w_value,
    w_out,
    w_in,
    w_ffout,
    w_proj,
    gain_attn,
    gain_ffn,
    gain_final,
    rel_bias,
):
    micro_count = states.shape[1]
    length = states.shape[2]
    model_width = states.shape[3]
    item_count = lengths.shape[2]
    bucket_count, head_count = rel_bias.shape
    head_dim = model_width // head_count
    ff_width = w_in.shape[1]
    tower_index = lax.axis_index("tower")
    dp_index = lax.axis_index("dp")
    dp_count = lax.axis_size("dp")
    row_count = item_count * dp_count
    rows = micro_count * length
    net = Net()
    bits = net.size.bit_length() - 1
    core = 0
    chips = tuple(range(1, bits))
    gather_order = (0, 4, 1, 2, 3) if bits == 5 else tuple(range(bits))

    bucket = bucket_table(length)
    code_full = (
        bucket[:, :, None] == jnp.arange(bucket_count, dtype=jnp.int32)[None, None, :]
    ).astype(jnp.float32)
    bias_map = jnp.einsum("qkb,bh->hqk", code_full, rel_bias, precision=highest)
    code_low = code_full.astype(jnp.bfloat16)

    segment = segment_ids[0]
    same_seg = segment[:, :, None] == segment[:, None, :]

    def heads(value):
        return value.reshape(micro_count, length, head_count, head_dim)

    states_f = states[0].reshape(rows, model_width).astype(jnp.float32)
    normed, back_attn = jax.vjp(rms_scale, states_f, gain_attn)
    normed_low = normed.astype(jnp.bfloat16)
    query_h = heads(mm(normed_low, w_query).astype(jnp.bfloat16))
    key_h = heads(mm(normed_low, w_key).astype(jnp.bfloat16))
    value_h = heads(mm(normed_low, w_value).astype(jnp.bfloat16))

    def scores_of():
        raw = (
            jnp.einsum("bqhd,bkhd->bhqk", query_h, key_h, preferred_element_type=jnp.float32)
            + bias_map[None]
        )
        return jnp.where(same_seg[:, None], raw, -1000000000.0)

    scores = scores_of()
    maxima = jnp.max(scores, axis=-1, keepdims=True)
    expo_vals = jnp.exp(scores - maxima)
    row_total = jnp.sum(expo_vals, axis=-1, keepdims=True)
    log_norm = maxima + jnp.log(row_total)
    probs_low = (expo_vals / row_total).astype(jnp.bfloat16)
    mixed_low = (
        jnp.einsum("bhqk,bkhd->bqhd", probs_low, value_h, preferred_element_type=jnp.float32)
        .reshape(rows, model_width)
        .astype(jnp.bfloat16)
    )
    hidden = states_f + mm(mixed_low, w_out)
    normed_two, back_ffn = jax.vjp(rms_scale, hidden, gain_ffn)
    normed_two_low = normed_two.astype(jnp.bfloat16)
    inner = mm(normed_two_low, w_in)
    activ_low = jnp.maximum(inner, 0.0).astype(jnp.bfloat16)
    output = hidden + mm(activ_low, w_ffout)
    final_norm, back_final = jax.vjp(rms_scale, output, gain_final)
    member = (segment[:, :, None] == jnp.arange(item_count, dtype=jnp.int32)).astype(jnp.float32)
    count_f = lengths[0].astype(jnp.float32)[:, :, None]
    pooled_low = (
        jnp.einsum(
            "btc,btf->bcf",
            member,
            final_norm.reshape(micro_count, length, model_width),
            precision=highest,
        )
        / count_f
    ).astype(jnp.bfloat16)
    pooled_flat = pooled_low.reshape(micro_count * item_count, model_width)
    embed = mm(pooled_flat, w_proj)
    unit_embed, back_unit = jax.vjp(unit_rows, embed)

    every = unit_embed[None]
    for b in reversed(gather_order):
        every = join(every, net.swap(every, b), net.bit(b))
    every = every.reshape((2,) * bits + (micro_count, item_count, model_width))
    place = [bits - 1 - b for b in gather_order]
    every = jnp.transpose(
        every,
        [bits]
        + [gather_order.index(b) for b in reversed(range(bits))]
        + [bits + 1, bits + 2],
    ).reshape(micro_count, 2, row_count, model_width)
    queries_all = every[:, 0]
    passages_all = every[:, 1]
    columns = jnp.arange(row_count, dtype=jnp.int32)[None, :]
    loss_sum = jnp.zeros((), jnp.float32)
    grad_embed = []
    for m in range(micro_count):
        logits = logit_scale * jnp.dot(queries_all[m], passages_all[m].T, precision=highest)
        target_hot = (columns == positives[m][:, None]).astype(jnp.float32)
        loss_part, grad_logits = softmax_terms(logits, target_hot)
        loss_sum = loss_sum + loss_part
        own_rows = lax.dynamic_slice_in_dim(grad_logits, dp_index * item_count, item_count, 0)
        own_cols = lax.dynamic_slice_in_dim(grad_logits, dp_index * item_count, item_count, 1)
        own = jnp.where(tower_index == 0, own_rows, own_cols.T)
        others = jnp.where(tower_index == 0, passages_all[m], queries_all[m])
        grad_embed.append(logit_scale * jnp.dot(own, others, precision=highest))
    grad_embed = jnp.concatenate(grad_embed, axis=0)
    (grad_e,) = back_unit(grad_embed)
    grad_e_low = grad_e.astype(jnp.bfloat16)
    grad_pooled = mm_t(grad_e_low, w_proj).reshape(micro_count, item_count, model_width)
    grad_final_norm = jnp.einsum(
        "btc,bcf->btf", member, grad_pooled / count_f, precision=highest
    ).reshape(rows, model_width)
    grad_output, grad_gain_final = back_final(grad_final_norm)
    grad_output_low = grad_output.astype(jnp.bfloat16)

    def halves(left, right, core_bit):
        wide = left.shape[1] // 2
        other = t_mm(
            lax.dynamic_slice_in_dim(left, (1 - core_bit) * wide, wide, 1), right
        )
        own = t_mm(lax.dynamic_slice_in_dim(left, core_bit * wide, wide, 1), right)
        return other, own

    core_bit = net.bit(core)
    if bits == 5:
        orders = (((0, 4, 1, 2, 3), (0, 1, 4, 2, 3)), ((0, 4, 2, 3, 1), (0, 1, 2, 3, 4)))
    else:
        orders = ((tuple(range(bits)),) * 2,) * 2

    def total(left, right, order):
        sent, kept = halves(left, right, core_bit)
        return gather_all(net, scatter_sum(net, sent, kept, order), order)

    ff_half = ff_width // 2
    whole_ffout = jnp.concatenate(
        [
            total(activ_low[:, :ff_half], grad_output_low, orders[0][0]),
            total(activ_low[:, ff_half:], grad_output_low, orders[0][1]),
        ],
        axis=0,
    )
    grad_activ = mm_t(grad_output_low, w_ffout)
    grad_inner_low = jnp.where(inner > 0, grad_activ, 0.0).astype(jnp.bfloat16)
    whole_in = jnp.concatenate(
        [
            total(normed_two_low, grad_inner_low[:, :ff_half], orders[1][0]),
            total(normed_two_low, grad_inner_low[:, ff_half:], orders[1][1]),
        ],
        axis=1,
    )
    grad_normed_two = mm_t(grad_inner_low, w_in)
    grad_hidden_norm, grad_gain_ffn = back_ffn(grad_normed_two)
    grad_hidden = grad_output + grad_hidden_norm
    grad_hidden_low = grad_hidden.astype(jnp.bfloat16)
    grad_mixed = heads(mm_t(grad_hidden_low, w_out).astype(jnp.bfloat16))
    probs_full = jnp.exp(scores_of() - log_norm)
    grad_probs = jnp.einsum(
        "bqhd,bkhd->bhqk", grad_mixed, value_h, preferred_element_type=jnp.float32
    )
    grad_scores = (
        probs_full * (grad_probs - jnp.sum(probs_full * grad_probs, axis=-1, keepdims=True))
    ).astype(jnp.bfloat16)

    def flat(value):
        return value.reshape(rows, model_width).astype(jnp.bfloat16)

    grad_query_h = flat(
        jnp.einsum("bhqk,bkhd->bqhd", grad_scores, key_h, preferred_element_type=jnp.float32)
    )
    grad_key_h = flat(
        jnp.einsum("bhqk,bqhd->bkhd", grad_scores, query_h, preferred_element_type=jnp.float32)
    )
    grad_value_h = flat(
        jnp.einsum(
            "bhqk,bqhd->bkhd",
            probs_full.astype(jnp.bfloat16),
            grad_mixed,
            preferred_element_type=jnp.float32,
        )
    )
    grad_bias = jnp.einsum(
        "hqk,qkn->nh", jnp.sum(grad_scores.astype(jnp.float32), axis=0), code_full,
    )
    grad_qkv = jnp.concatenate([grad_query_h, grad_key_h, grad_value_h], axis=1)
    grad_normed = (
        mm_t(grad_query_h, w_query) + mm_t(grad_key_h, w_key) + mm_t(grad_value_h, w_value)
    )
    cut = model_width // 2
    first_sent, first_kept = halves(normed_low, grad_qkv[:, : 5 * cut], core_bit)
    rest = [
        halves(normed_low, grad_qkv[:, 5 * cut :], core_bit),
        halves(mixed_low, grad_hidden_low, core_bit),
        halves(pooled_flat, grad_e_low, core_bit),
    ]
    last_sent = jnp.concatenate([r[0] for r in rest], axis=1)
    last_kept = jnp.concatenate([r[1] for r in rest], axis=1)
    order = orders[0][0]
    whole_first = gather_all(net, scatter_sum(net, first_sent, first_kept, order), order)
    order = orders[0][1]
    whole_last = gather_all(net, scatter_sum(net, last_sent, last_kept, order), order)

    grad_states_norm, grad_gain_attn = back_attn(grad_normed)
    grad_states = grad_hidden + grad_states_norm
    small = jnp.concatenate(
        [
            grad_gain_attn,
            grad_gain_ffn,
            grad_gain_final,
            grad_bias.reshape(-1),
            jnp.zeros((model_width - bucket_count * head_count,), jnp.float32),
        ]
    ).reshape(-1, 128)
    small = sum_small(net, small, tuple(range(bits))).reshape(-1)
    loss = loss_sum / (micro_count * row_count)
    width = model_width
    return (
        loss,
        unit_embed.reshape(1, micro_count, item_count, model_width),
        grad_states.reshape(1, micro_count, length, model_width),
        whole_first[:, :width],
        whole_first[:, width : 2 * width],
        jnp.concatenate([whole_first[:, 2 * width :], whole_last[:, :cut]], axis=1),
        whole_last[:, cut : cut + width],
        whole_in,
        whole_ffout,
        whole_last[:, cut + width :],
        small[:width],
        small[width : 2 * width],
        small[2 * width : 3 * width],
        small[3 * width : 3 * width + bucket_count * head_count].reshape(
            bucket_count, head_count
        ),
    )


def solution(mesh):
    return jax.shard_map(
        local,
        mesh=mesh,
        in_specs=(
            P("tower", None, "dp", None),
            P("tower", None, "dp"),
            P("tower", None, "dp"),
        )
        + (P(),) * 12,
        out_specs=(P(), P("tower", None, "dp", None), P("tower", None, "dp", None)) + (P(),) * 11,
        check_vma=False,
    )
```

```python
import jax
import jax.numpy as jnp
from jax import lax
from jax.experimental import pallas as pl
from jax.experimental.pallas import tpu as pltpu
from jax.sharding import PartitionSpec as P

highest = lax.Precision.HIGHEST
norm_epsilon = 1e-06
logit_scale = 50.0
bucket_edges = (12, 16, 23, 32, 46, 64, 91)
AXES = ("tower", "dp")
LANES = 128


def bucket_code(offset, bucket_count):
    distance = jnp.abs(offset)
    far_bucket = jnp.full_like(distance, 8)
    for edge_value in bucket_edges:
        far_bucket = far_bucket + (distance >= edge_value).astype(jnp.int32)
    bucket = jnp.where(distance < 8, distance, far_bucket) + jnp.where(offset > 0, 16, 0)
    return (bucket[:, None] == jnp.arange(bucket_count, dtype=jnp.int32)[None, :]).astype(jnp.float32)


def rms_scale(values, gain_vec):
    return (
        values
        * lax.rsqrt(jnp.mean(values * values, axis=-1, keepdims=True) + norm_epsilon)
        * gain_vec
    )


def unit_rows(values):
    return values * lax.rsqrt(jnp.sum(values * values, axis=-1, keepdims=True) + norm_epsilon)


def softmax_terms(logits, target_hot):
    maxima = jnp.max(logits, axis=1, keepdims=True)
    log_total = maxima + jnp.log(jnp.sum(jnp.exp(logits - maxima), axis=1, keepdims=True))
    loss_part = jnp.sum(log_total[:, 0] - jnp.sum(logits * target_hot, axis=1))
    return (loss_part, jnp.exp(logits - log_total) - target_hot)


def mm(a, b):
    return jnp.dot(a, b, preferred_element_type=jnp.float32)


def mm_t(a, b):
    return lax.dot_general(a, b, (((1,), (1,)), ((), ())), preferred_element_type=jnp.float32)


def t_mm(a, b):
    return lax.dot_general(a, b, (((0,), (0,)), ((), ())), preferred_element_type=jnp.float32)


def dot_nt(a, b):
    return lax.dot_general(a, b, (((1,), (1,)), ((), ())), preferred_element_type=jnp.float32)

def dot_tn(a, b):
    return lax.dot_general(a, b, (((0,), (0,)), ((), ())), preferred_element_type=jnp.float32)

def dot_nn(a, b):
    return lax.dot_general(a, b, (((1,), (0,)), ((), ())), preferred_element_type=jnp.float32)


def head_parts(value, head_dim):
    lane = lax.broadcasted_iota(jnp.int32, value.shape, 1)
    zero = jnp.zeros_like(value)
    return [
        jnp.where((lane >= a * head_dim) & (lane < (a + 1) * head_dim), value, zero)
        for a in range(value.shape[1] // head_dim)
    ]


def diagonals(row):
    wide = jnp.broadcast_to(row, (LANES, row.shape[1]))
    return pltpu.roll(wide, 0, 1, stride=1, stride_axis=0)


def forward_kernel(head_dim, q_ref, k_ref, v_ref, segc_ref, segr_ref, rows_ref, o_ref, diag_ref):
    length, width = q_ref.shape
    group = width // head_dim
    tiles = length // LANES

    @pl.when(pl.program_id(1) == 0)
    def _():
        for a in range(group):
            diag_ref[a] = diagonals(rows_ref[a])

    keys = head_parts(k_ref[...], head_dim)
    values = head_parts(v_ref[...], head_dim)
    segr = segr_ref[...]
    for t in range(tiles):
        here = slice(t * LANES, (t + 1) * LANES)
        query = q_ref[here, :]
        same = segc_ref[here, :] == segr
        total = None
        for a in range(group):
            s = dot_nt(query, keys[a])
            s = s + diag_ref[a, :, LANES * (tiles - t) : LANES * (tiles - t) + length]
            s = jnp.where(same, s, -1000000000.0)
            e = jnp.exp(s - jnp.max(s, axis=1, keepdims=True))
            p = e * (1.0 / jnp.sum(e, axis=1, keepdims=True))
            part = dot_nn(p.astype(jnp.bfloat16), values[a])
            total = part if total is None else total + part
        o_ref[here, :] = total.astype(o_ref.dtype)


def fold_diagonals(value):
    n = value.shape[1]
    rows = value.shape[0]
    while rows > 1:
        rows //= 2
        value = value[:rows] + pltpu.roll(value[rows:], n - rows, 1)
    return value


def backward_kernel(head_dim, q_ref, k_ref, v_ref, g_ref, segc_ref, segr_ref, rows_ref,
                    gq_ref, gk_ref, gv_ref, gb_ref, diag_ref, fold_ref):
    length, width = q_ref.shape
    group = width // head_dim
    tiles = length // LANES
    micro = pl.program_id(1)

    @pl.when(micro == 0)
    def _():
        for a in range(group):
            diag_ref[a] = diagonals(rows_ref[a])
        fold_ref[...] = jnp.zeros_like(fold_ref)

    keys = head_parts(k_ref[...], head_dim)
    values = head_parts(v_ref[...], head_dim)
    segc = segc_ref[...]
    chunk = 2 * LANES
    gk = [None]
    gv = [None]
    for c in range(length // chunk):
        here = slice(c * chunk, (c + 1) * chunk)
        query = q_ref[here, :]
        grad = g_ref[here, :]
        query_parts = head_parts(query, head_dim)
        grad_parts = head_parts(grad, head_dim)
        same = segc == segr_ref[:, here]
        gq = None
        for a in range(group):
            s = dot_nt(keys[a], query)
            bias = jnp.concatenate(
                [
                    diag_ref[a, :, LANES * (tiles - t) + c * chunk : LANES * (tiles - t) + (c + 1) * chunk]
                    for t in range(tiles)
                ],
                axis=0,
            )
            s = jnp.where(same, s + bias, -1000000000.0)
            e = jnp.exp(s - jnp.max(s, axis=0, keepdims=True))
            p = e * (1.0 / jnp.sum(e, axis=0, keepdims=True))
            gp = dot_nt(values[a], grad)
            gs = p * (gp - jnp.sum(p * gp, axis=0, keepdims=True))
            gs = gs.astype(jnp.bfloat16)
            p = p.astype(jnp.bfloat16)
            gs_f = gs.astype(jnp.float32)
            for t in range(tiles):
                at = LANES * (tiles - t) + c * chunk
                fold_ref[a, :, at : at + chunk] += gs_f[t * LANES : (t + 1) * LANES]
            part = dot_nn(gs, query_parts[a])
            gk[0] = part if gk[0] is None else gk[0] + part
            part = dot_nn(p, grad_parts[a])
            gv[0] = part if gv[0] is None else gv[0] + part
            part = dot_tn(gs, keys[a])
            gq = part if gq is None else gq + part
        gq_ref[here, :] = gq.astype(gq_ref.dtype)
    gk_ref[...] = gk[0].astype(gk_ref.dtype)
    gv_ref[...] = gv[0].astype(gv_ref.dtype)

    @pl.when(micro == pl.num_programs(1) - 1)
    def _():
        for a in range(group):
            gb_ref[a] = fold_diagonals(fold_ref[a])


def attention_specs(length, width, group, span):
    return (
        pl.BlockSpec((length, width), lambda h, m: (m, h)),
        pl.BlockSpec((length, 1), lambda h, m: (m, 0)),
        pl.BlockSpec((None, 1, length), lambda h, m: (m, 0, 0)),
        pl.BlockSpec((group, 1, span), lambda h, m: (h, 0, 0)),
    )


def attention(query, key, value, segment, rows, head_dim):
    micro_count, length = segment.shape
    model_width = query.shape[1]
    width = max(LANES, head_dim)
    group = width // head_dim
    block, segc, segr, line = attention_specs(length, width, group, rows.shape[2])
    return pl.pallas_call(
        lambda *refs: forward_kernel(head_dim, *refs),
        name="attention_forward",
        grid=(model_width // width, micro_count),
        in_specs=[block, block, block, segc, segr, line],
        out_specs=block,
        out_shape=jax.ShapeDtypeStruct(query.shape, jnp.bfloat16),
        scratch_shapes=[pltpu.VMEM((group, LANES, rows.shape[2]), jnp.float32)],
    )(query, key, value, segment.reshape(-1, 1), segment[:, None, :], rows)


def attention_grads(query, key, value, grad, segment, rows, head_dim):
    micro_count, length = segment.shape
    model_width = query.shape[1]
    width = max(LANES, head_dim)
    group = width // head_dim
    block, segc, segr, line = attention_specs(length, width, group, rows.shape[2])
    flat = jax.ShapeDtypeStruct(query.shape, jnp.bfloat16)
    return pl.pallas_call(
        lambda *refs: backward_kernel(head_dim, *refs),
        name="attention_backward",
        grid=(model_width // width, micro_count),
        in_specs=[block, block, block, block, segc, segr, line],
        out_specs=[block, block, block, line],
        out_shape=[flat, flat, flat, jax.ShapeDtypeStruct(rows.shape, jnp.float32)],
        scratch_shapes=[pltpu.VMEM((group, LANES, rows.shape[2]), jnp.float32)] * 2,
    )(query, key, value, grad, segment.reshape(-1, 1), segment[:, None, :], rows)


class Net:
    def __init__(self):
        self.dp = lax.axis_size("dp")
        self.size = self.dp * lax.axis_size("tower")
        self.index = lax.axis_index("tower") * self.dp + lax.axis_index("dp")

    def bit(self, b):
        return (self.index >> b) & 1

    def swap(self, value, b):
        return lax.ppermute(value, AXES, [(i, i ^ (1 << b)) for i in range(self.size)])


def join(own, other, bit):
    first = jnp.where(bit == 0, own, other)
    second = jnp.where(bit == 0, other, own)
    return jnp.concatenate([first, second], axis=0)


def half_of(value, which):
    rows = value.shape[0] // 2
    return lax.dynamic_slice_in_dim(value, which * rows, rows, 0)


def scatter_sum(net, sent, kept, order):
    got = net.swap(sent, order[0])
    for b in order[1:]:
        bit = net.bit(b)
        sent = half_of(kept, 1 - bit) + half_of(got, 1 - bit)
        kept = half_of(kept, bit) + half_of(got, bit)
        got = net.swap(sent, b)
    return kept + got


def gather_all(net, piece, order):
    for b in reversed(order):
        piece = join(piece, net.swap(piece, b), net.bit(b))
    return piece


def sum_small(net, value, order):
    for b in order:
        value = value + net.swap(value, b)
    return value


def local(
    states,
    segment_ids,
    lengths,
    positives,
    w_query,
    w_key,
    w_value,
    w_out,
    w_in,
    w_ffout,
    w_proj,
    gain_attn,
    gain_ffn,
    gain_final,
    rel_bias,
):
    micro_count = states.shape[1]
    length = states.shape[2]
    model_width = states.shape[3]
    item_count = lengths.shape[2]
    bucket_count, head_count = rel_bias.shape
    head_dim = model_width // head_count
    ff_width = w_in.shape[1]
    tower_index = lax.axis_index("tower")
    dp_index = lax.axis_index("dp")
    dp_count = lax.axis_size("dp")
    row_count = item_count * dp_count
    rows = micro_count * length
    net = Net()
    bits = net.size.bit_length() - 1
    core = 0
    chips = tuple(range(1, bits))
    gather_order = (0, 4, 1, 2, 3) if bits == 5 else tuple(range(bits))

    offset = jnp.arange(2 * length, dtype=jnp.int32) - length
    code = bucket_code(offset, bucket_count)
    code_back = bucket_code(-offset, bucket_count)

    def bias_rows(which):
        return jnp.dot(which, rel_bias, precision=highest).T[:, None, :]

    segment = segment_ids[0]

    states_f = states[0].reshape(rows, model_width).astype(jnp.float32)
    normed, back_attn = jax.vjp(rms_scale, states_f, gain_attn)
    normed_low = normed.astype(jnp.bfloat16)
    query_low = mm(normed_low, w_query).astype(jnp.bfloat16)
    key_low = mm(normed_low, w_key).astype(jnp.bfloat16)
    value_low = mm(normed_low, w_value).astype(jnp.bfloat16)
    mixed_low = attention(query_low, key_low, value_low, segment, bias_rows(code), head_dim)
    hidden = states_f + mm(mixed_low, w_out)
    normed_two, back_ffn = jax.vjp(rms_scale, hidden, gain_ffn)
    normed_two_low = normed_two.astype(jnp.bfloat16)
    activ_low = jnp.maximum(mm(normed_two_low, w_in), 0.0).astype(jnp.bfloat16)
    output = hidden + mm(activ_low, w_ffout)
    final_norm, back_final = jax.vjp(rms_scale, output, gain_final)
    member = (segment[:, :, None] == jnp.arange(item_count, dtype=jnp.int32)).astype(jnp.float32)
    count_f = lengths[0].astype(jnp.float32)[:, :, None]
    pooled_low = (
        jnp.einsum(
            "btc,btf->bcf",
            member,
            final_norm.reshape(micro_count, length, model_width),
            precision=highest,
        )
        / count_f
    ).astype(jnp.bfloat16)
    pooled_flat = pooled_low.reshape(micro_count * item_count, model_width)
    embed = mm(pooled_flat, w_proj)
    unit_embed, back_unit = jax.vjp(unit_rows, embed)

    every = unit_embed[None]
    for b in reversed(gather_order):
        every = join(every, net.swap(every, b), net.bit(b))
    every = every.reshape((2,) * bits + (micro_count, item_count, model_width))
    place = [bits - 1 - b for b in gather_order]
    every = jnp.transpose(
        every,
        [bits]
        + [gather_order.index(b) for b in reversed(range(bits))]
        + [bits + 1, bits + 2],
    ).reshape(micro_count, 2, row_count, model_width)
    queries_all = every[:, 0]
    passages_all = every[:, 1]
    columns = jnp.arange(row_count, dtype=jnp.int32)[None, :]
    loss_sum = jnp.zeros((), jnp.float32)
    grad_embed = []
    for m in range(micro_count):
        logits = logit_scale * jnp.dot(queries_all[m], passages_all[m].T, precision=highest)
        target_hot = (columns == positives[m][:, None]).astype(jnp.float32)
        loss_part, grad_logits = softmax_terms(logits, target_hot)
        loss_sum = loss_sum + loss_part
        own_rows = lax.dynamic_slice_in_dim(grad_logits, dp_index * item_count, item_count, 0)
        own_cols = lax.dynamic_slice_in_dim(grad_logits, dp_index * item_count, item_count, 1)
        own = jnp.where(tower_index == 0, own_rows, own_cols.T)
        others = jnp.where(tower_index == 0, passages_all[m], queries_all[m])
        grad_embed.append(logit_scale * jnp.dot(own, others, precision=highest))
    grad_embed = jnp.concatenate(grad_embed, axis=0)
    (grad_e,) = back_unit(grad_embed)
    grad_e_low = grad_e.astype(jnp.bfloat16)
    grad_pooled = mm_t(grad_e_low, w_proj).reshape(micro_count, item_count, model_width)
    grad_final_norm = jnp.einsum(
        "btc,bcf->btf", member, grad_pooled / count_f, precision=highest
    ).reshape(rows, model_width)
    grad_output, grad_gain_final = back_final(grad_final_norm)
    grad_output_low = grad_output.astype(jnp.bfloat16)

    def halves(left, right, core_bit):
        wide = left.shape[1] // 2
        other = t_mm(
            lax.dynamic_slice_in_dim(left, (1 - core_bit) * wide, wide, 1), right
        )
        own = t_mm(lax.dynamic_slice_in_dim(left, core_bit * wide, wide, 1), right)
        return other, own

    core_bit = net.bit(core)
    if bits == 5:
        orders = (((0, 4, 1, 2, 3), (0, 1, 4, 2, 3)), ((0, 4, 2, 3, 1), (0, 1, 2, 3, 4)))
    else:
        orders = ((tuple(range(bits)),) * 2,) * 2

    def total(left, right, order):
        sent, kept = halves(left, right, core_bit)
        return gather_all(net, scatter_sum(net, sent, kept, order), order)

    ff_half = ff_width // 2
    whole_ffout = jnp.concatenate(
        [
            total(activ_low[:, :ff_half], grad_output_low, orders[0][0]),
            total(activ_low[:, ff_half:], grad_output_low, orders[0][1]),
        ],
        axis=0,
    )
    grad_activ = mm_t(grad_output_low, w_ffout)
    grad_inner_low = jnp.where(activ_low > 0, grad_activ, 0.0).astype(jnp.bfloat16)
    whole_in = jnp.concatenate(
        [
            total(normed_two_low, grad_inner_low[:, :ff_half], orders[1][0]),
            total(normed_two_low, grad_inner_low[:, ff_half:], orders[1][1]),
        ],
        axis=1,
    )
    grad_normed_two = mm_t(grad_inner_low, w_in)
    grad_hidden_norm, grad_gain_ffn = back_ffn(grad_normed_two)
    grad_hidden = grad_output + grad_hidden_norm
    grad_hidden_low = grad_hidden.astype(jnp.bfloat16)
    grad_mixed = mm_t(grad_hidden_low, w_out).astype(jnp.bfloat16)
    grad_query_h, grad_key_h, grad_value_h, grad_rows = attention_grads(
        query_low, key_low, value_low, grad_mixed, segment, bias_rows(code_back), head_dim
    )
    grad_bias = jnp.einsum("hx,xb->bh", grad_rows[:, 0], code_back, precision=highest)
    grad_qkv = jnp.concatenate([grad_query_h, grad_key_h, grad_value_h], axis=1)
    grad_normed = (
        mm_t(grad_query_h, w_query) + mm_t(grad_key_h, w_key) + mm_t(grad_value_h, w_value)
    )
    cut = model_width // 2
    first_sent, first_kept = halves(normed_low, grad_qkv[:, : 5 * cut], core_bit)
    rest = [
        halves(normed_low, grad_qkv[:, 5 * cut :], core_bit),
        halves(mixed_low, grad_hidden_low, core_bit),
        halves(pooled_flat, grad_e_low, core_bit),
    ]
    last_sent = jnp.concatenate([r[0] for r in rest], axis=1)
    last_kept = jnp.concatenate([r[1] for r in rest], axis=1)
    order = orders[0][0]
    whole_first = gather_all(net, scatter_sum(net, first_sent, first_kept, order), order)
    order = orders[0][1]
    whole_last = gather_all(net, scatter_sum(net, last_sent, last_kept, order), order)

    grad_states_norm, grad_gain_attn = back_attn(grad_normed)
    grad_states = grad_hidden + grad_states_norm
    small = jnp.concatenate(
        [
            grad_gain_attn,
            grad_gain_ffn,
            grad_gain_final,
            grad_bias.reshape(-1),
            jnp.zeros((model_width - bucket_count * head_count,), jnp.float32),
        ]
    ).reshape(-1, 128)
    small = sum_small(net, small, tuple(range(bits))).reshape(-1)
    loss = loss_sum / (micro_count * row_count)
    width = model_width
    return (
        loss,
        unit_embed.reshape(1, micro_count, item_count, model_width),
        grad_states.reshape(1, micro_count, length, model_width),
        whole_first[:, :width],
        whole_first[:, width : 2 * width],
        jnp.concatenate([whole_first[:, 2 * width :], whole_last[:, :cut]], axis=1),
        whole_last[:, cut : cut + width],
        whole_in,
        whole_ffout,
        whole_last[:, cut + width :],
        small[:width],
        small[width : 2 * width],
        small[2 * width : 3 * width],
        small[3 * width : 3 * width + bucket_count * head_count].reshape(
            bucket_count, head_count
        ),
    )


def solution(mesh):
    return jax.shard_map(
        local,
        mesh=mesh,
        in_specs=(
            P("tower", None, "dp", None),
            P("tower", None, "dp"),
            P("tower", None, "dp"),
        )
        + (P(),) * 12,
        out_specs=(P(), P("tower", None, "dp", None), P("tower", None, "dp", None)) + (P(),) * 11,
        check_vma=False,
    )
```

```python
import jax
import jax.numpy as jnp
from jax import lax
from jax.experimental import pallas as pl
from jax.experimental.pallas import tpu as pltpu
from jax.sharding import PartitionSpec as P

highest = lax.Precision.HIGHEST
norm_epsilon = 1e-06
logit_scale = 50.0
bucket_edges = (12, 16, 23, 32, 46, 64, 91)
AXES = ("tower", "dp")
LANES = 128


def bucket_code(offset, bucket_count):
    distance = jnp.abs(offset)
    far_bucket = jnp.full_like(distance, 8)
    for edge_value in bucket_edges:
        far_bucket = far_bucket + (distance >= edge_value).astype(jnp.int32)
    bucket = jnp.where(distance < 8, distance, far_bucket) + jnp.where(offset > 0, 16, 0)
    return (bucket[:, None] == jnp.arange(bucket_count, dtype=jnp.int32)[None, :]).astype(jnp.float32)


def rms_scale(values, gain_vec):
    return (
        values
        * lax.rsqrt(jnp.mean(values * values, axis=-1, keepdims=True) + norm_epsilon)
        * gain_vec
    )


def unit_rows(values):
    return values * lax.rsqrt(jnp.sum(values * values, axis=-1, keepdims=True) + norm_epsilon)


def softmax_terms(logits, target_hot):
    maxima = jnp.max(logits, axis=1, keepdims=True)
    log_total = maxima + jnp.log(jnp.sum(jnp.exp(logits - maxima), axis=1, keepdims=True))
    loss_part = jnp.sum(log_total[:, 0] - jnp.sum(logits * target_hot, axis=1))
    return (loss_part, jnp.exp(logits - log_total) - target_hot)


def mm(a, b):
    return jnp.dot(a, b, preferred_element_type=jnp.float32)


def mm_t(a, b):
    return lax.dot_general(a, b, (((1,), (1,)), ((), ())), preferred_element_type=jnp.float32)


def dot_nt(a, b):
    return lax.dot_general(a, b, (((1,), (1,)), ((), ())), preferred_element_type=jnp.float32)

def dot_tn(a, b):
    return lax.dot_general(a, b, (((0,), (0,)), ((), ())), preferred_element_type=jnp.float32)

def dot_nn(a, b):
    return lax.dot_general(a, b, (((1,), (0,)), ((), ())), preferred_element_type=jnp.float32)


def head_parts(value, head_dim):
    lane = lax.broadcasted_iota(jnp.int32, value.shape, 1)
    zero = jnp.zeros_like(value)
    return [
        jnp.where((lane >= a * head_dim) & (lane < (a + 1) * head_dim), value, zero)
        for a in range(value.shape[1] // head_dim)
    ]


def diagonals(row):
    wide = jnp.broadcast_to(row, (LANES, row.shape[1]))
    return pltpu.roll(wide, 0, 1, stride=1, stride_axis=0)


def forward_kernel(head_dim, q_ref, k_ref, v_ref, segc_ref, segr_ref, rows_ref, o_ref, diag_ref):
    length, width = q_ref.shape
    group = width // head_dim
    tiles = length // LANES

    @pl.when(pl.program_id(1) == 0)
    def _():
        for a in range(group):
            diag_ref[a] = diagonals(rows_ref[a])

    keys = head_parts(k_ref[...], head_dim)
    values = head_parts(v_ref[...], head_dim)
    segr = segr_ref[...]
    for t in range(tiles):
        here = slice(t * LANES, (t + 1) * LANES)
        query = q_ref[here, :]
        same = segc_ref[here, :] == segr
        total = None
        for a in range(group):
            s = dot_nt(query, keys[a])
            s = s + diag_ref[a, :, LANES * (tiles - t) : LANES * (tiles - t) + length]
            s = jnp.where(same, s, -1000000000.0)
            e = jnp.exp(s - jnp.max(s, axis=1, keepdims=True))
            p = e * (1.0 / jnp.sum(e, axis=1, keepdims=True))
            part = dot_nn(p.astype(jnp.bfloat16), values[a])
            total = part if total is None else total + part
        o_ref[here, :] = total.astype(o_ref.dtype)


def fold_diagonals(value):
    n = value.shape[1]
    rows = value.shape[0]
    while rows > 1:
        rows //= 2
        value = value[:rows] + pltpu.roll(value[rows:], n - rows, 1)
    return value


def backward_kernel(head_dim, q_ref, k_ref, v_ref, g_ref, segc_ref, segr_ref, rows_ref,
                    gq_ref, gk_ref, gv_ref, gb_ref, diag_ref, fold_ref):
    length, width = q_ref.shape
    group = width // head_dim
    tiles = length // LANES
    micro = pl.program_id(1)

    @pl.when(micro == 0)
    def _():
        for a in range(group):
            diag_ref[a] = diagonals(rows_ref[a])
        fold_ref[...] = jnp.zeros_like(fold_ref)

    keys = head_parts(k_ref[...], head_dim)
    values = head_parts(v_ref[...], head_dim)
    segc = segc_ref[...]
    chunk = 2 * LANES
    gk = [None]
    gv = [None]
    for c in range(length // chunk):
        here = slice(c * chunk, (c + 1) * chunk)
        query = q_ref[here, :]
        grad = g_ref[here, :]
        query_parts = head_parts(query, head_dim)
        grad_parts = head_parts(grad, head_dim)
        same = segc == segr_ref[:, here]
        gq = None
        for a in range(group):
            s = dot_nt(keys[a], query)
            bias = jnp.concatenate(
                [
                    diag_ref[a, :, LANES * (tiles - t) + c * chunk : LANES * (tiles - t) + (c + 1) * chunk]
                    for t in range(tiles)
                ],
                axis=0,
            )
            s = jnp.where(same, s + bias, -1000000000.0)
            e = jnp.exp(s - jnp.max(s, axis=0, keepdims=True))
            p = e * (1.0 / jnp.sum(e, axis=0, keepdims=True))
            gp = dot_nt(values[a], grad)
            gs = p * (gp - jnp.sum(p * gp, axis=0, keepdims=True))
            gs = gs.astype(jnp.bfloat16)
            p = p.astype(jnp.bfloat16)
            gs_f = gs.astype(jnp.float32)
            for t in range(tiles):
                at = LANES * (tiles - t) + c * chunk
                fold_ref[a, :, at : at + chunk] += gs_f[t * LANES : (t + 1) * LANES]
            part = dot_nn(gs, query_parts[a])
            gk[0] = part if gk[0] is None else gk[0] + part
            part = dot_nn(p, grad_parts[a])
            gv[0] = part if gv[0] is None else gv[0] + part
            part = dot_tn(gs, keys[a])
            gq = part if gq is None else gq + part
        gq_ref[here, :] = gq.astype(gq_ref.dtype)
    gk_ref[...] = gk[0].astype(gk_ref.dtype)
    gv_ref[...] = gv[0].astype(gv_ref.dtype)

    @pl.when(micro == pl.num_programs(1) - 1)
    def _():
        for a in range(group):
            gb_ref[a] = fold_diagonals(fold_ref[a])


def attention_specs(length, width, group, span, first):
    return (
        pl.BlockSpec((length, width), lambda h, m: (m, first + h)),
        pl.BlockSpec((length, 1), lambda h, m: (m, 0)),
        pl.BlockSpec((None, 1, length), lambda h, m: (m, 0, 0)),
        pl.BlockSpec((group, 1, span), lambda h, m: (first + h, 0, 0)),
    )


def attention(query, key, value, segment, rows, head_dim):
    micro_count, length = segment.shape
    model_width = query.shape[1]
    width = max(LANES, head_dim)
    group = width // head_dim
    block, segc, segr, line = attention_specs(length, width, group, rows.shape[2], 0)
    return pl.pallas_call(
        lambda *refs: forward_kernel(head_dim, *refs),
        name="attention_forward",
        grid=(model_width // width, micro_count),
        in_specs=[block, block, block, segc, segr, line],
        out_specs=block,
        out_shape=jax.ShapeDtypeStruct(query.shape, jnp.bfloat16),
        scratch_shapes=[pltpu.VMEM((group, LANES, rows.shape[2]), jnp.float32)],
    )(query, key, value, segment.reshape(-1, 1), segment[:, None, :], rows)


def attention_grads(query, key, value, grad, segment, rows, head_dim, part, parts, before):
    micro_count, length = segment.shape
    model_width = query.shape[1]
    width = max(LANES, head_dim)
    group = width // head_dim
    count = model_width // width // parts
    first = part * count
    block, segc, segr, line = attention_specs(length, width, group, rows.shape[2], first)
    flat = jax.ShapeDtypeStruct(query.shape, jnp.bfloat16)
    kept = len(before)

    def kernel(*refs):
        backward_kernel(head_dim, *refs[:7], *refs[7 + kept :])

    return pl.pallas_call(
        kernel,
        name="attention_backward",
        grid=(count, micro_count),
        in_specs=[block, block, block, block, segc, segr, line]
        + [pl.BlockSpec(memory_space=pl.ANY)] * kept,
        out_specs=[block, block, block, line],
        out_shape=[flat, flat, flat, jax.ShapeDtypeStruct(rows.shape, jnp.float32)],
        input_output_aliases={7 + n: n for n in range(kept)},
        scratch_shapes=[pltpu.VMEM((group, LANES, rows.shape[2]), jnp.float32)] * 2,
    )(query, key, value, grad, segment.reshape(-1, 1), segment[:, None, :], rows, *before)


class Net:
    def __init__(self):
        self.dp = lax.axis_size("dp")
        self.size = self.dp * lax.axis_size("tower")
        self.index = lax.axis_index("tower") * self.dp + lax.axis_index("dp")
        count = self.size.bit_length() - 1
        if count == 5:
            self.steps = ((0, 0), (4, 1), (1, 4), (2, 2), (3, 3))
        else:
            self.steps = tuple((b, b) for b in range(count))
        self.bits = [self.bit_of(k) for k in range(count)]

    def bit(self, b):
        return (self.index >> b) & 1

    def bit_of(self, k):
        first, second = self.steps[k]
        if first == second:
            return self.bit(first)
        return jnp.where(self.bit(0) == 0, self.bit(first), self.bit(second))

    def swap(self, value, b):
        return lax.ppermute(value, AXES, [(i, i ^ (1 << b)) for i in range(self.size)])

    def swap_step(self, value, k):
        pairs = [(i, i ^ (1 << self.steps[k][i & 1])) for i in range(self.size)]
        return lax.ppermute(value, AXES, pairs)


def join(own, other, bit):
    rows, width = own.shape
    side = lax.broadcasted_iota(jnp.int32, (2, rows, width), 0)
    return jnp.where(side == bit, own[None], other[None]).reshape(2 * rows, width)


def half_of(value, which):
    rows = value.shape[0] // 2
    return lax.dynamic_slice_in_dim(value, which * rows, rows, 0)


def weight_grads(bit, lefts, rights):
    height = lefts[0].shape[1] // 2
    width = min(r.shape[1] for r in rights)
    rows = max(r for r in range(LANES, min(height, 512) + 1, LANES) if height % r == 0)
    stacks = height // rows
    ends = [sum(r.shape[1] for r in rights[: n + 1]) // width for n in range(len(rights))]
    starts = [end - r.shape[1] // width for end, r in zip(ends, rights)]
    columns = ends[-1]
    count = len(lefts)

    def kernel(bit_ref, *refs):
        left_refs, right_refs, (sent_ref, kept_ref) = refs[:count], refs[count:-2], refs[-2:]
        side, column = pl.program_id(0), pl.program_id(2)

        def one(left_ref, right_ref):
            value = dot_tn(left_ref[...], right_ref[...])

            @pl.when(side == 0)
            def _():
                sent_ref[...] = value

            @pl.when(side == 1)
            def _():
                kept_ref[...] = value

        for left_ref, right_ref, start, end in zip(left_refs, right_refs, starts, ends):
            inside = (column >= start) & (column < end)
            pl.when(inside)(lambda left_ref=left_ref, right_ref=right_ref: one(left_ref, right_ref))

    def left_place(side, stack, column, bit_ref):
        half = jnp.where(side == 0, 1 - bit_ref[0], bit_ref[0])
        return (0, half * stacks + stack)

    def right_place(start, end):
        return lambda side, stack, column, bit_ref: (0, jnp.clip(column - start, 0, end - start - 1))

    def sent_place(side, stack, column, bit_ref):
        return (jnp.where(side == 0, stack, stacks - 1), jnp.where(side == 0, column, columns - 1))

    def kept_place(side, stack, column, bit_ref):
        return (jnp.where(side == 1, stack, 0), jnp.where(side == 1, column, 0))

    return pl.pallas_call(
        kernel,
        name="weight_grads",
        grid_spec=pltpu.PrefetchScalarGridSpec(
            num_scalar_prefetch=1,
            grid=(2, stacks, columns),
            in_specs=[pl.BlockSpec((v.shape[0], rows), left_place) for v in lefts]
            + [
                pl.BlockSpec((v.shape[0], width), right_place(start, end))
                for v, start, end in zip(rights, starts, ends)
            ],
            out_specs=[
                pl.BlockSpec((rows, width), sent_place),
                pl.BlockSpec((rows, width), kept_place),
            ],
        ),
        out_shape=[jax.ShapeDtypeStruct((height, columns * width), jnp.float32)] * 2,
    )(bit.reshape(1), *lefts, *rights)


def feed_backward_kernel(
    go_ref, act_ref, hid_ref, gain_ref, wff_ref, win_ref, wout_ref,
    gu_ref, gh_ref, ghl_ref, gm_ref, gg_ref,
):
    grad_output = go_ref[...]
    grad_activ = dot_nt(grad_output.astype(jnp.bfloat16), wff_ref[...])
    grad_inner = jnp.where(act_ref[...] > 0, grad_activ, 0.0).astype(jnp.bfloat16)
    gu_ref[...] = grad_inner
    grad_normed = dot_nt(grad_inner, win_ref[...])
    hidden = hid_ref[...]
    scale = lax.rsqrt(jnp.mean(hidden * hidden, axis=1, keepdims=True) + norm_epsilon)
    unit = hidden * scale

    @pl.when(pl.program_id(0) == 0)
    def _():
        gg_ref[...] = jnp.zeros_like(gg_ref)

    gg_ref[...] += jnp.sum(grad_normed * unit, axis=0, keepdims=True)
    scaled = grad_normed * gain_ref[...]
    grad_hidden = grad_output + scale * (
        scaled - unit * jnp.mean(unit * scaled, axis=1, keepdims=True)
    )
    gh_ref[...] = grad_hidden
    low = grad_hidden.astype(jnp.bfloat16)
    ghl_ref[...] = low
    gm_ref[...] = dot_nt(low, wout_ref[...]).astype(jnp.bfloat16)


def feed_backward(grad_output, activ, hidden, gain, w_ffout, w_in, w_out):
    rows, width = grad_output.shape
    inner = activ.shape[1]
    tile = 256

    def lines(n):
        return pl.BlockSpec((tile, n), lambda t: (t, 0))

    def whole(*shape):
        return pl.BlockSpec(shape, lambda t: (0, 0))

    return pl.pallas_call(
        feed_backward_kernel,
        name="feed_backward",
        grid=(rows // tile,),
        in_specs=[
            lines(width),
            lines(inner),
            lines(width),
            whole(1, width),
            whole(inner, width),
            whole(width, inner),
            whole(width, width),
        ],
        out_specs=[lines(inner), lines(width), lines(width), lines(width), whole(1, width)],
        out_shape=[
            jax.ShapeDtypeStruct((rows, inner), jnp.bfloat16),
            jax.ShapeDtypeStruct((rows, width), jnp.float32),
            jax.ShapeDtypeStruct((rows, width), jnp.bfloat16),
            jax.ShapeDtypeStruct((rows, width), jnp.bfloat16),
            jax.ShapeDtypeStruct((1, width), jnp.float32),
        ],
    )(grad_output, activ, hidden, gain[None], w_ffout, w_in, w_out)


def put_together(own, other, bit, widths):
    half = 4
    rows, wide = own.shape
    block = rows // half

    def kernel(bit_ref, own_ref, other_ref, *out_refs):
        is_own = pl.program_id(0) // half == bit_ref[0]

        def copy(source):
            at = 0
            for out, width in zip(out_refs, widths):
                out[...] = source[:, at : at + width]
                at += width

        pl.when(is_own)(lambda: copy(own_ref))
        pl.when(jnp.logical_not(is_own))(lambda: copy(other_ref))

    def place(side):
        def index(step, bit_ref):
            first = jnp.where(side == 0, bit_ref[0], 1 - bit_ref[0]) * half
            return (jnp.clip(step - first, 0, half - 1), 0)

        return index

    return pl.pallas_call(
        kernel,
        name="put_together",
        grid_spec=pltpu.PrefetchScalarGridSpec(
            num_scalar_prefetch=1,
            grid=(2 * half,),
            in_specs=[pl.BlockSpec((block, wide), place(side)) for side in (0, 1)],
            out_specs=[pl.BlockSpec((block, w), lambda step, bit_ref: (step, 0)) for w in widths],
        ),
        out_shape=[jax.ShapeDtypeStruct((2 * rows, w), own.dtype) for w in widths],
        cost_estimate=pl.CostEstimate(
            flops=0, transcendentals=0, bytes_accessed=16 * rows * wide
        ),
    )(bit.reshape(1), own, other)


def tie(*values):
    return lax.optimization_barrier(values)


class Sum:
    def __init__(self, net, lefts, rights):
        self.net = net
        self.widths = [r.shape[1] for r in rights]
        self.step = 0
        self.back = False
        self.done = False
        self.held = weight_grads(net.bits[0], lefts, rights)

    def go(self):
        if self.back:
            self.got = self.net.swap_step(self.held[0], self.step - 1)
        else:
            self.got = self.net.swap_step(self.held[0], self.step)

    def end(self):
        bits = self.net.bits
        if self.back:
            self.step -= 1
            self.done = self.step == 0
            if self.done:
                self.held = put_together(self.held[0], self.got, bits[0], self.widths)
            else:
                self.held = [join(self.held[0], self.got, bits[self.step])]
            return
        self.step += 1
        self.back = self.step == len(bits)
        kept, got = self.held[1], self.got
        if self.back:
            self.held = [kept + got]
        else:
            bit = bits[self.step]
            self.held = [
                half_of(kept, 1 - bit) + half_of(got, 1 - bit),
                half_of(kept, bit) + half_of(got, bit),
            ]


def tie_all(sums, *values):
    values, held = tie(values, [s.held for s in sums])
    for s, h in zip(sums, held):
        s.held = h
    return values


def advance(sums, steps):
    for s, count in zip(sums, steps):
        for _ in range(count):
            if not s.done:
                s.go()
                s.end()


def local(
    states,
    segment_ids,
    lengths,
    positives,
    w_query,
    w_key,
    w_value,
    w_out,
    w_in,
    w_ffout,
    w_proj,
    gain_attn,
    gain_ffn,
    gain_final,
    rel_bias,
):
    micro_count = states.shape[1]
    length = states.shape[2]
    model_width = states.shape[3]
    item_count = lengths.shape[2]
    bucket_count, head_count = rel_bias.shape
    head_dim = model_width // head_count
    ff_width = w_in.shape[1]
    tower_index = lax.axis_index("tower")
    dp_index = lax.axis_index("dp")
    dp_count = lax.axis_size("dp")
    row_count = item_count * dp_count
    rows = micro_count * length
    net = Net()
    bits = len(net.steps)
    gather_order = (0, 4, 1, 2, 3) if bits == 5 else tuple(range(bits))

    offset = jnp.arange(2 * length, dtype=jnp.int32) - length
    code = bucket_code(offset, bucket_count)
    code_back = bucket_code(-offset, bucket_count)

    def bias_rows(which):
        return jnp.dot(which, rel_bias, precision=highest).T[:, None, :]

    segment = segment_ids[0]

    states_f = states[0].reshape(rows, model_width).astype(jnp.float32)
    normed, back_attn = jax.vjp(rms_scale, states_f, gain_attn)
    normed_low = normed.astype(jnp.bfloat16)
    query_low = mm(normed_low, w_query).astype(jnp.bfloat16)
    key_low = mm(normed_low, w_key).astype(jnp.bfloat16)
    value_low = mm(normed_low, w_value).astype(jnp.bfloat16)
    mixed_low = attention(query_low, key_low, value_low, segment, bias_rows(code), head_dim)
    hidden = states_f + mm(mixed_low, w_out)
    normed_two = rms_scale(hidden, gain_ffn)
    normed_two_low = normed_two.astype(jnp.bfloat16)
    activ_low = jnp.maximum(mm(normed_two_low, w_in), 0.0).astype(jnp.bfloat16)
    output = hidden + mm(activ_low, w_ffout)
    final_norm, back_final = jax.vjp(rms_scale, output, gain_final)
    member = (segment[:, :, None] == jnp.arange(item_count, dtype=jnp.int32)).astype(jnp.float32)
    count_f = lengths[0].astype(jnp.float32)[:, :, None]
    pooled_low = (
        jnp.einsum(
            "btc,btf->bcf",
            member,
            final_norm.reshape(micro_count, length, model_width),
            precision=highest,
        )
        / count_f
    ).astype(jnp.bfloat16)
    pooled_flat = pooled_low.reshape(micro_count * item_count, model_width)
    embed = mm(pooled_flat, w_proj)
    unit_embed, back_unit = jax.vjp(unit_rows, embed)

    every = unit_embed
    for b in reversed(gather_order):
        every = join(every, net.swap(every, b), net.bit(b))
    every = every.reshape((2,) * bits + (micro_count, item_count, model_width))
    place = [bits - 1 - b for b in gather_order]
    every = jnp.transpose(
        every,
        [bits]
        + [gather_order.index(b) for b in reversed(range(bits))]
        + [bits + 1, bits + 2],
    ).reshape(micro_count, 2, row_count, model_width)
    queries_all = every[:, 0]
    passages_all = every[:, 1]
    columns = jnp.arange(row_count, dtype=jnp.int32)[None, :]
    loss_sum = jnp.zeros((), jnp.float32)
    grad_embed = []
    for m in range(micro_count):
        logits = logit_scale * jnp.dot(queries_all[m], passages_all[m].T, precision=highest)
        target_hot = (columns == positives[m][:, None]).astype(jnp.float32)
        loss_part, grad_logits = softmax_terms(logits, target_hot)
        loss_sum = loss_sum + loss_part
        own_rows = lax.dynamic_slice_in_dim(grad_logits, dp_index * item_count, item_count, 0)
        own_cols = lax.dynamic_slice_in_dim(grad_logits, dp_index * item_count, item_count, 1)
        own = jnp.where(tower_index == 0, own_rows, own_cols.T)
        others = jnp.where(tower_index == 0, passages_all[m], queries_all[m])
        grad_embed.append(logit_scale * jnp.dot(own, others, precision=highest))
    grad_embed = jnp.concatenate(grad_embed, axis=0)
    (grad_e,) = back_unit(grad_embed)
    grad_e_low = grad_e.astype(jnp.bfloat16)
    grad_pooled = mm_t(grad_e_low, w_proj).reshape(micro_count, item_count, model_width)
    grad_final_norm = jnp.einsum(
        "btc,bcf->btf", member, grad_pooled / count_f, precision=highest
    ).reshape(rows, model_width)
    grad_output, grad_gain_final = back_final(grad_final_norm)
    grad_output_low = grad_output.astype(jnp.bfloat16)

    first = Sum(net, [activ_low], [grad_output_low])
    (grad_output,) = tie_all([first], grad_output)
    first.go()
    grad_inner_low, grad_hidden, grad_hidden_low, grad_mixed, grad_gain_ffn = feed_backward(
        grad_output, activ_low, hidden, gain_ffn, w_ffout, w_in, w_out
    )
    first.end()
    grad_inner_low, grad_hidden_low, grad_mixed = tie_all(
        [first], grad_inner_low, grad_hidden_low, grad_mixed
    )
    first.go()
    parts = 3
    rows_back = bias_rows(code_back)

    def attention_part(part, query, before):
        return attention_grads(
            query, key_low, value_low, grad_mixed, segment, rows_back, head_dim, part, parts, before
        )

    grads = attention_part(0, query_low, ())
    second = Sum(net, [normed_two_low], [grad_inner_low])
    first.end()
    query_low, grads = tie_all([first, second], query_low, grads)
    first.go()
    second.go()
    grads = attention_part(1, query_low, grads)
    first.end()
    second.end()
    query_low, grads = tie_all([first, second], query_low, grads)
    first.go()
    second.go()
    grads = attention_part(2, query_low, grads)
    first.end()
    (grads,) = tie_all([first], grads)
    grad_query_h, grad_key_h, grad_value_h, grad_rows = grads
    first.go()
    third = Sum(
        net,
        [normed_low] * 3 + [mixed_low, pooled_flat],
        [grad_query_h, grad_key_h, grad_value_h, grad_hidden_low, grad_e_low],
    )
    first.end()
    second.end()
    grad_query_h, grad_key_h, grad_value_h = tie_all(
        [first, second, third], grad_query_h, grad_key_h, grad_value_h
    )
    sums = [first, second, third]
    advance(sums, (1, 1, 1))
    grad_bias = jnp.einsum("hx,xb->bh", grad_rows[:, 0], code_back, precision=highest)
    grad_normed = (
        mm_t(grad_query_h, w_query) + mm_t(grad_key_h, w_key) + mm_t(grad_value_h, w_value)
    )
    grad_states_norm, grad_gain_attn = back_attn(grad_normed)
    grad_states = grad_hidden + grad_states_norm
    small = jnp.concatenate(
        [grad_gain_attn, grad_gain_ffn[0], grad_gain_final, grad_bias.reshape(-1)]
    )
    lines = -(-small.shape[0] // (8 * LANES)) * 8
    small = jnp.pad(small, (0, lines * LANES - small.shape[0])).reshape(lines, LANES)
    (grad_states,) = tie_all(sums, grad_states)
    if bits == 5:
        plan = ((1, 1, 1), (1, 2, 1), (1, 1, 1), (1, 1, 1), (0, 1, 2), (0, 1, 1), (0, 0, 1), (0, 0, 1))
    else:
        plan = ((1, 1, 1),) * (2 * bits)
    for turn, steps in enumerate(plan):
        advance(sums, steps)
        if turn < bits:
            small = small + net.swap(small, turn)
        if turn + 1 < len(plan):
            (small,) = tie_all(sums, small)
    (whole_ffout,) = first.held
    (whole_in,) = second.held
    whole_query, whole_key, whole_value, whole_out, whole_proj = third.held
    small = small.reshape(-1)
    loss = loss_sum / (micro_count * row_count)
    width = model_width
    return (
        loss,
        unit_embed.reshape(1, micro_count, item_count, model_width),
        grad_states.reshape(1, micro_count, length, model_width),
        whole_query,
        whole_key,
        whole_value,
        whole_out,
        whole_in,
        whole_ffout,
        whole_proj,
        small[:width],
        small[width : 2 * width],
        small[2 * width : 3 * width],
        small[3 * width : 3 * width + bucket_count * head_count].reshape(
            bucket_count, head_count
        ),
    )


def solution(mesh):
    return jax.shard_map(
        local,
        mesh=mesh,
        in_specs=(
            P("tower", None, "dp", None),
            P("tower", None, "dp"),
            P("tower", None, "dp"),
        )
        + (P(),) * 12,
        out_specs=(P(), P("tower", None, "dp", None), P("tower", None, "dp", None)) + (P(),) * 11,
        check_vma=False,
    )
```

```python
import jax
import jax.numpy as jnp
from jax import lax
from jax.experimental import pallas as pl
from jax.experimental.pallas import tpu as pltpu
from jax.sharding import PartitionSpec as P

highest = lax.Precision.HIGHEST
norm_epsilon = 1e-06
logit_scale = 50.0
bucket_edges = (12, 16, 23, 32, 46, 64, 91)
AXES = ("tower", "dp")
LANES = 128
TILE = 256


def bucket_code(offset, bucket_count):
    distance = jnp.abs(offset)
    far_bucket = jnp.full_like(distance, 8)
    for edge_value in bucket_edges:
        far_bucket = far_bucket + (distance >= edge_value).astype(jnp.int32)
    bucket = jnp.where(distance < 8, distance, far_bucket) + jnp.where(offset > 0, 16, 0)
    return (bucket[:, None] == jnp.arange(bucket_count, dtype=jnp.int32)[None, :]).astype(jnp.float32)


def rms_scale(values, gain_vec):
    return (
        values
        * lax.rsqrt(jnp.mean(values * values, axis=-1, keepdims=True) + norm_epsilon)
        * gain_vec
    )


def unit_rows(values):
    return values * lax.rsqrt(jnp.sum(values * values, axis=-1, keepdims=True) + norm_epsilon)


def softmax_terms(logits, target_hot):
    maxima = jnp.max(logits, axis=1, keepdims=True)
    log_total = maxima + jnp.log(jnp.sum(jnp.exp(logits - maxima), axis=1, keepdims=True))
    loss_part = jnp.sum(log_total[:, 0] - jnp.sum(logits * target_hot, axis=1))
    return (loss_part, jnp.exp(logits - log_total) - target_hot)


def mm(a, b):
    return jnp.dot(a, b, preferred_element_type=jnp.float32)


def mm_t(a, b):
    return lax.dot_general(a, b, (((1,), (1,)), ((), ())), preferred_element_type=jnp.float32)


def dot_nt(a, b):
    return lax.dot_general(a, b, (((1,), (1,)), ((), ())), preferred_element_type=jnp.float32)

def dot_tn(a, b):
    return lax.dot_general(a, b, (((0,), (0,)), ((), ())), preferred_element_type=jnp.float32)

def dot_nn(a, b):
    return lax.dot_general(a, b, (((1,), (0,)), ((), ())), preferred_element_type=jnp.float32)


def head_parts(value, head_dim):
    lane = lax.broadcasted_iota(jnp.int32, value.shape, 1)
    zero = jnp.zeros_like(value)
    return [
        jnp.where((lane >= a * head_dim) & (lane < (a + 1) * head_dim), value, zero)
        for a in range(value.shape[1] // head_dim)
    ]


def diagonals(row):
    wide = jnp.broadcast_to(row, (LANES, row.shape[1]))
    return pltpu.roll(wide, 0, 1, stride=1, stride_axis=0)


def forward_kernel(head_dim, q_ref, k_ref, v_ref, segc_ref, segr_ref, rows_ref, o_ref, diag_ref):
    length, width = q_ref.shape
    group = width // head_dim
    tiles = length // LANES

    @pl.when(pl.program_id(1) == 0)
    def _():
        for a in range(group):
            diag_ref[a] = diagonals(rows_ref[a])

    keys = head_parts(k_ref[...], head_dim)
    values = head_parts(v_ref[...], head_dim)
    segr = segr_ref[...]
    deep = 2
    for c in range(tiles // deep):
        here = slice(c * deep * LANES, (c + 1) * deep * LANES)
        query = q_ref[here, :]
        same = segc_ref[here, :] == segr
        total = None
        for a in range(group):
            s = dot_nt(query, keys[a])
            bias = [
                diag_ref[a, :, LANES * (tiles - t) : LANES * (tiles - t) + length]
                for t in range(c * deep, (c + 1) * deep)
            ]
            s = s + jnp.concatenate(bias, axis=0)
            s = jnp.where(same, s, -1000000000.0)
            e = jnp.exp(s - jnp.max(s, axis=1, keepdims=True))
            p = e * (1.0 / jnp.sum(e, axis=1, keepdims=True))
            part = dot_nn(p.astype(jnp.bfloat16), values[a])
            total = part if total is None else total + part
        o_ref[here, :] = total.astype(o_ref.dtype)


def fold_diagonals(value):
    n = value.shape[1]
    rows = value.shape[0]
    while rows > 1:
        rows //= 2
        value = value[:rows] + pltpu.roll(value[rows:], n - rows, 1)
    return value


def backward_kernel(head_dim, q_ref, k_ref, v_ref, g_ref, segc_ref, segr_ref, rows_ref,
                    gq_ref, gk_ref, gv_ref, gb_ref, diag_ref, fold_ref):
    length, width = q_ref.shape
    group = width // head_dim
    tiles = length // LANES
    micro = pl.program_id(1)

    @pl.when(micro == 0)
    def _():
        for a in range(group):
            diag_ref[a] = diagonals(rows_ref[a])
        fold_ref[...] = jnp.zeros_like(fold_ref)

    keys = head_parts(k_ref[...], head_dim)
    values = head_parts(v_ref[...], head_dim)
    segc = segc_ref[...]
    chunk = length
    gk = [None]
    gv = [None]
    for c in range(length // chunk):
        here = slice(c * chunk, (c + 1) * chunk)
        query = q_ref[here, :]
        grad = g_ref[here, :]
        query_parts = head_parts(query, head_dim)
        grad_parts = head_parts(grad, head_dim)
        same = segc == segr_ref[:, here]
        gq = None
        for a in range(group):
            s = dot_nt(keys[a], query)
            bias = jnp.concatenate(
                [
                    diag_ref[a, :, LANES * (tiles - t) + c * chunk : LANES * (tiles - t) + (c + 1) * chunk]
                    for t in range(tiles)
                ],
                axis=0,
            )
            s = jnp.where(same, s + bias, -1000000000.0)
            e = jnp.exp(s - jnp.max(s, axis=0, keepdims=True))
            p = e * (1.0 / jnp.sum(e, axis=0, keepdims=True))
            gp = dot_nt(values[a], grad)
            gs = p * (gp - jnp.sum(p * gp, axis=0, keepdims=True))
            gs = gs.astype(jnp.bfloat16)
            p = p.astype(jnp.bfloat16)
            gs_f = gs.astype(jnp.float32)
            for t in range(tiles):
                at = LANES * (tiles - t) + c * chunk
                fold_ref[a, :, at : at + chunk] += gs_f[t * LANES : (t + 1) * LANES]
            part = dot_nn(gs, query_parts[a])
            gk[0] = part if gk[0] is None else gk[0] + part
            part = dot_nn(p, grad_parts[a])
            gv[0] = part if gv[0] is None else gv[0] + part
            part = dot_tn(gs, keys[a])
            gq = part if gq is None else gq + part
        gq_ref[here, :] = gq.astype(gq_ref.dtype)
    gk_ref[...] = gk[0].astype(gk_ref.dtype)
    gv_ref[...] = gv[0].astype(gv_ref.dtype)

    @pl.when(micro == pl.num_programs(1) - 1)
    def _():
        for a in range(group):
            gb_ref[a] = fold_diagonals(fold_ref[a])


def attention_specs(length, width, group, span, first):
    return (
        pl.BlockSpec((length, width), lambda h, m: (m, first + h)),
        pl.BlockSpec((length, 1), lambda h, m: (m, 0)),
        pl.BlockSpec((None, 1, length), lambda h, m: (m, 0, 0)),
        pl.BlockSpec((group, 1, span), lambda h, m: (first + h, 0, 0)),
    )


def attention(query, key, value, segment, rows, head_dim):
    micro_count, length = segment.shape
    model_width = query.shape[1]
    width = max(LANES, head_dim)
    group = width // head_dim
    block, segc, segr, line = attention_specs(length, width, group, rows.shape[2], 0)
    return pl.pallas_call(
        lambda *refs: forward_kernel(head_dim, *refs),
        name="attention_forward",
        grid=(model_width // width, micro_count),
        in_specs=[block, block, block, segc, segr, line],
        out_specs=block,
        out_shape=jax.ShapeDtypeStruct(query.shape, jnp.bfloat16),
        scratch_shapes=[pltpu.VMEM((group, LANES, rows.shape[2]), jnp.float32)],
    )(query, key, value, segment.reshape(-1, 1), segment[:, None, :], rows)


def attention_grads(query, key, value, grad, segment, rows, head_dim, part, parts, before):
    micro_count, length = segment.shape
    model_width = query.shape[1]
    width = max(LANES, head_dim)
    group = width // head_dim
    count = model_width // width // parts
    first = part * count
    block, segc, segr, line = attention_specs(length, width, group, rows.shape[2], first)
    flat = jax.ShapeDtypeStruct(query.shape, jnp.bfloat16)
    kept = len(before)

    def kernel(*refs):
        backward_kernel(head_dim, *refs[:7], *refs[7 + kept :])

    return pl.pallas_call(
        kernel,
        name="attention_backward",
        grid=(count, micro_count),
        in_specs=[block, block, block, block, segc, segr, line]
        + [pl.BlockSpec(memory_space=pl.ANY)] * kept,
        out_specs=[block, block, block, line],
        out_shape=[flat, flat, flat, jax.ShapeDtypeStruct(rows.shape, jnp.float32)],
        input_output_aliases={7 + n: n for n in range(kept)},
        scratch_shapes=[pltpu.VMEM((group, LANES, rows.shape[2]), jnp.float32)] * 2,
    )(query, key, value, grad, segment.reshape(-1, 1), segment[:, None, :], rows, *before)


class Net:
    def __init__(self):
        self.dp = lax.axis_size("dp")
        self.size = self.dp * lax.axis_size("tower")
        self.index = lax.axis_index("tower") * self.dp + lax.axis_index("dp")
        self.count = self.size.bit_length() - 1
        if self.count == 5:
            self.stages = (((0,), (0,)), ((4,), (1,)), ((1,), (4,)), ((2, 3), (2, 3)))
        else:
            self.stages = tuple(((b,), (b,)) for b in range(self.count))
        self.digits = [self.digit_of(stage) for stage in self.stages]

    def bit(self, b):
        return (self.index >> b) & 1

    def digit_of(self, stage):
        first, second = (sum(self.bit(b) << n for n, b in enumerate(bits)) for bits in stage)
        return first if stage[0] == stage[1] else jnp.where(self.bit(0) == 0, first, second)

    def swap(self, value, b):
        return lax.ppermute(value, AXES, [(i, i ^ (1 << b)) for i in range(self.size)])

    def peers(self, k):
        return range(1, 1 << len(self.stages[k][0]))

    def send(self, value, k, r):
        return self.send_by(value, self.stages[k], r)

    def send_by(self, value, stage, r):
        masks = [sum(((r >> n) & 1) << b for n, b in enumerate(bits)) for bits in stage]
        return lax.ppermute(value, AXES, [(i, i ^ masks[i & 1]) for i in range(self.size)])

    def collect(self, value, stage):
        peers = range(1, 1 << len(stage[0]))
        return place([value, *(self.send_by(value, stage, r) for r in peers)], self.digit_of(stage))


def place(pieces, digit):
    rows, width = pieces[0].shape
    source = lax.broadcasted_iota(jnp.int32, (len(pieces), rows, width), 0) ^ digit
    value = pieces[0][None]
    for r, piece in enumerate(pieces[1:], 1):
        value = jnp.where(source == r, piece[None], value)
    return value.reshape(len(pieces) * rows, width)


def part_of(value, which, count):
    rows = value.shape[0] // count
    return lax.dynamic_slice_in_dim(value, which * rows, rows, 0)


def weight_grads(bit, lefts, rights):
    height = lefts[0].shape[1] // 2
    width = min(r.shape[1] for r in rights)
    rows = max(r for r in range(LANES, min(height, 512) + 1, LANES) if height % r == 0)
    stacks = height // rows
    ends = [sum(r.shape[1] for r in rights[: n + 1]) // width for n in range(len(rights))]
    starts = [end - r.shape[1] // width for end, r in zip(ends, rights)]
    columns = ends[-1]
    count = len(lefts)
    fresh = [n == 0 or lefts[n] is not lefts[n - 1] for n in range(count)]
    owners = [max(m for m in range(n + 1) if fresh[m]) for n in range(count)]

    def kernel(bit_ref, *refs):
        other_refs, own_refs, right_refs = (refs[n * count : (n + 1) * count] for n in range(3))
        sent_ref, kept_ref = refs[3 * count : 3 * count + 2]
        turned_refs = refs[3 * count + 2 :]
        column = pl.program_id(1)

        def one(n):
            if fresh[n]:

                @pl.when(column == starts[n])
                def _():
                    turned_refs[n][:rows] = other_refs[n][...].T
                    turned_refs[n][rows:] = own_refs[n][...].T

            value = dot_nn(turned_refs[owners[n]][...], right_refs[n][...])
            sent_ref[...] = value[:rows]
            kept_ref[...] = value[rows:]

        for n in range(count):
            pl.when((column >= starts[n]) & (column < ends[n]))(lambda n=n: one(n))

    def left_place(side):
        def index(stack, column, bit_ref):
            half = jnp.where(side == 0, 1 - bit_ref[0], bit_ref[0])
            return (0, half * stacks + stack)

        return index

    def right_place(start, end):
        return lambda stack, column, bit_ref: (0, jnp.clip(column - start, 0, end - start - 1))

    return pl.pallas_call(
        kernel,
        name="weight_grads",
        grid_spec=pltpu.PrefetchScalarGridSpec(
            num_scalar_prefetch=1,
            grid=(stacks, columns),
            in_specs=[
                pl.BlockSpec((v.shape[0], rows), left_place(side)) for side in (0, 1) for v in lefts
            ]
            + [
                pl.BlockSpec((v.shape[0], width), right_place(start, end))
                for v, start, end in zip(rights, starts, ends)
            ],
            out_specs=[pl.BlockSpec((rows, width), lambda stack, column, bit_ref: (stack, column))]
            * 2,
            scratch_shapes=[pltpu.VMEM((2 * rows, v.shape[0]), v.dtype) for v in lefts],
        ),
        out_shape=[jax.ShapeDtypeStruct((height, columns * width), jnp.float32)] * 2,
    )(bit.reshape(1), *lefts, *lefts, *rights)


def row_tiles(rows):
    tile = min(rows, TILE)

    def lines(n):
        return pl.BlockSpec((tile, n), lambda t: (t, 0))

    def whole(*shape):
        return pl.BlockSpec(shape, lambda t: (0, 0))

    return tile, lines, whole


def norm_backward(values, grad, gain, sum_ref):
    scale = lax.rsqrt(jnp.mean(values * values, axis=1, keepdims=True) + norm_epsilon)
    unit = values * scale

    @pl.when(pl.program_id(0) == 0)
    def _():
        sum_ref[...] = jnp.zeros_like(sum_ref)

    sum_ref[...] += jnp.sum(grad * unit, axis=0, keepdims=True)
    scaled = grad * gain
    return scale * (scaled - unit * jnp.mean(unit * scaled, axis=1, keepdims=True))


def project_backward_kernel(
    gq_ref, gk_ref, gv_ref, gh_ref, x_ref, gain_ref, wq_ref, wk_ref, wv_ref, gx_ref, gg_ref
):
    grad = (
        dot_nt(gq_ref[...], wq_ref[...])
        + dot_nt(gk_ref[...], wk_ref[...])
        + dot_nt(gv_ref[...], wv_ref[...])
    )
    values = x_ref[...].astype(jnp.float32)
    gx_ref[...] = gh_ref[...] + norm_backward(values, grad, gain_ref[...], gg_ref)


def project_backward(grads, grad_hidden, states, gain, weights):
    rows, width = grad_hidden.shape
    tile, lines, whole = row_tiles(rows)
    return pl.pallas_call(
        project_backward_kernel,
        name="project_backward",
        grid=(rows // tile,),
        in_specs=[lines(width)] * 5 + [whole(1, width)] + [whole(width, width)] * 3,
        out_specs=[lines(width), whole(1, width)],
        out_shape=[
            jax.ShapeDtypeStruct((rows, width), jnp.float32),
            jax.ShapeDtypeStruct((1, width), jnp.float32),
        ],
    )(*grads, grad_hidden, states, gain[None], *weights)


def feed_backward_kernel(
    go_ref, act_ref, hid_ref, gain_ref, wff_ref, win_ref, wout_ref,
    gu_ref, gh_ref, ghl_ref, gm_ref, gg_ref,
):
    grad_output = go_ref[...]
    grad_activ = dot_nt(grad_output.astype(jnp.bfloat16), wff_ref[...])
    grad_inner = jnp.where(act_ref[...] > 0, grad_activ, 0.0).astype(jnp.bfloat16)
    gu_ref[...] = grad_inner
    grad_normed = dot_nt(grad_inner, win_ref[...])
    grad_hidden = grad_output + norm_backward(hid_ref[...], grad_normed, gain_ref[...], gg_ref)
    gh_ref[...] = grad_hidden
    low = grad_hidden.astype(jnp.bfloat16)
    ghl_ref[...] = low
    gm_ref[...] = dot_nt(low, wout_ref[...]).astype(jnp.bfloat16)


def feed_backward(grad_output, activ, hidden, gain, w_ffout, w_in, w_out):
    rows, width = grad_output.shape
    inner = activ.shape[1]
    tile, lines, whole = row_tiles(rows)
    return pl.pallas_call(
        feed_backward_kernel,
        name="feed_backward",
        grid=(rows // tile,),
        in_specs=[
            lines(width),
            lines(inner),
            lines(width),
            whole(1, width),
            whole(inner, width),
            whole(width, inner),
            whole(width, width),
        ],
        out_specs=[lines(inner), lines(width), lines(width), lines(width), whole(1, width)],
        out_shape=[
            jax.ShapeDtypeStruct((rows, inner), jnp.bfloat16),
            jax.ShapeDtypeStruct((rows, width), jnp.float32),
            jax.ShapeDtypeStruct((rows, width), jnp.bfloat16),
            jax.ShapeDtypeStruct((rows, width), jnp.bfloat16),
            jax.ShapeDtypeStruct((1, width), jnp.float32),
        ],
    )(grad_output, activ, hidden, gain[None], w_ffout, w_in, w_out)


def put(pieces, places, count, widths, before=()):
    rows, wide = pieces[0].shape
    splits = 1
    while rows % (16 * splits) == 0 and rows // splits * wide > 320 * 1024:
        splits *= 2
    block = rows // splits
    number, kept = len(pieces), len(before)

    def kernel(places_ref, *refs):
        out_refs = refs[number + kept :]

        def copy(source):
            at = 0
            for out, width in zip(out_refs, widths):
                out[...] = source[:, at : at + width]
                at += width

        for n in range(number):
            pl.when(pl.program_id(0) // splits == n)(lambda n=n: copy(refs[n]))

    def source(n):
        return lambda step, places_ref: (jnp.clip(step - n * splits, 0, splits - 1), 0)

    def target(step, places_ref):
        return (places_ref[step // splits] * splits + step % splits, 0)

    return pl.pallas_call(
        kernel,
        name="put",
        grid_spec=pltpu.PrefetchScalarGridSpec(
            num_scalar_prefetch=1,
            grid=(number * splits,),
            in_specs=[pl.BlockSpec((block, wide), source(n)) for n in range(number)]
            + [pl.BlockSpec(memory_space=pl.ANY)] * kept,
            out_specs=[pl.BlockSpec((block, w), target) for w in widths],
        ),
        out_shape=[jax.ShapeDtypeStruct((count * rows, w), pieces[0].dtype) for w in widths],
        input_output_aliases={1 + number + n: n for n in range(kept)},
    )(jnp.stack(places), *pieces, *before)


def tie(*values):
    return lax.optimization_barrier(values)


class Sum:
    def __init__(self, net, lefts, rights):
        self.net = net
        self.widths = [r.shape[1] for r in rights]
        self.step = 0
        self.back = False
        self.done = False
        sent, kept = weight_grads(net.digits[0], lefts, rights)
        self.held = [[sent], [kept]]
        self.cuts = [[]]

    def go(self):
        net = self.net
        if not self.back:
            self.got = [
                net.send(v, self.step, r) for r, v in zip(net.peers(self.step), self.held[0])
            ]
            return
        (piece,) = self.held
        k = self.step - 1
        self.got = [net.send(piece, k, r) for r in net.peers(k)]
        self.whole = piece.shape[0] % 8 == 0
        if self.whole:
            widths = [piece.shape[1]] if k else self.widths
            self.base = put([piece], [net.digits[k]], len(self.got) + 1, widths)

    def end(self):
        net = self.net
        if self.back:
            self.step -= 1
            k = self.step
            self.done = k == 0
            digit, peers = net.digits[k], net.peers(k)
            if self.whole:
                widths = self.widths if self.done else [self.held[0].shape[1]]
                self.held = put(
                    self.got, [digit ^ r for r in peers], len(peers) + 1, widths, self.base
                )
            else:
                self.held = [place([self.held[0], *self.got], digit)]
                if self.done:
                    ends = [sum(self.widths[: n + 1]) for n in range(len(self.widths))]
                    self.held = [
                        self.held[0][:, end - width : end] for end, width in zip(ends, self.widths)
                    ]
            return
        terms = [*self.held[1], *self.got]
        self.cuts += [[] for _ in self.got]
        self.step += 1
        self.back = self.step == len(net.stages)

        def total(more):
            value = None
            for term, cuts in zip(terms, self.cuts):
                for which, count in cuts + more:
                    term = part_of(term, which, count)
                value = term if value is None else value + term
            return value

        if self.back:
            self.held = [total([])]
            return
        digit, peers = net.digits[self.step], net.peers(self.step)
        count = len(peers) + 1
        self.held = [[total([(digit ^ r, count)]) for r in peers], terms]
        for cuts in self.cuts:
            cuts.append((digit, count))


def tie_all(sums, *values):
    values, held = tie(values, [s.held for s in sums])
    for s, h in zip(sums, held):
        s.held = h
    return values


def advance(sums):
    for s in sums:
        s.go()
    for s in sums:
        s.end()


def local(
    states,
    segment_ids,
    lengths,
    positives,
    w_query,
    w_key,
    w_value,
    w_out,
    w_in,
    w_ffout,
    w_proj,
    gain_attn,
    gain_ffn,
    gain_final,
    rel_bias,
):
    micro_count = states.shape[1]
    length = states.shape[2]
    model_width = states.shape[3]
    item_count = lengths.shape[2]
    bucket_count, head_count = rel_bias.shape
    head_dim = model_width // head_count
    ff_width = w_in.shape[1]
    tower_index = lax.axis_index("tower")
    dp_index = lax.axis_index("dp")
    dp_count = lax.axis_size("dp")
    row_count = item_count * dp_count
    rows = micro_count * length
    net = Net()
    bits = net.count

    offset = jnp.arange(2 * length, dtype=jnp.int32) - length
    code = bucket_code(offset, bucket_count)
    code_back = bucket_code(-offset, bucket_count)

    def bias_rows(which):
        return jnp.dot(which, rel_bias, precision=highest).T[:, None, :]

    segment = segment_ids[0]

    states_f = states[0].reshape(rows, model_width).astype(jnp.float32)
    normed = rms_scale(states_f, gain_attn)
    normed_low = normed.astype(jnp.bfloat16)
    query_low = mm(normed_low, w_query).astype(jnp.bfloat16)
    key_low = mm(normed_low, w_key).astype(jnp.bfloat16)
    value_low = mm(normed_low, w_value).astype(jnp.bfloat16)
    mixed_low = attention(query_low, key_low, value_low, segment, bias_rows(code), head_dim)
    hidden = states_f + mm(mixed_low, w_out)
    normed_two = rms_scale(hidden, gain_ffn)
    normed_two_low = normed_two.astype(jnp.bfloat16)
    activ_low = jnp.maximum(mm(normed_two_low, w_in), 0.0).astype(jnp.bfloat16)
    output = hidden + mm(activ_low, w_ffout)
    final_norm, back_final = jax.vjp(rms_scale, output, gain_final)
    member = (segment[:, :, None] == jnp.arange(item_count, dtype=jnp.int32)).astype(jnp.float32)
    count_f = lengths[0].astype(jnp.float32)[:, :, None]
    pooled_low = (
        jnp.einsum(
            "btc,btf->bcf",
            member,
            final_norm.reshape(micro_count, length, model_width),
            precision=highest,
        )
        / count_f
    ).astype(jnp.bfloat16)
    pooled_flat = pooled_low.reshape(micro_count * item_count, model_width)
    embed = mm(pooled_flat, w_proj)
    unit_embed, back_unit = jax.vjp(unit_rows, embed)

    every = unit_embed
    if bits == 5:
        for k in (3, 1, 2):
            every = net.collect(every, net.stages[k])
        every = every.reshape(2, 2, -1, model_width)
        every = jnp.where(net.bit(0) == 0, jnp.swapaxes(every, 0, 1), every)
        every = net.collect(every.reshape(-1, model_width), net.stages[0])
        every = every.reshape(2, 2, 2, -1, micro_count, item_count, model_width)
        every = jnp.transpose(every, (4, 1, 3, 2, 0, 5, 6))
    else:
        for b in range(bits):
            every = net.collect(every, ((b,), (b,)))
        every = every.reshape(2, net.dp, micro_count, item_count, model_width)
        every = jnp.transpose(every, (2, 0, 1, 3, 4))
    every = every.reshape(micro_count, 2, row_count, model_width)
    queries_all = every[:, 0]
    passages_all = every[:, 1]
    columns = jnp.arange(row_count, dtype=jnp.int32)[None, :]
    loss_sum = jnp.zeros((), jnp.float32)
    grad_embed = []
    for m in range(micro_count):
        logits = logit_scale * jnp.dot(queries_all[m], passages_all[m].T, precision=highest)
        target_hot = (columns == positives[m][:, None]).astype(jnp.float32)
        loss_part, grad_logits = softmax_terms(logits, target_hot)
        loss_sum = loss_sum + loss_part
        own_rows = lax.dynamic_slice_in_dim(grad_logits, dp_index * item_count, item_count, 0)
        own_cols = lax.dynamic_slice_in_dim(grad_logits, dp_index * item_count, item_count, 1)
        own = jnp.where(tower_index == 0, own_rows, own_cols.T)
        others = jnp.where(tower_index == 0, passages_all[m], queries_all[m])
        grad_embed.append(logit_scale * jnp.dot(own, others, precision=highest))
    grad_embed = jnp.concatenate(grad_embed, axis=0)
    (grad_e,) = back_unit(grad_embed)
    grad_e_low = grad_e.astype(jnp.bfloat16)
    grad_pooled = mm_t(grad_e_low, w_proj).reshape(micro_count, item_count, model_width)
    grad_final_norm = jnp.einsum(
        "btc,bcf->btf", member, grad_pooled / count_f, precision=highest
    ).reshape(rows, model_width)
    grad_output, grad_gain_final = back_final(grad_final_norm)
    grad_output_low = grad_output.astype(jnp.bfloat16)

    first = Sum(net, [activ_low], [grad_output_low])
    (grad_output,) = tie_all([first], grad_output)
    first.go()
    grad_inner_low, grad_hidden, grad_hidden_low, grad_mixed, grad_gain_ffn = feed_backward(
        grad_output, activ_low, hidden, gain_ffn, w_ffout, w_in, w_out
    )
    first.end()
    grad_inner_low, grad_hidden_low, grad_mixed = tie_all(
        [first], grad_inner_low, grad_hidden_low, grad_mixed
    )
    first.go()
    parts = 3
    rows_back = bias_rows(code_back)

    def attention_part(part, query, before):
        return attention_grads(
            query, key_low, value_low, grad_mixed, segment, rows_back, head_dim, part, parts, before
        )

    grads = attention_part(0, query_low, ())
    second = Sum(
        net,
        [normed_two_low, mixed_low, pooled_flat],
        [grad_inner_low, grad_hidden_low, grad_e_low],
    )
    first.end()
    query_low, grads = tie_all([first, second], query_low, grads)
    first.go()
    second.go()
    grads = attention_part(1, query_low, grads)
    first.end()
    second.end()
    query_low, grads = tie_all([first, second], query_low, grads)
    first.go()
    second.go()
    grads = attention_part(2, query_low, grads)
    *grad_heads, grad_rows = grads
    third = Sum(net, [normed_low] * 3, grad_heads)
    grad_states, grad_gain_attn = project_backward(
        grad_heads,
        grad_hidden,
        states[0].reshape(rows, model_width),
        gain_attn,
        (w_query, w_key, w_value),
    )
    first.end()
    second.end()
    grad_bias = jnp.einsum("hx,xb->bh", grad_rows[:, 0], code_back, precision=highest)
    small = jnp.concatenate(
        [grad_gain_attn[0], grad_gain_ffn[0], grad_gain_final, grad_bias.reshape(-1)]
    )
    lines = -(-small.shape[0] // (8 * LANES)) * 8
    small = jnp.pad(small, (0, lines * LANES - small.shape[0])).reshape(lines, LANES)
    sums = [first, second, third]
    small, grad_states = tie_all(sums, small, grad_states)
    def swap_small(value, which):
        for b in which:
            value = value + net.swap(value, b)
        return value

    if bits == 5:
        advance(sums)
        (small,) = tie_all(sums, small)
        advance(sums)
        small = swap_small(small, (0, 1, 2))
        (small,) = tie_all(sums, small)
        advance(sums)
        small = swap_small(small, (3, 4))
        tie_all(sums)
        first.go()
        advance([second, third])
        tie_all([second, third])
        second.go()
        third.go()
        first.end()
        third.end()
        third.go()
        first.held, second.base = tie(first.held, second.base)
        second.end()
        third.end()
        tie_all([second, third])
        third.go()
        second.go()
        second.end()
        second.held, third.base = tie(second.held, third.base)
        third.end()
        tie_all([second, third])
        advance([third])
    else:
        while not all(s.done for s in sums):
            advance([s for s in sums if not s.done])
        small = swap_small(small, range(bits))
    (whole_ffout,) = first.held
    whole_in, whole_out, whole_proj = second.held
    whole_query, whole_key, whole_value = third.held
    small = small.reshape(-1)
    loss = loss_sum / (micro_count * row_count)
    width = model_width
    return (
        loss,
        unit_embed.reshape(1, micro_count, item_count, model_width),
        grad_states.reshape(1, micro_count, length, model_width),
        whole_query,
        whole_key,
        whole_value,
        whole_out,
        whole_in,
        whole_ffout,
        whole_proj,
        small[:width],
        small[width : 2 * width],
        small[2 * width : 3 * width],
        small[3 * width : 3 * width + bucket_count * head_count].reshape(
            bucket_count, head_count
        ),
    )


def solution(mesh):
    return jax.shard_map(
        local,
        mesh=mesh,
        in_specs=(
            P("tower", None, "dp", None),
            P("tower", None, "dp"),
            P("tower", None, "dp"),
        )
        + (P(),) * 12,
        out_specs=(P(), P("tower", None, "dp", None), P("tower", None, "dp", None)) + (P(),) * 11,
        check_vma=False,
    )
```

```python
import jax
import jax.numpy as jnp
from jax import lax
from jax.experimental import pallas as pl
from jax.experimental.pallas import tpu as pltpu
from jax.sharding import PartitionSpec as P

highest = lax.Precision.HIGHEST
norm_epsilon = 1e-06
logit_scale = 50.0
bucket_edges = (12, 16, 23, 32, 46, 64, 91)
AXES = ("tower", "dp")
LANES = 128
TILE = 256
BIAS_AT = 32


def bucket_code(offset, bucket_count):
    distance = jnp.abs(offset)
    far_bucket = jnp.full_like(distance, 8)
    for edge_value in bucket_edges:
        far_bucket = far_bucket + (distance >= edge_value).astype(jnp.int32)
    bucket = jnp.where(distance < 8, distance, far_bucket) + jnp.where(offset > 0, 16, 0)
    return (bucket[:, None] == jnp.arange(bucket_count, dtype=jnp.int32)[None, :]).astype(jnp.float32)


def rms_scale(values, gain_vec):
    return (
        values
        * lax.rsqrt(jnp.mean(values * values, axis=-1, keepdims=True) + norm_epsilon)
        * gain_vec
    )


def unit_rows(values):
    return values * lax.rsqrt(jnp.sum(values * values, axis=-1, keepdims=True) + norm_epsilon)


def softmax_terms(logits, target_hot):
    maxima = jnp.max(logits, axis=1, keepdims=True)
    log_total = maxima + jnp.log(jnp.sum(jnp.exp(logits - maxima), axis=1, keepdims=True))
    loss_part = jnp.sum(log_total[:, 0] - jnp.sum(logits * target_hot, axis=1))
    return (loss_part, jnp.exp(logits - log_total) - target_hot)


def mm(a, b):
    return jnp.dot(a, b, preferred_element_type=jnp.float32)


def mm_t(a, b):
    return lax.dot_general(a, b, (((1,), (1,)), ((), ())), preferred_element_type=jnp.float32)


def dot_nt(a, b):
    return lax.dot_general(a, b, (((1,), (1,)), ((), ())), preferred_element_type=jnp.float32)

def dot_tn(a, b):
    return lax.dot_general(a, b, (((0,), (0,)), ((), ())), preferred_element_type=jnp.float32)

def dot_nn(a, b):
    return lax.dot_general(a, b, (((1,), (0,)), ((), ())), preferred_element_type=jnp.float32)


def head_parts(value, head_dim):
    lane = lax.broadcasted_iota(jnp.int32, value.shape, 1)
    zero = jnp.zeros_like(value)
    return [
        jnp.where((lane >= a * head_dim) & (lane < (a + 1) * head_dim), value, zero)
        for a in range(value.shape[1] // head_dim)
    ]


def diagonals(row):
    wide = jnp.broadcast_to(row, (LANES, row.shape[1]))
    return pltpu.roll(wide, 0, 1, stride=1, stride_axis=0)


def forward_kernel(head_dim, q_ref, k_ref, v_ref, segc_ref, segr_ref, rows_ref, o_ref, diag_ref):
    length, width = q_ref.shape
    group = width // head_dim
    tiles = length // LANES

    @pl.when(pl.program_id(1) == 0)
    def _():
        for a in range(group):
            diag_ref[a] = diagonals(rows_ref[a])

    keys = head_parts(k_ref[...], head_dim)
    values = head_parts(v_ref[...], head_dim)
    segr = segr_ref[...]
    deep = 2
    for c in range(tiles // deep):
        here = slice(c * deep * LANES, (c + 1) * deep * LANES)
        query = q_ref[here, :]
        same = segc_ref[here, :] == segr
        total = None
        for a in range(group):
            s = dot_nt(query, keys[a])
            bias = [
                diag_ref[a, :, LANES * (tiles - t) : LANES * (tiles - t) + length]
                for t in range(c * deep, (c + 1) * deep)
            ]
            s = s + jnp.concatenate(bias, axis=0)
            s = jnp.where(same, s, -1000000000.0)
            e = jnp.exp(s - jnp.max(s, axis=1, keepdims=True))
            p = e * (1.0 / jnp.sum(e, axis=1, keepdims=True))
            part = dot_nn(p.astype(jnp.bfloat16), values[a])
            total = part if total is None else total + part
        o_ref[here, :] = total.astype(o_ref.dtype)


def fold_diagonals(value):
    n = value.shape[1]
    rows = value.shape[0]
    while rows > 1:
        rows //= 2
        value = value[:rows] + pltpu.roll(value[rows:], n - rows, 1)
    return value


def backward_kernel(head_dim, q_ref, k_ref, v_ref, g_ref, segc_ref, segr_ref, rows_ref,
                    gq_ref, gk_ref, gv_ref, gb_ref, diag_ref, fold_ref):
    length, width = q_ref.shape
    group = width // head_dim
    tiles = length // LANES
    micro = pl.program_id(1)

    @pl.when(micro == 0)
    def _():
        for a in range(group):
            diag_ref[a] = diagonals(rows_ref[a])
        fold_ref[...] = jnp.zeros_like(fold_ref)

    keys = head_parts(k_ref[...], head_dim)
    values = head_parts(v_ref[...], head_dim)
    segc = segc_ref[...]
    chunk = length
    gk = [None]
    gv = [None]
    for c in range(length // chunk):
        here = slice(c * chunk, (c + 1) * chunk)
        query = q_ref[here, :]
        grad = g_ref[here, :]
        query_parts = head_parts(query, head_dim)
        grad_parts = head_parts(grad, head_dim)
        same = segc == segr_ref[:, here]
        gq = None
        for a in range(group):
            s = dot_nt(keys[a], query)
            bias = jnp.concatenate(
                [
                    diag_ref[a, :, LANES * (tiles - t) + c * chunk : LANES * (tiles - t) + (c + 1) * chunk]
                    for t in range(tiles)
                ],
                axis=0,
            )
            s = jnp.where(same, s + bias, -1000000000.0)
            e = jnp.exp(s - jnp.max(s, axis=0, keepdims=True))
            p = e * (1.0 / jnp.sum(e, axis=0, keepdims=True))
            gp = dot_nt(values[a], grad)
            gs = p * (gp - jnp.sum(p * gp, axis=0, keepdims=True))
            gs = gs.astype(jnp.bfloat16)
            p = p.astype(jnp.bfloat16)
            gs_f = gs.astype(jnp.float32)
            for t in range(tiles):
                at = LANES * (tiles - t) + c * chunk
                fold_ref[a, :, at : at + chunk] += gs_f[t * LANES : (t + 1) * LANES]
            part = dot_nn(gs, query_parts[a])
            gk[0] = part if gk[0] is None else gk[0] + part
            part = dot_nn(p, grad_parts[a])
            gv[0] = part if gv[0] is None else gv[0] + part
            part = dot_tn(gs, keys[a])
            gq = part if gq is None else gq + part
        gq_ref[here, :] = gq.astype(gq_ref.dtype)
    gk_ref[...] = gk[0].astype(gk_ref.dtype)
    gv_ref[...] = gv[0].astype(gv_ref.dtype)

    @pl.when(micro == pl.num_programs(1) - 1)
    def _():
        for a in range(group):
            gb_ref[a] = fold_diagonals(fold_ref[a])


def attention_specs(length, width, group, span, first):
    return (
        pl.BlockSpec((length, width), lambda h, m: (m, first + h)),
        pl.BlockSpec((length, 1), lambda h, m: (m, 0)),
        pl.BlockSpec((None, 1, length), lambda h, m: (m, 0, 0)),
        pl.BlockSpec((group, 1, span), lambda h, m: (first + h, 0, 0)),
    )


def attention(query, key, value, segment, rows, head_dim):
    micro_count, length = segment.shape
    model_width = query.shape[1]
    width = max(LANES, head_dim)
    group = width // head_dim
    block, segc, segr, line = attention_specs(length, width, group, rows.shape[2], 0)
    return pl.pallas_call(
        lambda *refs: forward_kernel(head_dim, *refs),
        name="attention_forward",
        grid=(model_width // width, micro_count),
        in_specs=[block, block, block, segc, segr, line],
        out_specs=block,
        out_shape=jax.ShapeDtypeStruct(query.shape, jnp.bfloat16),
        scratch_shapes=[pltpu.VMEM((group, LANES, rows.shape[2]), jnp.float32)],
    )(query, key, value, segment.reshape(-1, 1), segment[:, None, :], rows)


def attention_grads(query, key, value, grad, segment, rows, head_dim, part, parts, before):
    micro_count, length = segment.shape
    model_width = query.shape[1]
    width = max(LANES, head_dim)
    group = width // head_dim
    count = model_width // width // parts
    first = part * count
    block, segc, segr, line = attention_specs(length, width, group, rows.shape[2], first)
    flat = jax.ShapeDtypeStruct(query.shape, jnp.bfloat16)
    kept = len(before)

    def kernel(*refs):
        backward_kernel(head_dim, *refs[:7], *refs[7 + kept :])

    return pl.pallas_call(
        kernel,
        name="attention_backward",
        grid=(count, micro_count),
        in_specs=[block, block, block, block, segc, segr, line]
        + [pl.BlockSpec(memory_space=pl.ANY)] * kept,
        out_specs=[block, block, block, line],
        out_shape=[flat, flat, flat, jax.ShapeDtypeStruct(rows.shape, jnp.float32)],
        input_output_aliases={7 + n: n for n in range(kept)},
        scratch_shapes=[pltpu.VMEM((group, LANES, rows.shape[2]), jnp.float32)] * 2,
    )(query, key, value, grad, segment.reshape(-1, 1), segment[:, None, :], rows, *before)


def pack_small(gains, grad_rows, code):
    width = gains[0].shape[1]
    heads = grad_rows.shape[0]
    buckets = code.shape[0]

    def kernel(*refs):
        *gain_refs, rows_ref, code_ref, out_ref = refs
        line = lax.broadcasted_iota(jnp.int32, (LANES, width), 0)
        value = jnp.zeros((LANES, width), jnp.float32)
        for n, ref in enumerate(gain_refs):
            value = jnp.where(line == n, ref[...], value)
        out_ref[...] = value.T
        lane = lax.broadcasted_iota(jnp.int32, (buckets, LANES), 1)
        value = out_ref[:buckets, :]
        for h in range(heads):
            part = jnp.sum(code_ref[...] * rows_ref[h], axis=1, keepdims=True)
            value = jnp.where(lane == BIAS_AT + h, part, value)
        out_ref[:buckets, :] = value

    return pl.pallas_call(
        kernel,
        name="pack_small",
        out_shape=jax.ShapeDtypeStruct((width, LANES), jnp.float32),
    )(*gains, grad_rows, code)


class Net:
    def __init__(self):
        self.dp = lax.axis_size("dp")
        self.size = self.dp * lax.axis_size("tower")
        self.index = lax.axis_index("tower") * self.dp + lax.axis_index("dp")
        self.count = self.size.bit_length() - 1
        if self.count == 5:
            self.stages = (((0,), (0,)), ((4,), (1,)), ((1,), (4,)), ((2, 3), (2, 3)))
        else:
            self.stages = tuple(((b,), (b,)) for b in range(self.count))
        self.digits = [self.digit_of(stage) for stage in self.stages]

    def bit(self, b):
        return (self.index >> b) & 1

    def digit_of(self, stage):
        first, second = (sum(self.bit(b) << n for n, b in enumerate(bits)) for bits in stage)
        return first if stage[0] == stage[1] else jnp.where(self.bit(0) == 0, first, second)

    def swap(self, value, b):
        return lax.ppermute(value, AXES, [(i, i ^ (1 << b)) for i in range(self.size)])

    def peers(self, k):
        return range(1, 1 << len(self.stages[k][0]))

    def send(self, value, k, r):
        return self.send_by(value, self.stages[k], r)

    def send_by(self, value, stage, r):
        masks = [sum(((r >> n) & 1) << b for n, b in enumerate(bits)) for bits in stage]
        return lax.ppermute(value, AXES, [(i, i ^ masks[i & 1]) for i in range(self.size)])

    def collect(self, value, stage):
        peers = range(1, 1 << len(stage[0]))
        return place([value, *(self.send_by(value, stage, r) for r in peers)], self.digit_of(stage))


def place(pieces, digit):
    rows, width = pieces[0].shape
    source = lax.broadcasted_iota(jnp.int32, (len(pieces), rows, width), 0) ^ digit
    value = pieces[0][None]
    for r, piece in enumerate(pieces[1:], 1):
        value = jnp.where(source == r, piece[None], value)
    return value.reshape(len(pieces) * rows, width)


def part_of(value, which, count):
    rows = value.shape[0] // count
    return lax.dynamic_slice_in_dim(value, which * rows, rows, 0)


def weight_grads(bit, lefts, rights, extra=()):
    height = lefts[0].shape[1] // 2
    width = min(r.shape[1] for r in rights)
    rows = max(r for r in range(LANES, min(height, 512) + 1, LANES) if height % r == 0)
    stacks = height // rows
    ends = [sum(r.shape[1] for r in rights[: n + 1]) // width for n in range(len(rights))]
    starts = [end - r.shape[1] // width for end, r in zip(ends, rights)]
    columns = ends[-1]
    count = len(lefts)
    narrow = len(extra)
    total = columns * width + sum(v.shape[1] for v in extra)
    fresh = [n == 0 or lefts[n] is not lefts[n - 1] for n in range(count)]
    owners = [max(m for m in range(n + 1) if fresh[m]) for n in range(count)]

    def kernel(bit_ref, *refs):
        other_refs, own_refs, right_refs = (refs[n * count : (n + 1) * count] for n in range(3))
        extra_refs, refs = refs[3 * count : 3 * count + 2 * narrow], refs[3 * count + 2 * narrow :]
        sent_ref, kept_ref = refs[:2]
        turned_refs = refs[2:]
        column = pl.program_id(1)

        def one(n):
            if fresh[n]:

                @pl.when(column == starts[n])
                def _():
                    turned_refs[n][:rows] = other_refs[n][...].T
                    turned_refs[n][rows:] = own_refs[n][...].T

            value = dot_nn(turned_refs[owners[n]][...], right_refs[n][...])
            sent_ref[...] = value[:rows]
            kept_ref[...] = value[rows:]

        for n in range(count):
            pl.when((column >= starts[n]) & (column < ends[n]))(lambda n=n: one(n))

        if narrow:

            @pl.when(column == columns)
            def _():
                sent_ref[:, : extra[0].shape[1]] = extra_refs[0][...]
                kept_ref[:, : extra[0].shape[1]] = extra_refs[1][...]

    def row_place(side):
        def index(stack, column, bit_ref):
            half = jnp.where(side == 0, 1 - bit_ref[0], bit_ref[0])
            return half * stacks + stack

        return index

    def left_place(side):
        return lambda *at: (0, row_place(side)(*at))

    def extra_place(side):
        return lambda *at: (row_place(side)(*at), 0)

    def right_place(start, end):
        return lambda stack, column, bit_ref: (0, jnp.clip(column - start, 0, end - start - 1))

    return pl.pallas_call(
        kernel,
        name="weight_grads",
        grid_spec=pltpu.PrefetchScalarGridSpec(
            num_scalar_prefetch=1,
            grid=(stacks, columns + narrow),
            in_specs=[
                pl.BlockSpec((v.shape[0], rows), left_place(side)) for side in (0, 1) for v in lefts
            ]
            + [
                pl.BlockSpec((v.shape[0], width), right_place(start, end))
                for v, start, end in zip(rights, starts, ends)
            ]
            + [
                pl.BlockSpec((rows, v.shape[1]), extra_place(side)) for side in (0, 1) for v in extra
            ],
            out_specs=[pl.BlockSpec((rows, width), lambda stack, column, bit_ref: (stack, column))]
            * 2,
            scratch_shapes=[pltpu.VMEM((2 * rows, v.shape[0]), v.dtype) for v in lefts],
        ),
        out_shape=[jax.ShapeDtypeStruct((height, total), jnp.float32)] * 2,
    )(bit.reshape(1), *lefts, *lefts, *rights, *extra, *extra)


def row_tiles(rows):
    tile = min(rows, TILE)

    def lines(n):
        return pl.BlockSpec((tile, n), lambda t: (t, 0))

    def whole(*shape):
        return pl.BlockSpec(shape, lambda t: (0, 0))

    return tile, lines, whole


def norm_backward(values, grad, gain, sum_ref):
    scale = lax.rsqrt(jnp.mean(values * values, axis=1, keepdims=True) + norm_epsilon)
    unit = values * scale

    @pl.when(pl.program_id(0) == 0)
    def _():
        sum_ref[...] = jnp.zeros_like(sum_ref)

    sum_ref[...] += jnp.sum(grad * unit, axis=0, keepdims=True)
    scaled = grad * gain
    return scale * (scaled - unit * jnp.mean(unit * scaled, axis=1, keepdims=True))


def project_backward_kernel(
    gq_ref, gk_ref, gv_ref, gh_ref, x_ref, gain_ref, wq_ref, wk_ref, wv_ref, gx_ref, gg_ref
):
    grad = (
        dot_nt(gq_ref[...], wq_ref[...])
        + dot_nt(gk_ref[...], wk_ref[...])
        + dot_nt(gv_ref[...], wv_ref[...])
    )
    values = x_ref[...].astype(jnp.float32)
    gx_ref[...] = gh_ref[...] + norm_backward(values, grad, gain_ref[...], gg_ref)


def project_backward(grads, grad_hidden, states, gain, weights):
    rows, width = grad_hidden.shape
    tile, lines, whole = row_tiles(rows)
    return pl.pallas_call(
        project_backward_kernel,
        name="project_backward",
        grid=(rows // tile,),
        in_specs=[lines(width)] * 5 + [whole(1, width)] + [whole(width, width)] * 3,
        out_specs=[lines(width), whole(1, width)],
        out_shape=[
            jax.ShapeDtypeStruct((rows, width), jnp.float32),
            jax.ShapeDtypeStruct((1, width), jnp.float32),
        ],
    )(*grads, grad_hidden, states, gain[None], *weights)


def feed_backward_kernel(
    go_ref, act_ref, hid_ref, gain_ref, wff_ref, win_ref, wout_ref,
    gu_ref, gh_ref, ghl_ref, gm_ref, gg_ref,
):
    grad_output = go_ref[...]
    grad_activ = dot_nt(grad_output.astype(jnp.bfloat16), wff_ref[...])
    grad_inner = jnp.where(act_ref[...] > 0, grad_activ, 0.0).astype(jnp.bfloat16)
    gu_ref[...] = grad_inner
    grad_normed = dot_nt(grad_inner, win_ref[...])
    grad_hidden = grad_output + norm_backward(hid_ref[...], grad_normed, gain_ref[...], gg_ref)
    gh_ref[...] = grad_hidden
    low = grad_hidden.astype(jnp.bfloat16)
    ghl_ref[...] = low
    gm_ref[...] = dot_nt(low, wout_ref[...]).astype(jnp.bfloat16)


def feed_backward(grad_output, activ, hidden, gain, w_ffout, w_in, w_out):
    rows, width = grad_output.shape
    inner = activ.shape[1]
    tile, lines, whole = row_tiles(rows)
    return pl.pallas_call(
        feed_backward_kernel,
        name="feed_backward",
        grid=(rows // tile,),
        in_specs=[
            lines(width),
            lines(inner),
            lines(width),
            whole(1, width),
            whole(inner, width),
            whole(width, inner),
            whole(width, width),
        ],
        out_specs=[lines(inner), lines(width), lines(width), lines(width), whole(1, width)],
        out_shape=[
            jax.ShapeDtypeStruct((rows, inner), jnp.bfloat16),
            jax.ShapeDtypeStruct((rows, width), jnp.float32),
            jax.ShapeDtypeStruct((rows, width), jnp.bfloat16),
            jax.ShapeDtypeStruct((rows, width), jnp.bfloat16),
            jax.ShapeDtypeStruct((1, width), jnp.float32),
        ],
    )(grad_output, activ, hidden, gain[None], w_ffout, w_in, w_out)


def put(pieces, places, count, widths, before=()):
    rows, wide = pieces[0].shape
    splits = 1
    while rows % (16 * splits) == 0 and rows // splits * wide > 320 * 1024:
        splits *= 2
    block = rows // splits
    number, kept = len(pieces), len(before)

    def kernel(places_ref, *refs):
        out_refs = refs[number + kept :]

        def copy(source):
            at = 0
            for out, width in zip(out_refs, widths):
                out[...] = source[:, at : at + width]
                at += width

        for n in range(number):
            pl.when(pl.program_id(0) // splits == n)(lambda n=n: copy(refs[n]))

    def source(n):
        return lambda step, places_ref: (jnp.clip(step - n * splits, 0, splits - 1), 0)

    def target(step, places_ref):
        return (places_ref[step // splits] * splits + step % splits, 0)

    return pl.pallas_call(
        kernel,
        name="put",
        grid_spec=pltpu.PrefetchScalarGridSpec(
            num_scalar_prefetch=1,
            grid=(number * splits,),
            in_specs=[pl.BlockSpec((block, wide), source(n)) for n in range(number)]
            + [pl.BlockSpec(memory_space=pl.ANY)] * kept,
            out_specs=[pl.BlockSpec((block, w), target) for w in widths],
        ),
        out_shape=[jax.ShapeDtypeStruct((count * rows, w), pieces[0].dtype) for w in widths],
        input_output_aliases={1 + number + n: n for n in range(kept)},
    )(jnp.stack(places), *pieces, *before)


def tie(*values):
    return lax.optimization_barrier(values)


class Sum:
    def __init__(self, net, lefts, rights, extra=()):
        self.net = net
        self.widths = [v.shape[1] for v in (*rights, *extra)]
        self.step = 0
        self.back = False
        self.done = False
        sent, kept = weight_grads(net.digits[0], lefts, rights, extra)
        self.held = [[sent], [kept]]
        self.cuts = [[]]

    def go(self):
        net = self.net
        if not self.back:
            self.got = [
                net.send(v, self.step, r) for r, v in zip(net.peers(self.step), self.held[0])
            ]
            return
        (piece,) = self.held
        k = self.step - 1
        self.got = [net.send(piece, k, r) for r in net.peers(k)]
        self.whole = piece.shape[0] % 8 == 0 and len(self.got) == 1
        if self.whole:
            widths = [piece.shape[1]] if k else self.widths
            self.base = put([piece], [net.digits[k]], len(self.got) + 1, widths)

    def end(self):
        net = self.net
        if self.back:
            self.step -= 1
            k = self.step
            self.done = k == 0
            digit, peers = net.digits[k], net.peers(k)
            if self.whole:
                widths = self.widths if self.done else [self.held[0].shape[1]]
                self.held = put(
                    self.got, [digit ^ r for r in peers], len(peers) + 1, widths, self.base
                )
            else:
                self.held = [place([self.held[0], *self.got], digit)]
                if self.done:
                    ends = [sum(self.widths[: n + 1]) for n in range(len(self.widths))]
                    self.held = [
                        self.held[0][:, end - width : end] for end, width in zip(ends, self.widths)
                    ]
            return
        terms = [*self.held[1], *self.got]
        self.cuts += [[] for _ in self.got]
        self.step += 1
        self.back = self.step == len(net.stages)

        def total(more):
            value = None
            for term, cuts in zip(terms, self.cuts):
                for which, count in cuts + more:
                    term = part_of(term, which, count)
                value = term if value is None else value + term
            return value

        if self.back:
            self.held = [total([])]
            return
        digit, peers = net.digits[self.step], net.peers(self.step)
        count = len(peers) + 1
        self.held = [[total([(digit ^ r, count)]) for r in peers], terms]
        for cuts in self.cuts:
            cuts.append((digit, count))


def tie_all(sums, *values):
    values, held = tie(values, [s.held for s in sums])
    for s, h in zip(sums, held):
        s.held = h
    return values


def advance(sums):
    for s in sums:
        s.go()
    for s in sums:
        s.end()


def local(
    states,
    segment_ids,
    lengths,
    positives,
    w_query,
    w_key,
    w_value,
    w_out,
    w_in,
    w_ffout,
    w_proj,
    gain_attn,
    gain_ffn,
    gain_final,
    rel_bias,
):
    micro_count = states.shape[1]
    length = states.shape[2]
    model_width = states.shape[3]
    item_count = lengths.shape[2]
    bucket_count, head_count = rel_bias.shape
    head_dim = model_width // head_count
    ff_width = w_in.shape[1]
    tower_index = lax.axis_index("tower")
    dp_index = lax.axis_index("dp")
    dp_count = lax.axis_size("dp")
    row_count = item_count * dp_count
    rows = micro_count * length
    net = Net()
    bits = net.count

    offset = jnp.arange(2 * length, dtype=jnp.int32) - length
    code = bucket_code(offset, bucket_count)
    code_back = bucket_code(-offset, bucket_count)

    def bias_rows(which):
        return jnp.dot(which, rel_bias, precision=highest).T[:, None, :]

    segment = segment_ids[0]

    states_f = states[0].reshape(rows, model_width).astype(jnp.float32)
    normed = rms_scale(states_f, gain_attn)
    normed_low = normed.astype(jnp.bfloat16)
    query_low = mm(normed_low, w_query).astype(jnp.bfloat16)
    key_low = mm(normed_low, w_key).astype(jnp.bfloat16)
    value_low = mm(normed_low, w_value).astype(jnp.bfloat16)
    mixed_low = attention(query_low, key_low, value_low, segment, bias_rows(code), head_dim)
    hidden = states_f + mm(mixed_low, w_out)
    normed_two = rms_scale(hidden, gain_ffn)
    normed_two_low = normed_two.astype(jnp.bfloat16)
    activ_low = jnp.maximum(mm(normed_two_low, w_in), 0.0).astype(jnp.bfloat16)
    output = hidden + mm(activ_low, w_ffout)
    final_norm, back_final = jax.vjp(rms_scale, output, gain_final)
    member = (segment[:, :, None] == jnp.arange(item_count, dtype=jnp.int32)).astype(jnp.float32)
    count_f = lengths[0].astype(jnp.float32)[:, :, None]
    pooled_low = (
        jnp.einsum(
            "btc,btf->bcf",
            member,
            final_norm.reshape(micro_count, length, model_width),
            precision=highest,
        )
        / count_f
    ).astype(jnp.bfloat16)
    pooled_flat = pooled_low.reshape(micro_count * item_count, model_width)
    embed = mm(pooled_flat, w_proj)
    unit_embed, back_unit = jax.vjp(unit_rows, embed)

    every = unit_embed
    if bits == 5:
        for k in (3, 1, 2):
            every = net.collect(every, net.stages[k])
        every = every.reshape(2, 2, -1, model_width)
        every = jnp.where(net.bit(0) == 0, jnp.swapaxes(every, 0, 1), every)
        every = net.collect(every.reshape(-1, model_width), net.stages[0])
        every = every.reshape(2, 2, 2, -1, micro_count, item_count, model_width)
        every = jnp.transpose(every, (4, 1, 3, 2, 0, 5, 6))
    else:
        for b in range(bits):
            every = net.collect(every, ((b,), (b,)))
        every = every.reshape(2, net.dp, micro_count, item_count, model_width)
        every = jnp.transpose(every, (2, 0, 1, 3, 4))
    every = every.reshape(micro_count, 2, row_count, model_width)
    queries_all = every[:, 0]
    passages_all = every[:, 1]
    columns = jnp.arange(row_count, dtype=jnp.int32)[None, :]
    loss_sum = jnp.zeros((), jnp.float32)
    grad_embed = []
    for m in range(micro_count):
        logits = logit_scale * jnp.dot(queries_all[m], passages_all[m].T, precision=highest)
        target_hot = (columns == positives[m][:, None]).astype(jnp.float32)
        loss_part, grad_logits = softmax_terms(logits, target_hot)
        loss_sum = loss_sum + loss_part
        own_rows = lax.dynamic_slice_in_dim(grad_logits, dp_index * item_count, item_count, 0)
        own_cols = lax.dynamic_slice_in_dim(grad_logits, dp_index * item_count, item_count, 1)
        own = jnp.where(tower_index == 0, own_rows, own_cols.T)
        others = jnp.where(tower_index == 0, passages_all[m], queries_all[m])
        grad_embed.append(logit_scale * jnp.dot(own, others, precision=highest))
    grad_embed = jnp.concatenate(grad_embed, axis=0)
    (grad_e,) = back_unit(grad_embed)
    grad_e_low = grad_e.astype(jnp.bfloat16)
    grad_pooled = mm_t(grad_e_low, w_proj).reshape(micro_count, item_count, model_width)
    grad_final_norm = jnp.einsum(
        "btc,bcf->btf", member, grad_pooled / count_f, precision=highest
    ).reshape(rows, model_width)
    grad_output, grad_gain_final = back_final(grad_final_norm)
    grad_output_low = grad_output.astype(jnp.bfloat16)

    first = Sum(net, [activ_low], [grad_output_low])
    (grad_output,) = tie_all([first], grad_output)
    first.go()
    grad_inner_low, grad_hidden, grad_hidden_low, grad_mixed, grad_gain_ffn = feed_backward(
        grad_output, activ_low, hidden, gain_ffn, w_ffout, w_in, w_out
    )
    first.end()
    grad_inner_low, grad_hidden_low, grad_mixed = tie_all(
        [first], grad_inner_low, grad_hidden_low, grad_mixed
    )
    first.go()
    parts = 3
    rows_back = bias_rows(code_back)

    def attention_part(part, query, before):
        return attention_grads(
            query, key_low, value_low, grad_mixed, segment, rows_back, head_dim, part, parts, before
        )

    grads = attention_part(0, query_low, ())
    second = Sum(
        net,
        [normed_two_low, mixed_low, pooled_flat],
        [grad_inner_low, grad_hidden_low, grad_e_low],
    )
    first.end()
    query_low, grads = tie_all([first, second], query_low, grads)
    first.go()
    second.go()
    grads = attention_part(1, query_low, grads)
    first.end()
    second.end()
    query_low, grads = tie_all([first, second], query_low, grads)
    first.go()
    second.go()
    grads = attention_part(2, query_low, grads)
    *grad_heads, grad_rows = grads
    grad_states, grad_gain_attn = project_backward(
        grad_heads,
        grad_hidden,
        states[0].reshape(rows, model_width),
        gain_attn,
        (w_query, w_key, w_value),
    )
    small = pack_small(
        (grad_gain_attn, grad_gain_ffn, grad_gain_final[None]), grad_rows, code_back.T
    )
    third = Sum(net, [normed_low] * 3, grad_heads, [small])
    first.end()
    second.end()
    sums = [first, second, third]
    (grad_states,) = tie_all(sums, grad_states)
    if bits == 5:
        for _ in range(3):
            advance(sums)
            tie_all(sums)
        for s in sums:
            s.go()
        first.end()
        first.held, second.base = tie(first.held, second.base)
        second.end()
        third.end()
        tie_all(sums)
        second.go()
        third.go()
        third.end()
        third.go()
        second.end()
        third.end()
        tie_all([second, third])
        third.go()
        second.go()
        second.end()
        second.held, third.base = tie(second.held, third.base)
        third.end()
        tie_all([second, third])
        advance([third])
    else:
        while not all(s.done for s in sums):
            advance([s for s in sums if not s.done])
    (whole_ffout,) = first.held
    whole_in, whole_out, whole_proj = second.held
    whole_query, whole_key, whole_value, small = third.held
    loss = loss_sum / (micro_count * row_count)
    width = model_width
    return (
        loss,
        unit_embed.reshape(1, micro_count, item_count, model_width),
        grad_states.reshape(1, micro_count, length, model_width),
        whole_query,
        whole_key,
        whole_value,
        whole_out,
        whole_in,
        whole_ffout,
        whole_proj,
        small[:, 0],
        small[:, 1],
        small[:, 2],
        small[:bucket_count, BIAS_AT : BIAS_AT + head_count],
    )


def solution(mesh):
    return jax.shard_map(
        local,
        mesh=mesh,
        in_specs=(
            P("tower", None, "dp", None),
            P("tower", None, "dp"),
            P("tower", None, "dp"),
        )
        + (P(),) * 12,
        out_specs=(P(), P("tower", None, "dp", None), P("tower", None, "dp", None)) + (P(),) * 11,
        check_vma=False,
    )
```

```python
import jax
import jax.numpy as jnp
from jax import lax
from jax.experimental import pallas as pl
from jax.experimental.pallas import tpu as pltpu
from jax.sharding import PartitionSpec as P

highest = lax.Precision.HIGHEST
norm_epsilon = 1e-06
logit_scale = 50.0
bucket_edges = (12, 16, 23, 32, 46, 64, 91)
AXES = ("tower", "dp")
LANES = 128
TILE = 256
BIAS_AT = 32


def bucket_code(offset, bucket_count):
    distance = jnp.abs(offset)
    far_bucket = jnp.full_like(distance, 8)
    for edge_value in bucket_edges:
        far_bucket = far_bucket + (distance >= edge_value).astype(jnp.int32)
    bucket = jnp.where(distance < 8, distance, far_bucket) + jnp.where(offset > 0, 16, 0)
    return (bucket[:, None] == jnp.arange(bucket_count, dtype=jnp.int32)[None, :]).astype(jnp.float32)


def rms_scale(values, gain_vec):
    return (
        values
        * lax.rsqrt(jnp.mean(values * values, axis=-1, keepdims=True) + norm_epsilon)
        * gain_vec
    )


def unit_rows(values):
    return values * lax.rsqrt(jnp.sum(values * values, axis=-1, keepdims=True) + norm_epsilon)


def softmax_terms(logits, target_hot):
    maxima = jnp.max(logits, axis=1, keepdims=True)
    log_total = maxima + jnp.log(jnp.sum(jnp.exp(logits - maxima), axis=1, keepdims=True))
    loss_part = jnp.sum(log_total[:, 0] - jnp.sum(logits * target_hot, axis=1))
    return (loss_part, jnp.exp(logits - log_total) - target_hot)


def mm(a, b):
    return jnp.dot(a, b, preferred_element_type=jnp.float32)


def mm_t(a, b):
    return lax.dot_general(a, b, (((1,), (1,)), ((), ())), preferred_element_type=jnp.float32)


def dot_nt(a, b):
    return lax.dot_general(a, b, (((1,), (1,)), ((), ())), preferred_element_type=jnp.float32)

def dot_tn(a, b):
    return lax.dot_general(a, b, (((0,), (0,)), ((), ())), preferred_element_type=jnp.float32)

def dot_nn(a, b):
    return lax.dot_general(a, b, (((1,), (0,)), ((), ())), preferred_element_type=jnp.float32)


def head_parts(value, head_dim):
    lane = lax.broadcasted_iota(jnp.int32, value.shape, 1)
    zero = jnp.zeros_like(value)
    return [
        jnp.where((lane >= a * head_dim) & (lane < (a + 1) * head_dim), value, zero)
        for a in range(value.shape[1] // head_dim)
    ]


def diagonals(row):
    wide = jnp.broadcast_to(row, (LANES, row.shape[1]))
    return pltpu.roll(wide, 0, 1, stride=1, stride_axis=0)


def forward_kernel(head_dim, q_ref, k_ref, v_ref, segc_ref, segr_ref, rows_ref, o_ref, diag_ref):
    length, width = q_ref.shape
    group = width // head_dim
    tiles = length // LANES

    @pl.when(pl.program_id(1) == 0)
    def _():
        for a in range(group):
            diag_ref[a] = diagonals(rows_ref[a])

    keys = head_parts(k_ref[...], head_dim)
    values = head_parts(v_ref[...], head_dim)
    segr = segr_ref[...]
    deep = 2
    for c in range(tiles // deep):
        here = slice(c * deep * LANES, (c + 1) * deep * LANES)
        query = q_ref[here, :]
        same = segc_ref[here, :] == segr
        total = None
        for a in range(group):
            s = dot_nt(query, keys[a])
            bias = [
                diag_ref[a, :, LANES * (tiles - t) : LANES * (tiles - t) + length]
                for t in range(c * deep, (c + 1) * deep)
            ]
            s = s + jnp.concatenate(bias, axis=0)
            s = jnp.where(same, s, -1000000000.0)
            e = jnp.exp(s - jnp.max(s, axis=1, keepdims=True))
            p = e * (1.0 / jnp.sum(e, axis=1, keepdims=True))
            part = dot_nn(p.astype(jnp.bfloat16), values[a])
            total = part if total is None else total + part
        o_ref[here, :] = total.astype(o_ref.dtype)


def fold_diagonals(value):
    n = value.shape[1]
    rows = value.shape[0]
    while rows > 1:
        rows //= 2
        value = value[:rows] + pltpu.roll(value[rows:], n - rows, 1)
    return value


def backward_kernel(head_dim, q_ref, k_ref, v_ref, g_ref, segc_ref, segr_ref, rows_ref,
                    gq_ref, gk_ref, gv_ref, gb_ref, diag_ref, fold_ref):
    length, width = q_ref.shape
    group = width // head_dim
    tiles = length // LANES
    micro = pl.program_id(1)

    @pl.when(micro == 0)
    def _():
        for a in range(group):
            diag_ref[a] = diagonals(rows_ref[a])
        fold_ref[...] = jnp.zeros_like(fold_ref)

    keys = head_parts(k_ref[...], head_dim)
    values = head_parts(v_ref[...], head_dim)
    segc = segc_ref[...]
    chunk = length
    gk = [None]
    gv = [None]
    for c in range(length // chunk):
        here = slice(c * chunk, (c + 1) * chunk)
        query = q_ref[here, :]
        grad = g_ref[here, :]
        query_parts = head_parts(query, head_dim)
        grad_parts = head_parts(grad, head_dim)
        same = segc == segr_ref[:, here]
        gq = None
        for a in range(group):
            s = dot_nt(keys[a], query)
            bias = jnp.concatenate(
                [
                    diag_ref[a, :, LANES * (tiles - t) + c * chunk : LANES * (tiles - t) + (c + 1) * chunk]
                    for t in range(tiles)
                ],
                axis=0,
            )
            s = jnp.where(same, s + bias, -1000000000.0)
            e = jnp.exp(s - jnp.max(s, axis=0, keepdims=True))
            p = e * (1.0 / jnp.sum(e, axis=0, keepdims=True))
            gp = dot_nt(values[a], grad)
            gs = p * (gp - jnp.sum(p * gp, axis=0, keepdims=True))
            gs = gs.astype(jnp.bfloat16)
            p = p.astype(jnp.bfloat16)
            gs_f = gs.astype(jnp.float32)
            for t in range(tiles):
                at = LANES * (tiles - t) + c * chunk
                fold_ref[a, :, at : at + chunk] += gs_f[t * LANES : (t + 1) * LANES]
            part = dot_nn(gs, query_parts[a])
            gk[0] = part if gk[0] is None else gk[0] + part
            part = dot_nn(p, grad_parts[a])
            gv[0] = part if gv[0] is None else gv[0] + part
            part = dot_tn(gs, keys[a])
            gq = part if gq is None else gq + part
        gq_ref[here, :] = gq.astype(gq_ref.dtype)
    gk_ref[...] = gk[0].astype(gk_ref.dtype)
    gv_ref[...] = gv[0].astype(gv_ref.dtype)

    @pl.when(micro == pl.num_programs(1) - 1)
    def _():
        for a in range(group):
            gb_ref[a] = fold_diagonals(fold_ref[a])


def attention_specs(length, width, group, span, first):
    return (
        pl.BlockSpec((length, width), lambda h, m: (m, first + h)),
        pl.BlockSpec((length, 1), lambda h, m: (m, 0)),
        pl.BlockSpec((None, 1, length), lambda h, m: (m, 0, 0)),
        pl.BlockSpec((group, 1, span), lambda h, m: (first + h, 0, 0)),
    )


def attention(query, key, value, segment, rows, head_dim):
    micro_count, length = segment.shape
    model_width = query.shape[1]
    width = max(LANES, head_dim)
    group = width // head_dim
    block, segc, segr, line = attention_specs(length, width, group, rows.shape[2], 0)
    return pl.pallas_call(
        lambda *refs: forward_kernel(head_dim, *refs),
        name="attention_forward",
        grid=(model_width // width, micro_count),
        in_specs=[block, block, block, segc, segr, line],
        out_specs=block,
        out_shape=jax.ShapeDtypeStruct(query.shape, jnp.bfloat16),
        scratch_shapes=[pltpu.VMEM((group, LANES, rows.shape[2]), jnp.float32)],
    )(query, key, value, segment.reshape(-1, 1), segment[:, None, :], rows)


def attention_grads(query, key, value, grad, segment, rows, head_dim, part, parts, before):
    micro_count, length = segment.shape
    model_width = query.shape[1]
    width = max(LANES, head_dim)
    group = width // head_dim
    count = model_width // width // parts
    first = part * count
    block, segc, segr, line = attention_specs(length, width, group, rows.shape[2], first)
    flat = jax.ShapeDtypeStruct(query.shape, jnp.bfloat16)
    kept = len(before)

    def kernel(*refs):
        backward_kernel(head_dim, *refs[:7], *refs[7 + kept :])

    return pl.pallas_call(
        kernel,
        name="attention_backward",
        grid=(count, micro_count),
        in_specs=[block, block, block, block, segc, segr, line]
        + [pl.BlockSpec(memory_space=pl.ANY)] * kept,
        out_specs=[block, block, block, line],
        out_shape=[flat, flat, flat, jax.ShapeDtypeStruct(rows.shape, jnp.float32)],
        input_output_aliases={7 + n: n for n in range(kept)},
        scratch_shapes=[pltpu.VMEM((group, LANES, rows.shape[2]), jnp.float32)] * 2,
    )(query, key, value, grad, segment.reshape(-1, 1), segment[:, None, :], rows, *before)


def pack_small(gains, grad_rows, code):
    width = gains[0].shape[1]
    heads = grad_rows.shape[0]
    buckets = code.shape[0]
    lines = width // LANES

    def kernel(*refs):
        *gain_refs, rows_ref, code_ref, out_ref = refs
        out_ref[...] = jnp.zeros_like(out_ref)
        for n, ref in enumerate(gain_refs):
            for line in range(lines):
                at = n * lines + line
                out_ref[at : at + 1, :] = ref[:, line * LANES : (line + 1) * LANES]
        lane = lax.broadcasted_iota(jnp.int32, (buckets, LANES), 1)
        value = jnp.zeros((buckets, LANES), jnp.float32)
        for h in range(heads):
            part = jnp.sum(code_ref[...] * rows_ref[h], axis=1, keepdims=True)
            value = jnp.where(lane == h, part, value)
        out_ref[BIAS_AT : BIAS_AT + buckets, :] = value

    return pl.pallas_call(
        kernel,
        name="pack_small",
        out_shape=jax.ShapeDtypeStruct((width, LANES), jnp.float32),
    )(*gains, grad_rows, code)


class Net:
    def __init__(self):
        self.dp = lax.axis_size("dp")
        self.size = self.dp * lax.axis_size("tower")
        self.index = lax.axis_index("tower") * self.dp + lax.axis_index("dp")
        self.count = self.size.bit_length() - 1
        if self.count == 5:
            self.stages = (((0,), (0,)), ((4,), (1,)), ((1,), (4,)), ((2, 3), (2, 3)))
        else:
            self.stages = tuple(((b,), (b,)) for b in range(self.count))
        self.digits = [self.digit_of(stage) for stage in self.stages]

    def bit(self, b):
        return (self.index >> b) & 1

    def digit_of(self, stage):
        first, second = (sum(self.bit(b) << n for n, b in enumerate(bits)) for bits in stage)
        return first if stage[0] == stage[1] else jnp.where(self.bit(0) == 0, first, second)

    def swap(self, value, b):
        return lax.ppermute(value, AXES, [(i, i ^ (1 << b)) for i in range(self.size)])

    def peers(self, k):
        return range(1, 1 << len(self.stages[k][0]))

    def send(self, value, k, r):
        return self.send_by(value, self.stages[k], r)

    def send_by(self, value, stage, r):
        masks = [sum(((r >> n) & 1) << b for n, b in enumerate(bits)) for bits in stage]
        return lax.ppermute(value, AXES, [(i, i ^ masks[i & 1]) for i in range(self.size)])

    def collect(self, value, stage):
        peers = range(1, 1 << len(stage[0]))
        return place([value, *(self.send_by(value, stage, r) for r in peers)], self.digit_of(stage))


def place(pieces, digit):
    rows, width = pieces[0].shape
    source = lax.broadcasted_iota(jnp.int32, (len(pieces), rows, width), 0) ^ digit
    value = pieces[0][None]
    for r, piece in enumerate(pieces[1:], 1):
        value = jnp.where(source == r, piece[None], value)
    return value.reshape(len(pieces) * rows, width)


def part_of(value, which, count):
    rows = value.shape[0] // count
    return lax.dynamic_slice_in_dim(value, which * rows, rows, 0)


def weight_grads(bit, lefts, rights, extra=()):
    height = lefts[0].shape[1] // 2
    width = min(r.shape[1] for r in rights)
    rows = max(r for r in range(LANES, min(height, 512) + 1, LANES) if height % r == 0)
    stacks = height // rows
    ends = [sum(r.shape[1] for r in rights[: n + 1]) // width for n in range(len(rights))]
    starts = [end - r.shape[1] // width for end, r in zip(ends, rights)]
    columns = ends[-1]
    count = len(lefts)
    narrow = len(extra)
    total = columns * width + sum(v.shape[1] for v in extra)
    fresh = [n == 0 or lefts[n] is not lefts[n - 1] for n in range(count)]
    owners = [max(m for m in range(n + 1) if fresh[m]) for n in range(count)]

    def kernel(bit_ref, *refs):
        other_refs, own_refs, right_refs = (refs[n * count : (n + 1) * count] for n in range(3))
        extra_refs, refs = refs[3 * count : 3 * count + 2 * narrow], refs[3 * count + 2 * narrow :]
        sent_ref, kept_ref = refs[:2]
        turned_refs = refs[2:]
        column = pl.program_id(1)

        def one(n):
            if fresh[n]:

                @pl.when(column == starts[n])
                def _():
                    turned_refs[n][:rows] = other_refs[n][...].T
                    turned_refs[n][rows:] = own_refs[n][...].T

            value = dot_nn(turned_refs[owners[n]][...], right_refs[n][...])
            sent_ref[...] = value[:rows]
            kept_ref[...] = value[rows:]

        for n in range(count):
            pl.when((column >= starts[n]) & (column < ends[n]))(lambda n=n: one(n))

        if narrow:

            @pl.when(column == columns)
            def _():
                sent_ref[:, : extra[0].shape[1]] = extra_refs[0][...]
                kept_ref[:, : extra[0].shape[1]] = extra_refs[1][...]

    def row_place(side):
        def index(stack, column, bit_ref):
            half = jnp.where(side == 0, 1 - bit_ref[0], bit_ref[0])
            return half * stacks + stack

        return index

    def left_place(side):
        return lambda *at: (0, row_place(side)(*at))

    def extra_place(side):
        return lambda *at: (row_place(side)(*at), 0)

    def right_place(start, end):
        return lambda stack, column, bit_ref: (0, jnp.clip(column - start, 0, end - start - 1))

    return pl.pallas_call(
        kernel,
        name="weight_grads",
        grid_spec=pltpu.PrefetchScalarGridSpec(
            num_scalar_prefetch=1,
            grid=(stacks, columns + narrow),
            in_specs=[
                pl.BlockSpec((v.shape[0], rows), left_place(side)) for side in (0, 1) for v in lefts
            ]
            + [
                pl.BlockSpec((v.shape[0], width), right_place(start, end))
                for v, start, end in zip(rights, starts, ends)
            ]
            + [
                pl.BlockSpec((rows, v.shape[1]), extra_place(side)) for side in (0, 1) for v in extra
            ],
            out_specs=[pl.BlockSpec((rows, width), lambda stack, column, bit_ref: (stack, column))]
            * 2,
            scratch_shapes=[pltpu.VMEM((2 * rows, v.shape[0]), v.dtype) for v in lefts],
        ),
        out_shape=[jax.ShapeDtypeStruct((height, total), jnp.float32)] * 2,
    )(bit.reshape(1), *lefts, *lefts, *rights, *extra, *extra)


def row_tiles(rows):
    tile = min(rows, TILE)

    def lines(n):
        return pl.BlockSpec((tile, n), lambda t: (t, 0))

    def whole(*shape):
        return pl.BlockSpec(shape, lambda t: (0, 0))

    return tile, lines, whole


def norm_low(values, gain):
    scale = lax.rsqrt(jnp.mean(values * values, axis=1, keepdims=True) + norm_epsilon)
    return (values * scale * gain).astype(jnp.bfloat16)


def project_kernel(x_ref, gain_ref, wq_ref, wk_ref, wv_ref, n_ref, q_ref, k_ref, v_ref):
    normed = norm_low(x_ref[...].astype(jnp.float32), gain_ref[...])
    n_ref[...] = normed
    for weight, out in ((wq_ref, q_ref), (wk_ref, k_ref), (wv_ref, v_ref)):
        out[...] = dot_nn(normed, weight[...]).astype(jnp.bfloat16)


def project(states, gain, weights):
    rows, width = states.shape
    tile, lines, whole = row_tiles(rows)
    return pl.pallas_call(
        project_kernel,
        name="project",
        grid=(rows // tile,),
        in_specs=[lines(width), whole(1, width)] + [whole(width, width)] * 3,
        out_specs=[lines(width)] * 4,
        out_shape=[jax.ShapeDtypeStruct((rows, width), jnp.bfloat16)] * 4,
    )(states, gain[None], *weights)


def feed_kernel(
    mix_ref, x_ref, gain_ref, wout_ref, win_ref, wff_ref, hid_ref, n_ref, act_ref, y_ref
):
    hidden = x_ref[...].astype(jnp.float32) + dot_nn(mix_ref[...], wout_ref[...])
    hid_ref[...] = hidden
    normed = norm_low(hidden, gain_ref[...])
    n_ref[...] = normed
    activ = jnp.maximum(dot_nn(normed, win_ref[...]), 0.0).astype(jnp.bfloat16)
    act_ref[...] = activ
    y_ref[...] = hidden + dot_nn(activ, wff_ref[...])


def feed(mixed, states, gain, w_out, w_in, w_ffout):
    rows, width = states.shape
    inner = w_in.shape[1]
    tile, lines, whole = row_tiles(rows)
    return pl.pallas_call(
        feed_kernel,
        name="feed_forward",
        grid=(rows // tile,),
        in_specs=[
            lines(width),
            lines(width),
            whole(1, width),
            whole(width, width),
            whole(width, inner),
            whole(inner, width),
        ],
        out_specs=[lines(width), lines(width), lines(inner), lines(width)],
        out_shape=[
            jax.ShapeDtypeStruct((rows, width), jnp.float32),
            jax.ShapeDtypeStruct((rows, width), jnp.bfloat16),
            jax.ShapeDtypeStruct((rows, inner), jnp.bfloat16),
            jax.ShapeDtypeStruct((rows, width), jnp.float32),
        ],
    )(mixed, states, gain[None], w_out, w_in, w_ffout)


def norm_backward(values, grad, gain, sum_ref):
    scale = lax.rsqrt(jnp.mean(values * values, axis=1, keepdims=True) + norm_epsilon)
    unit = values * scale

    @pl.when(pl.program_id(0) == 0)
    def _():
        sum_ref[...] = jnp.zeros_like(sum_ref)

    sum_ref[...] += jnp.sum(grad * unit, axis=0, keepdims=True)
    scaled = grad * gain
    return scale * (scaled - unit * jnp.mean(unit * scaled, axis=1, keepdims=True))


def project_backward_kernel(
    gq_ref, gk_ref, gv_ref, gh_ref, x_ref, gain_ref, wq_ref, wk_ref, wv_ref, gx_ref, gg_ref
):
    grad = (
        dot_nt(gq_ref[...], wq_ref[...])
        + dot_nt(gk_ref[...], wk_ref[...])
        + dot_nt(gv_ref[...], wv_ref[...])
    )
    values = x_ref[...].astype(jnp.float32)
    gx_ref[...] = gh_ref[...] + norm_backward(values, grad, gain_ref[...], gg_ref)


def project_backward(grads, grad_hidden, states, gain, weights):
    rows, width = grad_hidden.shape
    tile, lines, whole = row_tiles(rows)
    return pl.pallas_call(
        project_backward_kernel,
        name="project_backward",
        grid=(rows // tile,),
        in_specs=[lines(width)] * 5 + [whole(1, width)] + [whole(width, width)] * 3,
        out_specs=[lines(width), whole(1, width)],
        out_shape=[
            jax.ShapeDtypeStruct((rows, width), jnp.float32),
            jax.ShapeDtypeStruct((1, width), jnp.float32),
        ],
    )(*grads, grad_hidden, states, gain[None], *weights)


def feed_backward_kernel(
    go_ref, act_ref, hid_ref, gain_ref, wff_ref, win_ref, wout_ref,
    gu_ref, gh_ref, ghl_ref, gm_ref, gg_ref,
):
    grad_output = go_ref[...]
    grad_activ = dot_nt(grad_output.astype(jnp.bfloat16), wff_ref[...])
    grad_inner = jnp.where(act_ref[...] > 0, grad_activ, 0.0).astype(jnp.bfloat16)
    gu_ref[...] = grad_inner
    grad_normed = dot_nt(grad_inner, win_ref[...])
    grad_hidden = grad_output + norm_backward(hid_ref[...], grad_normed, gain_ref[...], gg_ref)
    gh_ref[...] = grad_hidden
    low = grad_hidden.astype(jnp.bfloat16)
    ghl_ref[...] = low
    gm_ref[...] = dot_nt(low, wout_ref[...]).astype(jnp.bfloat16)


def feed_backward(grad_output, activ, hidden, gain, w_ffout, w_in, w_out):
    rows, width = grad_output.shape
    inner = activ.shape[1]
    tile, lines, whole = row_tiles(rows)
    return pl.pallas_call(
        feed_backward_kernel,
        name="feed_backward",
        grid=(rows // tile,),
        in_specs=[
            lines(width),
            lines(inner),
            lines(width),
            whole(1, width),
            whole(inner, width),
            whole(width, inner),
            whole(width, width),
        ],
        out_specs=[lines(inner), lines(width), lines(width), lines(width), whole(1, width)],
        out_shape=[
            jax.ShapeDtypeStruct((rows, inner), jnp.bfloat16),
            jax.ShapeDtypeStruct((rows, width), jnp.float32),
            jax.ShapeDtypeStruct((rows, width), jnp.bfloat16),
            jax.ShapeDtypeStruct((rows, width), jnp.bfloat16),
            jax.ShapeDtypeStruct((1, width), jnp.float32),
        ],
    )(grad_output, activ, hidden, gain[None], w_ffout, w_in, w_out)


def put(pieces, places, count, widths, before=()):
    rows, wide = pieces[0].shape
    splits = 1
    while rows % (16 * splits) == 0 and rows // splits * wide > 320 * 1024:
        splits *= 2
    block = rows // splits
    number, kept = len(pieces), len(before)

    def kernel(places_ref, *refs):
        out_refs = refs[number + kept :]

        def copy(source):
            at = 0
            for out, width in zip(out_refs, widths):
                out[...] = source[:, at : at + width]
                at += width

        for n in range(number):
            pl.when(pl.program_id(0) // splits == n)(lambda n=n: copy(refs[n]))

    def source(n):
        return lambda step, places_ref: (jnp.clip(step - n * splits, 0, splits - 1), 0)

    def target(step, places_ref):
        return (places_ref[step // splits] * splits + step % splits, 0)

    return pl.pallas_call(
        kernel,
        name="put",
        grid_spec=pltpu.PrefetchScalarGridSpec(
            num_scalar_prefetch=1,
            grid=(number * splits,),
            in_specs=[pl.BlockSpec((block, wide), source(n)) for n in range(number)]
            + [pl.BlockSpec(memory_space=pl.ANY)] * kept,
            out_specs=[pl.BlockSpec((block, w), target) for w in widths],
        ),
        out_shape=[jax.ShapeDtypeStruct((count * rows, w), pieces[0].dtype) for w in widths],
        input_output_aliases={1 + number + n: n for n in range(kept)},
    )(jnp.stack(places), *pieces, *before)


def tie(*values):
    return lax.optimization_barrier(values)


class Sum:
    def __init__(self, net, lefts, rights, extra=()):
        self.net = net
        self.widths = [v.shape[1] for v in (*rights, *extra)]
        self.step = 0
        self.back = False
        self.done = False
        sent, kept = weight_grads(net.digits[0], lefts, rights, extra)
        self.held = [[sent], [kept]]
        self.cuts = [[]]

    def go(self):
        net = self.net
        if not self.back:
            self.got = [
                net.send(v, self.step, r) for r, v in zip(net.peers(self.step), self.held[0])
            ]
            return
        (piece,) = self.held
        k = self.step - 1
        self.got = [net.send(piece, k, r) for r in net.peers(k)]
        self.whole = piece.shape[0] % 8 == 0 and len(self.got) == 1
        if self.whole:
            widths = [piece.shape[1]] if k else self.widths
            self.base = put([piece], [net.digits[k]], len(self.got) + 1, widths)

    def end(self):
        net = self.net
        if self.back:
            self.step -= 1
            k = self.step
            self.done = k == 0
            digit, peers = net.digits[k], net.peers(k)
            if self.whole:
                widths = self.widths if self.done else [self.held[0].shape[1]]
                self.held = put(
                    self.got, [digit ^ r for r in peers], len(peers) + 1, widths, self.base
                )
            else:
                self.held = [place([self.held[0], *self.got], digit)]
                if self.done:
                    ends = [sum(self.widths[: n + 1]) for n in range(len(self.widths))]
                    self.held = [
                        self.held[0][:, end - width : end] for end, width in zip(ends, self.widths)
                    ]
            return
        terms = [*self.held[1], *self.got]
        self.cuts += [[] for _ in self.got]
        self.step += 1
        self.back = self.step == len(net.stages)

        def total(more):
            value = None
            for term, cuts in zip(terms, self.cuts):
                for which, count in cuts + more:
                    term = part_of(term, which, count)
                value = term if value is None else value + term
            return value

        if self.back:
            self.held = [total([])]
            return
        digit, peers = net.digits[self.step], net.peers(self.step)
        count = len(peers) + 1
        self.held = [[total([(digit ^ r, count)]) for r in peers], terms]
        for cuts in self.cuts:
            cuts.append((digit, count))


def tie_all(sums, *values):
    values, held = tie(values, [s.held for s in sums])
    for s, h in zip(sums, held):
        s.held = h
    return values


def advance(sums):
    for s in sums:
        s.go()
    for s in sums:
        s.end()


def local(
    states,
    segment_ids,
    lengths,
    positives,
    w_query,
    w_key,
    w_value,
    w_out,
    w_in,
    w_ffout,
    w_proj,
    gain_attn,
    gain_ffn,
    gain_final,
    rel_bias,
):
    micro_count = states.shape[1]
    length = states.shape[2]
    model_width = states.shape[3]
    item_count = lengths.shape[2]
    bucket_count, head_count = rel_bias.shape
    head_dim = model_width // head_count
    ff_width = w_in.shape[1]
    tower_index = lax.axis_index("tower")
    dp_index = lax.axis_index("dp")
    dp_count = lax.axis_size("dp")
    row_count = item_count * dp_count
    rows = micro_count * length
    net = Net()
    bits = net.count

    offset = jnp.arange(2 * length, dtype=jnp.int32) - length
    code = bucket_code(offset, bucket_count)
    code_back = bucket_code(-offset, bucket_count)

    def bias_rows(which):
        return jnp.dot(which, rel_bias, precision=highest).T[:, None, :]

    segment = segment_ids[0]

    states_low = states[0].reshape(rows, model_width)
    normed_low, query_low, key_low, value_low = project(
        states_low, gain_attn, (w_query, w_key, w_value)
    )
    mixed_low = attention(query_low, key_low, value_low, segment, bias_rows(code), head_dim)
    hidden = states_low.astype(jnp.float32) + mm(mixed_low, w_out)
    normed_two = rms_scale(hidden, gain_ffn)
    normed_two_low = normed_two.astype(jnp.bfloat16)
    activ_low = jnp.maximum(mm(normed_two_low, w_in), 0.0).astype(jnp.bfloat16)
    output = hidden + mm(activ_low, w_ffout)
    final_norm, back_final = jax.vjp(rms_scale, output, gain_final)
    member = (segment[:, :, None] == jnp.arange(item_count, dtype=jnp.int32)).astype(jnp.float32)
    count_f = lengths[0].astype(jnp.float32)[:, :, None]
    pooled_low = (
        jnp.einsum(
            "btc,btf->bcf",
            member,
            final_norm.reshape(micro_count, length, model_width),
            precision=highest,
        )
        / count_f
    ).astype(jnp.bfloat16)
    pooled_flat = pooled_low.reshape(micro_count * item_count, model_width)
    embed = mm(pooled_flat, w_proj)
    unit_embed, back_unit = jax.vjp(unit_rows, embed)

    every = unit_embed
    if bits == 5:
        for k in (3, 1, 2):
            every = net.collect(every, net.stages[k])
        every = every.reshape(2, 2, -1, model_width)
        every = jnp.where(net.bit(0) == 0, jnp.swapaxes(every, 0, 1), every)
        every = net.collect(every.reshape(-1, model_width), net.stages[0])
        every = every.reshape(2, 2, 2, -1, micro_count, item_count, model_width)
        every = jnp.transpose(every, (4, 1, 3, 2, 0, 5, 6))
    else:
        for b in range(bits):
            every = net.collect(every, ((b,), (b,)))
        every = every.reshape(2, net.dp, micro_count, item_count, model_width)
        every = jnp.transpose(every, (2, 0, 1, 3, 4))
    every = every.reshape(micro_count, 2, row_count, model_width)
    queries_all = every[:, 0]
    passages_all = every[:, 1]
    columns = jnp.arange(row_count, dtype=jnp.int32)[None, :]
    loss_sum = jnp.zeros((), jnp.float32)
    grad_embed = []
    for m in range(micro_count):
        logits = logit_scale * jnp.dot(queries_all[m], passages_all[m].T, precision=highest)
        target_hot = (columns == positives[m][:, None]).astype(jnp.float32)
        loss_part, grad_logits = softmax_terms(logits, target_hot)
        loss_sum = loss_sum + loss_part
        own_rows = lax.dynamic_slice_in_dim(grad_logits, dp_index * item_count, item_count, 0)
        own_cols = lax.dynamic_slice_in_dim(grad_logits, dp_index * item_count, item_count, 1)
        own = jnp.where(tower_index == 0, own_rows, own_cols.T)
        others = jnp.where(tower_index == 0, passages_all[m], queries_all[m])
        grad_embed.append(logit_scale * jnp.dot(own, others, precision=highest))
    grad_embed = jnp.concatenate(grad_embed, axis=0)
    (grad_e,) = back_unit(grad_embed)
    grad_e_low = grad_e.astype(jnp.bfloat16)
    grad_pooled = mm_t(grad_e_low, w_proj).reshape(micro_count, item_count, model_width)
    grad_final_norm = jnp.einsum(
        "btc,bcf->btf", member, grad_pooled / count_f, precision=highest
    ).reshape(rows, model_width)
    grad_output, grad_gain_final = back_final(grad_final_norm)
    grad_output_low = grad_output.astype(jnp.bfloat16)

    first = Sum(net, [activ_low], [grad_output_low])
    (grad_output,) = tie_all([first], grad_output)
    first.go()
    grad_inner_low, grad_hidden, grad_hidden_low, grad_mixed, grad_gain_ffn = feed_backward(
        grad_output, activ_low, hidden, gain_ffn, w_ffout, w_in, w_out
    )
    first.end()
    grad_inner_low, grad_hidden_low, grad_mixed = tie_all(
        [first], grad_inner_low, grad_hidden_low, grad_mixed
    )
    first.go()
    parts = 3
    rows_back = bias_rows(code_back)

    def attention_part(part, query, before):
        return attention_grads(
            query, key_low, value_low, grad_mixed, segment, rows_back, head_dim, part, parts, before
        )

    grads = attention_part(0, query_low, ())
    second = Sum(
        net,
        [normed_two_low, mixed_low, pooled_flat],
        [grad_inner_low, grad_hidden_low, grad_e_low],
    )
    first.end()
    query_low, grads = tie_all([first, second], query_low, grads)
    first.go()
    second.go()
    grads = attention_part(1, query_low, grads)
    first.end()
    second.end()
    query_low, grads = tie_all([first, second], query_low, grads)
    first.go()
    second.go()
    grads = attention_part(2, query_low, grads)
    *grad_heads, grad_rows = grads
    grad_states, grad_gain_attn = project_backward(
        grad_heads,
        grad_hidden,
        states_low,
        gain_attn,
        (w_query, w_key, w_value),
    )
    small = pack_small(
        (grad_gain_attn, grad_gain_ffn, grad_gain_final[None]), grad_rows, code_back.T
    )
    third = Sum(net, [normed_low] * 3, grad_heads, [small])
    first.end()
    second.end()
    sums = [first, second, third]
    (grad_states,) = tie_all(sums, grad_states)
    if bits == 5:
        for _ in range(3):
            advance(sums)
            tie_all(sums)
        for s in sums:
            s.go()
        second.end()
        third.end()
        second.held, third.held, first.base = tie(second.held, third.held, first.base)
        second.go()
        third.go()
        first.end()
        third.end()
        first.held, third.held = tie(first.held, third.held)
        third.go()
        second.end()
        third.end()
        tie_all([second, third])
        third.go()
        second.go()
        second.end()
        second.held, third.base = tie(second.held, third.base)
        third.end()
        tie_all([second, third])
        advance([third])
    else:
        while not all(s.done for s in sums):
            advance([s for s in sums if not s.done])
    (whole_ffout,) = first.held
    whole_in, whole_out, whole_proj = second.held
    whole_query, whole_key, whole_value, small = third.held
    lines = model_width // LANES
    loss = loss_sum / (micro_count * row_count)
    return (
        loss,
        unit_embed.reshape(1, micro_count, item_count, model_width),
        grad_states.reshape(1, micro_count, length, model_width),
        whole_query,
        whole_key,
        whole_value,
        whole_out,
        whole_in,
        whole_ffout,
        whole_proj,
        *(small[n * lines : (n + 1) * lines].reshape(-1) for n in range(3)),
        small[BIAS_AT : BIAS_AT + bucket_count, :head_count],
    )


def solution(mesh):
    return jax.shard_map(
        local,
        mesh=mesh,
        in_specs=(
            P("tower", None, "dp", None),
            P("tower", None, "dp"),
            P("tower", None, "dp"),
        )
        + (P(),) * 12,
        out_specs=(P(), P("tower", None, "dp", None), P("tower", None, "dp", None)) + (P(),) * 11,
        check_vma=False,
    )
```

```python
import jax
import jax.numpy as jnp
from jax import lax
from jax.experimental import pallas as pl
from jax.experimental.pallas import tpu as pltpu
from jax.sharding import PartitionSpec as P

highest = lax.Precision.HIGHEST
norm_epsilon = 1e-06
logit_scale = 50.0
bucket_edges = (12, 16, 23, 32, 46, 64, 91)
AXES = ("tower", "dp")
LANES = 128
TILE = 256
BIAS_AT = 32


def bucket_code(offset, bucket_count):
    distance = jnp.abs(offset)
    far_bucket = jnp.full_like(distance, 8)
    for edge_value in bucket_edges:
        far_bucket = far_bucket + (distance >= edge_value).astype(jnp.int32)
    bucket = jnp.where(distance < 8, distance, far_bucket) + jnp.where(offset > 0, 16, 0)
    return (bucket[:, None] == jnp.arange(bucket_count, dtype=jnp.int32)[None, :]).astype(jnp.float32)


def rms_scale(values, gain_vec):
    return (
        values
        * lax.rsqrt(jnp.mean(values * values, axis=-1, keepdims=True) + norm_epsilon)
        * gain_vec
    )


def unit_rows(values):
    return values * lax.rsqrt(jnp.sum(values * values, axis=-1, keepdims=True) + norm_epsilon)


def softmax_terms(logits, target_hot):
    maxima = jnp.max(logits, axis=1, keepdims=True)
    log_total = maxima + jnp.log(jnp.sum(jnp.exp(logits - maxima), axis=1, keepdims=True))
    loss_part = jnp.sum(log_total[:, 0] - jnp.sum(logits * target_hot, axis=1))
    return (loss_part, jnp.exp(logits - log_total) - target_hot)


def mm(a, b):
    return jnp.dot(a, b, preferred_element_type=jnp.float32)


def mm_t(a, b):
    return lax.dot_general(a, b, (((1,), (1,)), ((), ())), preferred_element_type=jnp.float32)


def dot_nt(a, b):
    return lax.dot_general(a, b, (((1,), (1,)), ((), ())), preferred_element_type=jnp.float32)

def dot_tn(a, b):
    return lax.dot_general(a, b, (((0,), (0,)), ((), ())), preferred_element_type=jnp.float32)

def dot_nn(a, b):
    return lax.dot_general(a, b, (((1,), (0,)), ((), ())), preferred_element_type=jnp.float32)


def head_parts(value, head_dim):
    lane = lax.broadcasted_iota(jnp.int32, value.shape, 1)
    zero = jnp.zeros_like(value)
    return [
        jnp.where((lane >= a * head_dim) & (lane < (a + 1) * head_dim), value, zero)
        for a in range(value.shape[1] // head_dim)
    ]


def diagonals(row):
    wide = jnp.broadcast_to(row, (LANES, row.shape[1]))
    return pltpu.roll(wide, 0, 1, stride=1, stride_axis=0)


def forward_kernel(head_dim, q_ref, k_ref, v_ref, segc_ref, segr_ref, rows_ref, o_ref, diag_ref):
    length, width = q_ref.shape
    group = width // head_dim
    tiles = length // LANES

    @pl.when(pl.program_id(1) == 0)
    def _():
        for a in range(group):
            diag_ref[a] = diagonals(rows_ref[a])

    keys = head_parts(k_ref[...], head_dim)
    values = head_parts(v_ref[...], head_dim)
    segr = segr_ref[...]
    deep = 2
    for c in range(tiles // deep):
        here = slice(c * deep * LANES, (c + 1) * deep * LANES)
        query = q_ref[here, :]
        same = segc_ref[here, :] == segr
        total = None
        for a in range(group):
            s = dot_nt(query, keys[a])
            bias = [
                diag_ref[a, :, LANES * (tiles - t) : LANES * (tiles - t) + length]
                for t in range(c * deep, (c + 1) * deep)
            ]
            s = s + jnp.concatenate(bias, axis=0)
            s = jnp.where(same, s, -1000000000.0)
            e = jnp.exp(s - jnp.max(s, axis=1, keepdims=True))
            p = e * (1.0 / jnp.sum(e, axis=1, keepdims=True))
            part = dot_nn(p.astype(jnp.bfloat16), values[a])
            total = part if total is None else total + part
        o_ref[here, :] = total.astype(o_ref.dtype)


def fold_diagonals(value):
    n = value.shape[1]
    rows = value.shape[0]
    while rows > 1:
        rows //= 2
        value = value[:rows] + pltpu.roll(value[rows:], n - rows, 1)
    return value


def backward_kernel(head_dim, q_ref, k_ref, v_ref, g_ref, segc_ref, segr_ref, rows_ref,
                    gq_ref, gk_ref, gv_ref, gb_ref, diag_ref, fold_ref):
    length, width = q_ref.shape
    group = width // head_dim
    tiles = length // LANES
    micro = pl.program_id(1)

    @pl.when(micro == 0)
    def _():
        for a in range(group):
            diag_ref[a] = diagonals(rows_ref[a])
        fold_ref[...] = jnp.zeros_like(fold_ref)

    keys = head_parts(k_ref[...], head_dim)
    values = head_parts(v_ref[...], head_dim)
    segc = segc_ref[...]
    chunk = length
    gk = [None]
    gv = [None]
    for c in range(length // chunk):
        here = slice(c * chunk, (c + 1) * chunk)
        query = q_ref[here, :]
        grad = g_ref[here, :]
        query_parts = head_parts(query, head_dim)
        grad_parts = head_parts(grad, head_dim)
        same = segc == segr_ref[:, here]
        gq = None
        for a in range(group):
            s = dot_nt(keys[a], query)
            bias = jnp.concatenate(
                [
                    diag_ref[a, :, LANES * (tiles - t) + c * chunk : LANES * (tiles - t) + (c + 1) * chunk]
                    for t in range(tiles)
                ],
                axis=0,
            )
            s = jnp.where(same, s + bias, -1000000000.0)
            e = jnp.exp(s - jnp.max(s, axis=0, keepdims=True))
            p = e * (1.0 / jnp.sum(e, axis=0, keepdims=True))
            gp = dot_nt(values[a], grad)
            gs = p * (gp - jnp.sum(p * gp, axis=0, keepdims=True))
            gs = gs.astype(jnp.bfloat16)
            p = p.astype(jnp.bfloat16)
            gs_f = gs.astype(jnp.float32)
            for t in range(tiles):
                at = LANES * (tiles - t) + c * chunk
                fold_ref[a, :, at : at + chunk] += gs_f[t * LANES : (t + 1) * LANES]
            part = dot_nn(gs, query_parts[a])
            gk[0] = part if gk[0] is None else gk[0] + part
            part = dot_nn(p, grad_parts[a])
            gv[0] = part if gv[0] is None else gv[0] + part
            part = dot_tn(gs, keys[a])
            gq = part if gq is None else gq + part
        gq_ref[here, :] = gq.astype(gq_ref.dtype)
    gk_ref[...] = gk[0].astype(gk_ref.dtype)
    gv_ref[...] = gv[0].astype(gv_ref.dtype)

    @pl.when(micro == pl.num_programs(1) - 1)
    def _():
        for a in range(group):
            gb_ref[a] = fold_diagonals(fold_ref[a])


def attention_specs(length, width, group, span, first):
    return (
        pl.BlockSpec((length, width), lambda h, m: (m, first + h)),
        pl.BlockSpec((length, 1), lambda h, m: (m, 0)),
        pl.BlockSpec((None, 1, length), lambda h, m: (m, 0, 0)),
        pl.BlockSpec((group, 1, span), lambda h, m: (first + h, 0, 0)),
    )


def attention(query, key, value, segment, rows, head_dim):
    micro_count, length = segment.shape
    model_width = query.shape[1]
    width = max(LANES, head_dim)
    group = width // head_dim
    block, segc, segr, line = attention_specs(length, width, group, rows.shape[2], 0)
    return pl.pallas_call(
        lambda *refs: forward_kernel(head_dim, *refs),
        name="attention_forward",
        grid=(model_width // width, micro_count),
        in_specs=[block, block, block, segc, segr, line],
        out_specs=block,
        out_shape=jax.ShapeDtypeStruct(query.shape, jnp.bfloat16),
        scratch_shapes=[pltpu.VMEM((group, LANES, rows.shape[2]), jnp.float32)],
    )(query, key, value, segment.reshape(-1, 1), segment[:, None, :], rows)


def attention_grads(query, key, value, grad, segment, rows, head_dim, part, parts, before):
    micro_count, length = segment.shape
    model_width = query.shape[1]
    width = max(LANES, head_dim)
    group = width // head_dim
    count = model_width // width // parts
    first = part * count
    block, segc, segr, line = attention_specs(length, width, group, rows.shape[2], first)
    flat = jax.ShapeDtypeStruct(query.shape, jnp.bfloat16)
    kept = len(before)

    def kernel(*refs):
        backward_kernel(head_dim, *refs[:7], *refs[7 + kept :])

    return pl.pallas_call(
        kernel,
        name="attention_backward",
        grid=(count, micro_count),
        in_specs=[block, block, block, block, segc, segr, line]
        + [pl.BlockSpec(memory_space=pl.ANY)] * kept,
        out_specs=[block, block, block, line],
        out_shape=[flat, flat, flat, jax.ShapeDtypeStruct(rows.shape, jnp.float32)],
        input_output_aliases={7 + n: n for n in range(kept)},
        scratch_shapes=[pltpu.VMEM((group, LANES, rows.shape[2]), jnp.float32)] * 2,
    )(query, key, value, grad, segment.reshape(-1, 1), segment[:, None, :], rows, *before)


def pack_small(gains, grad_rows, code):
    width = gains[0].shape[1]
    heads = grad_rows.shape[0]
    buckets = code.shape[0]
    lines = width // LANES

    def kernel(*refs):
        *gain_refs, rows_ref, code_ref, out_ref = refs
        out_ref[...] = jnp.zeros_like(out_ref)
        for n, ref in enumerate(gain_refs):
            for line in range(lines):
                at = n * lines + line
                out_ref[at : at + 1, :] = ref[:, line * LANES : (line + 1) * LANES]
        lane = lax.broadcasted_iota(jnp.int32, (buckets, LANES), 1)
        value = jnp.zeros((buckets, LANES), jnp.float32)
        for h in range(heads):
            part = jnp.sum(code_ref[...] * rows_ref[h], axis=1, keepdims=True)
            value = jnp.where(lane == h, part, value)
        out_ref[BIAS_AT : BIAS_AT + buckets, :] = value

    return pl.pallas_call(
        kernel,
        name="pack_small",
        out_shape=jax.ShapeDtypeStruct((width, LANES), jnp.float32),
    )(*gains, grad_rows, code)


class Net:
    def __init__(self):
        self.dp = lax.axis_size("dp")
        self.size = self.dp * lax.axis_size("tower")
        self.index = lax.axis_index("tower") * self.dp + lax.axis_index("dp")
        self.count = self.size.bit_length() - 1
        if self.count == 5:
            self.stages = (((0,), (0,)), ((4,), (1,)), ((1,), (4,)), ((2, 3), (2, 3)))
        else:
            self.stages = tuple(((b,), (b,)) for b in range(self.count))
        self.digits = [self.digit_of(stage) for stage in self.stages]

    def bit(self, b):
        return (self.index >> b) & 1

    def digit_of(self, stage):
        first, second = (sum(self.bit(b) << n for n, b in enumerate(bits)) for bits in stage)
        return first if stage[0] == stage[1] else jnp.where(self.bit(0) == 0, first, second)

    def swap(self, value, b):
        return lax.ppermute(value, AXES, [(i, i ^ (1 << b)) for i in range(self.size)])

    def peers(self, k):
        return range(1, 1 << len(self.stages[k][0]))

    def send(self, value, k, r):
        return self.send_by(value, self.stages[k], r)

    def send_by(self, value, stage, r):
        masks = [sum(((r >> n) & 1) << b for n, b in enumerate(bits)) for bits in stage]
        return lax.ppermute(value, AXES, [(i, i ^ masks[i & 1]) for i in range(self.size)])

    def collect(self, value, stage):
        peers = range(1, 1 << len(stage[0]))
        return place([value, *(self.send_by(value, stage, r) for r in peers)], self.digit_of(stage))


def place(pieces, digit):
    rows, width = pieces[0].shape
    source = lax.broadcasted_iota(jnp.int32, (len(pieces), rows, width), 0) ^ digit
    value = pieces[0][None]
    for r, piece in enumerate(pieces[1:], 1):
        value = jnp.where(source == r, piece[None], value)
    return value.reshape(len(pieces) * rows, width)


def part_of(value, which, count):
    rows = value.shape[0] // count
    return lax.dynamic_slice_in_dim(value, which * rows, rows, 0)


def weight_grads(bit, lefts, rights, extra=()):
    height = lefts[0].shape[1] // 2
    width = min(r.shape[1] for r in rights)
    rows = max(r for r in range(LANES, min(height, 512) + 1, LANES) if height % r == 0)
    stacks = height // rows
    ends = [sum(r.shape[1] for r in rights[: n + 1]) // width for n in range(len(rights))]
    starts = [end - r.shape[1] // width for end, r in zip(ends, rights)]
    columns = ends[-1]
    count = len(lefts)
    narrow = len(extra)
    total = columns * width + sum(v.shape[1] for v in extra)
    fresh = [n == 0 or lefts[n] is not lefts[n - 1] for n in range(count)]
    owners = [max(m for m in range(n + 1) if fresh[m]) for n in range(count)]

    def kernel(bit_ref, *refs):
        other_refs, own_refs, right_refs = (refs[n * count : (n + 1) * count] for n in range(3))
        extra_refs, refs = refs[3 * count : 3 * count + 2 * narrow], refs[3 * count + 2 * narrow :]
        sent_ref, kept_ref = refs[:2]
        turned_refs = refs[2:]
        column = pl.program_id(1)

        def one(n):
            if fresh[n]:

                @pl.when(column == starts[n])
                def _():
                    turned_refs[n][:rows] = other_refs[n][...].T
                    turned_refs[n][rows:] = own_refs[n][...].T

            value = dot_nn(turned_refs[owners[n]][...], right_refs[n][...])
            sent_ref[...] = value[:rows]
            kept_ref[...] = value[rows:]

        for n in range(count):
            pl.when((column >= starts[n]) & (column < ends[n]))(lambda n=n: one(n))

        if narrow:

            @pl.when(column == columns)
            def _():
                sent_ref[:, : extra[0].shape[1]] = extra_refs[0][...]
                kept_ref[:, : extra[0].shape[1]] = extra_refs[1][...]

    def row_place(side):
        def index(stack, column, bit_ref):
            half = jnp.where(side == 0, 1 - bit_ref[0], bit_ref[0])
            return half * stacks + stack

        return index

    def left_place(side):
        return lambda *at: (0, row_place(side)(*at))

    def extra_place(side):
        return lambda *at: (row_place(side)(*at), 0)

    def right_place(start, end):
        return lambda stack, column, bit_ref: (0, jnp.clip(column - start, 0, end - start - 1))

    return pl.pallas_call(
        kernel,
        name="weight_grads",
        grid_spec=pltpu.PrefetchScalarGridSpec(
            num_scalar_prefetch=1,
            grid=(stacks, columns + narrow),
            in_specs=[
                pl.BlockSpec((v.shape[0], rows), left_place(side)) for side in (0, 1) for v in lefts
            ]
            + [
                pl.BlockSpec((v.shape[0], width), right_place(start, end))
                for v, start, end in zip(rights, starts, ends)
            ]
            + [
                pl.BlockSpec((rows, v.shape[1]), extra_place(side)) for side in (0, 1) for v in extra
            ],
            out_specs=[pl.BlockSpec((rows, width), lambda stack, column, bit_ref: (stack, column))]
            * 2,
            scratch_shapes=[pltpu.VMEM((2 * rows, v.shape[0]), v.dtype) for v in lefts],
        ),
        out_shape=[jax.ShapeDtypeStruct((height, total), jnp.float32)] * 2,
    )(bit.reshape(1), *lefts, *lefts, *rights, *extra, *extra)


def row_tiles(rows):
    tile = min(rows, TILE)

    def lines(n):
        return pl.BlockSpec((tile, n), lambda t: (t, 0))

    def whole(*shape):
        return pl.BlockSpec(shape, lambda t: (0, 0))

    return tile, lines, whole


def norm_low(values, gain):
    scale = lax.rsqrt(jnp.mean(values * values, axis=1, keepdims=True) + norm_epsilon)
    return (values * scale * gain).astype(jnp.bfloat16)


def project_kernel(x_ref, gain_ref, wq_ref, wk_ref, wv_ref, n_ref, q_ref, k_ref, v_ref):
    normed = norm_low(x_ref[...].astype(jnp.float32), gain_ref[...])
    n_ref[...] = normed
    for weight, out in ((wq_ref, q_ref), (wk_ref, k_ref), (wv_ref, v_ref)):
        out[...] = dot_nn(normed, weight[...]).astype(jnp.bfloat16)


def project(states, gain, weights):
    rows, width = states.shape
    tile, lines, whole = row_tiles(rows)
    return pl.pallas_call(
        project_kernel,
        name="project",
        grid=(rows // tile,),
        in_specs=[lines(width), whole(1, width)] + [whole(width, width)] * 3,
        out_specs=[lines(width)] * 4,
        out_shape=[jax.ShapeDtypeStruct((rows, width), jnp.bfloat16)] * 4,
    )(states, gain[None], *weights)


def feed_kernel(
    mix_ref, x_ref, gain_ref, wout_ref, win_ref, wff_ref, hid_ref, n_ref, act_ref, y_ref
):
    hidden = x_ref[...].astype(jnp.float32) + dot_nn(mix_ref[...], wout_ref[...])
    hid_ref[...] = hidden
    normed = norm_low(hidden, gain_ref[...])
    n_ref[...] = normed
    activ = jnp.maximum(dot_nn(normed, win_ref[...]), 0.0).astype(jnp.bfloat16)
    act_ref[...] = activ
    y_ref[...] = hidden + dot_nn(activ, wff_ref[...])


def feed(mixed, states, gain, w_out, w_in, w_ffout):
    rows, width = states.shape
    inner = w_in.shape[1]
    tile, lines, whole = row_tiles(rows)
    return pl.pallas_call(
        feed_kernel,
        name="feed_forward",
        grid=(rows // tile,),
        in_specs=[
            lines(width),
            lines(width),
            whole(1, width),
            whole(width, width),
            whole(width, inner),
            whole(inner, width),
        ],
        out_specs=[lines(width), lines(width), lines(inner), lines(width)],
        out_shape=[
            jax.ShapeDtypeStruct((rows, width), jnp.float32),
            jax.ShapeDtypeStruct((rows, width), jnp.bfloat16),
            jax.ShapeDtypeStruct((rows, inner), jnp.bfloat16),
            jax.ShapeDtypeStruct((rows, width), jnp.float32),
        ],
    )(mixed, states, gain[None], w_out, w_in, w_ffout)


def norm_backward(values, grad, gain, sum_ref):
    scale = lax.rsqrt(jnp.mean(values * values, axis=1, keepdims=True) + norm_epsilon)
    unit = values * scale

    @pl.when(pl.program_id(0) == 0)
    def _():
        sum_ref[...] = jnp.zeros_like(sum_ref)

    sum_ref[...] += jnp.sum(grad * unit, axis=0, keepdims=True)
    scaled = grad * gain
    return scale * (scaled - unit * jnp.mean(unit * scaled, axis=1, keepdims=True))


def project_backward_kernel(
    gq_ref, gk_ref, gv_ref, gh_ref, x_ref, gain_ref, wq_ref, wk_ref, wv_ref, gx_ref, gg_ref
):
    grad = (
        dot_nt(gq_ref[...], wq_ref[...])
        + dot_nt(gk_ref[...], wk_ref[...])
        + dot_nt(gv_ref[...], wv_ref[...])
    )
    values = x_ref[...].astype(jnp.float32)
    gx_ref[...] = gh_ref[...] + norm_backward(values, grad, gain_ref[...], gg_ref)


def project_backward(grads, grad_hidden, states, gain, weights):
    rows, width = grad_hidden.shape
    tile, lines, whole = row_tiles(rows)
    return pl.pallas_call(
        project_backward_kernel,
        name="project_backward",
        grid=(rows // tile,),
        in_specs=[lines(width)] * 5 + [whole(1, width)] + [whole(width, width)] * 3,
        out_specs=[lines(width), whole(1, width)],
        out_shape=[
            jax.ShapeDtypeStruct((rows, width), jnp.float32),
            jax.ShapeDtypeStruct((1, width), jnp.float32),
        ],
    )(*grads, grad_hidden, states, gain[None], *weights)


def feed_backward_kernel(
    go_ref, act_ref, hid_ref, gain_ref, wff_ref, win_ref, wout_ref,
    gu_ref, gh_ref, ghl_ref, gm_ref, gg_ref,
):
    grad_output = go_ref[...]
    grad_activ = dot_nt(grad_output.astype(jnp.bfloat16), wff_ref[...])
    grad_inner = jnp.where(act_ref[...] > 0, grad_activ, 0.0).astype(jnp.bfloat16)
    gu_ref[...] = grad_inner
    grad_normed = dot_nt(grad_inner, win_ref[...])
    grad_hidden = grad_output + norm_backward(hid_ref[...], grad_normed, gain_ref[...], gg_ref)
    gh_ref[...] = grad_hidden
    low = grad_hidden.astype(jnp.bfloat16)
    ghl_ref[...] = low
    gm_ref[...] = dot_nt(low, wout_ref[...]).astype(jnp.bfloat16)


def feed_backward(grad_output, activ, hidden, gain, w_ffout, w_in, w_out):
    rows, width = grad_output.shape
    inner = activ.shape[1]
    tile, lines, whole = row_tiles(rows)
    return pl.pallas_call(
        feed_backward_kernel,
        name="feed_backward",
        grid=(rows // tile,),
        in_specs=[
            lines(width),
            lines(inner),
            lines(width),
            whole(1, width),
            whole(inner, width),
            whole(width, inner),
            whole(width, width),
        ],
        out_specs=[lines(inner), lines(width), lines(width), lines(width), whole(1, width)],
        out_shape=[
            jax.ShapeDtypeStruct((rows, inner), jnp.bfloat16),
            jax.ShapeDtypeStruct((rows, width), jnp.float32),
            jax.ShapeDtypeStruct((rows, width), jnp.bfloat16),
            jax.ShapeDtypeStruct((rows, width), jnp.bfloat16),
            jax.ShapeDtypeStruct((1, width), jnp.float32),
        ],
    )(grad_output, activ, hidden, gain[None], w_ffout, w_in, w_out)


def put(pieces, places, count, widths, before=()):
    rows, wide = pieces[0].shape
    splits = 1
    while splits < 4 and rows % (16 * splits) == 0 and rows // splits * wide > 320 * 1024:
        splits *= 2
    block = rows // splits
    number, kept = len(pieces), len(before)

    def kernel(places_ref, *refs):
        out_refs = refs[number + kept :]

        def copy(source):
            at = 0
            for out, width in zip(out_refs, widths):
                out[...] = source[:, at : at + width]
                at += width

        for n in range(number):
            pl.when(pl.program_id(0) // splits == n)(lambda n=n: copy(refs[n]))

    def source(n):
        return lambda step, places_ref: (jnp.clip(step - n * splits, 0, splits - 1), 0)

    def target(step, places_ref):
        return (places_ref[step // splits] * splits + step % splits, 0)

    return pl.pallas_call(
        kernel,
        name="put",
        grid_spec=pltpu.PrefetchScalarGridSpec(
            num_scalar_prefetch=1,
            grid=(number * splits,),
            in_specs=[pl.BlockSpec((block, wide), source(n)) for n in range(number)]
            + [pl.BlockSpec(memory_space=pl.ANY)] * kept,
            out_specs=[pl.BlockSpec((block, w), target) for w in widths],
        ),
        out_shape=[jax.ShapeDtypeStruct((count * rows, w), pieces[0].dtype) for w in widths],
        input_output_aliases={1 + number + n: n for n in range(kept)},
    )(jnp.stack(places), *pieces, *before)


def tie(*values):
    return lax.optimization_barrier(values)


class Sum:
    def __init__(self, net, lefts, rights, extra=()):
        self.net = net
        self.widths = [v.shape[1] for v in (*rights, *extra)]
        self.step = 0
        self.back = False
        self.done = False
        sent, kept = weight_grads(net.digits[0], lefts, rights, extra)
        self.held = [[sent], [kept]]
        self.cuts = [[]]

    def go(self):
        net = self.net
        if not self.back:
            self.got = [
                net.send(v, self.step, r) for r, v in zip(net.peers(self.step), self.held[0])
            ]
            return
        (piece,) = self.held
        k = self.step - 1
        self.got = [net.send(piece, k, r) for r in net.peers(k)]
        self.whole = piece.shape[0] % 8 == 0 and len(self.got) == 1
        if self.whole:
            widths = [piece.shape[1]] if k else self.widths
            self.base = put([piece], [net.digits[k]], len(self.got) + 1, widths)

    def end(self):
        net = self.net
        if self.back:
            self.step -= 1
            k = self.step
            self.done = k == 0
            digit, peers = net.digits[k], net.peers(k)
            if self.whole:
                widths = self.widths if self.done else [self.held[0].shape[1]]
                self.held = put(
                    self.got, [digit ^ r for r in peers], len(peers) + 1, widths, self.base
                )
            else:
                self.held = [place([self.held[0], *self.got], digit)]
                if self.done:
                    ends = [sum(self.widths[: n + 1]) for n in range(len(self.widths))]
                    self.held = [
                        self.held[0][:, end - width : end] for end, width in zip(ends, self.widths)
                    ]
            return
        terms = [*self.held[1], *self.got]
        self.cuts += [[] for _ in self.got]
        self.step += 1
        self.back = self.step == len(net.stages)

        def total(more):
            value = None
            for term, cuts in zip(terms, self.cuts):
                for which, count in cuts + more:
                    term = part_of(term, which, count)
                value = term if value is None else value + term
            return value

        if self.back:
            self.held = [total([])]
            return
        digit, peers = net.digits[self.step], net.peers(self.step)
        count = len(peers) + 1
        self.held = [[total([(digit ^ r, count)]) for r in peers], terms]
        for cuts in self.cuts:
            cuts.append((digit, count))


def tie_all(sums, *values):
    values, held = tie(values, [s.held for s in sums])
    for s, h in zip(sums, held):
        s.held = h
    return values


def advance(sums):
    for s in sums:
        s.go()
    for s in sums:
        s.end()


def local(
    states,
    segment_ids,
    lengths,
    positives,
    w_query,
    w_key,
    w_value,
    w_out,
    w_in,
    w_ffout,
    w_proj,
    gain_attn,
    gain_ffn,
    gain_final,
    rel_bias,
):
    micro_count = states.shape[1]
    length = states.shape[2]
    model_width = states.shape[3]
    item_count = lengths.shape[2]
    bucket_count, head_count = rel_bias.shape
    head_dim = model_width // head_count
    ff_width = w_in.shape[1]
    tower_index = lax.axis_index("tower")
    dp_index = lax.axis_index("dp")
    dp_count = lax.axis_size("dp")
    row_count = item_count * dp_count
    rows = micro_count * length
    net = Net()
    bits = net.count

    offset = jnp.arange(2 * length, dtype=jnp.int32) - length
    code = bucket_code(offset, bucket_count)
    code_back = bucket_code(-offset, bucket_count)

    def bias_rows(which):
        return jnp.dot(which, rel_bias, precision=highest).T[:, None, :]

    segment = segment_ids[0]

    states_low = states[0].reshape(rows, model_width)
    normed_low, query_low, key_low, value_low = project(
        states_low, gain_attn, (w_query, w_key, w_value)
    )
    mixed_low = attention(query_low, key_low, value_low, segment, bias_rows(code), head_dim)
    hidden = states_low.astype(jnp.float32) + mm(mixed_low, w_out)
    normed_two = rms_scale(hidden, gain_ffn)
    normed_two_low = normed_two.astype(jnp.bfloat16)
    activ_low = jnp.maximum(mm(normed_two_low, w_in), 0.0).astype(jnp.bfloat16)
    output = hidden + mm(activ_low, w_ffout)
    final_norm, back_final = jax.vjp(rms_scale, output, gain_final)
    member = (segment[:, :, None] == jnp.arange(item_count, dtype=jnp.int32)).astype(jnp.float32)
    count_f = lengths[0].astype(jnp.float32)[:, :, None]
    pooled_low = (
        jnp.einsum(
            "btc,btf->bcf",
            member,
            final_norm.reshape(micro_count, length, model_width),
            precision=highest,
        )
        / count_f
    ).astype(jnp.bfloat16)
    pooled_flat = pooled_low.reshape(micro_count * item_count, model_width)
    embed = mm(pooled_flat, w_proj)
    unit_embed, back_unit = jax.vjp(unit_rows, embed)

    every = unit_embed
    if bits == 5:
        for k in (3, 1, 2):
            every = net.collect(every, net.stages[k])
        every = every.reshape(2, 2, -1, model_width)
        every = jnp.where(net.bit(0) == 0, jnp.swapaxes(every, 0, 1), every)
        every = net.collect(every.reshape(-1, model_width), net.stages[0])
        every = every.reshape(2, 2, 2, -1, micro_count, item_count, model_width)
        every = jnp.transpose(every, (4, 1, 3, 2, 0, 5, 6))
    else:
        for b in range(bits):
            every = net.collect(every, ((b,), (b,)))
        every = every.reshape(2, net.dp, micro_count, item_count, model_width)
        every = jnp.transpose(every, (2, 0, 1, 3, 4))
    every = every.reshape(micro_count, 2, row_count, model_width)
    queries_all = every[:, 0]
    passages_all = every[:, 1]
    columns = jnp.arange(row_count, dtype=jnp.int32)[None, :]
    loss_sum = jnp.zeros((), jnp.float32)
    grad_embed = []
    for m in range(micro_count):
        logits = logit_scale * jnp.dot(queries_all[m], passages_all[m].T, precision=highest)
        target_hot = (columns == positives[m][:, None]).astype(jnp.float32)
        loss_part, grad_logits = softmax_terms(logits, target_hot)
        loss_sum = loss_sum + loss_part
        own_rows = lax.dynamic_slice_in_dim(grad_logits, dp_index * item_count, item_count, 0)
        own_cols = lax.dynamic_slice_in_dim(grad_logits, dp_index * item_count, item_count, 1)
        own = jnp.where(tower_index == 0, own_rows, own_cols.T)
        others = jnp.where(tower_index == 0, passages_all[m], queries_all[m])
        grad_embed.append(logit_scale * jnp.dot(own, others, precision=highest))
    grad_embed = jnp.concatenate(grad_embed, axis=0)
    (grad_e,) = back_unit(grad_embed)
    grad_e_low = grad_e.astype(jnp.bfloat16)
    grad_pooled = mm_t(grad_e_low, w_proj).reshape(micro_count, item_count, model_width)
    grad_final_norm = jnp.einsum(
        "btc,bcf->btf", member, grad_pooled / count_f, precision=highest
    ).reshape(rows, model_width)
    grad_output, grad_gain_final = back_final(grad_final_norm)
    grad_output_low = grad_output.astype(jnp.bfloat16)

    first = Sum(net, [activ_low], [grad_output_low])
    (grad_output,) = tie_all([first], grad_output)
    first.go()
    grad_inner_low, grad_hidden, grad_hidden_low, grad_mixed, grad_gain_ffn = feed_backward(
        grad_output, activ_low, hidden, gain_ffn, w_ffout, w_in, w_out
    )
    first.end()
    grad_inner_low, grad_hidden_low, grad_mixed = tie_all(
        [first], grad_inner_low, grad_hidden_low, grad_mixed
    )
    first.go()
    parts = 3
    rows_back = bias_rows(code_back)

    def attention_part(part, query, before):
        return attention_grads(
            query, key_low, value_low, grad_mixed, segment, rows_back, head_dim, part, parts, before
        )

    grads = attention_part(0, query_low, ())
    second = Sum(
        net,
        [normed_two_low, mixed_low, pooled_flat],
        [grad_inner_low, grad_hidden_low, grad_e_low],
    )
    first.end()
    query_low, grads = tie_all([first, second], query_low, grads)
    first.go()
    second.go()
    grads = attention_part(1, query_low, grads)
    first.end()
    second.end()
    query_low, grads = tie_all([first, second], query_low, grads)
    first.go()
    second.go()
    grads = attention_part(2, query_low, grads)
    *grad_heads, grad_rows = grads
    grad_states, grad_gain_attn = project_backward(
        grad_heads,
        grad_hidden,
        states_low,
        gain_attn,
        (w_query, w_key, w_value),
    )
    small = pack_small(
        (grad_gain_attn, grad_gain_ffn, grad_gain_final[None]), grad_rows, code_back.T
    )
    third = Sum(net, [normed_low] * 3, grad_heads, [small])
    first.end()
    second.end()
    sums = [first, second, third]
    (grad_states,) = tie_all(sums, grad_states)
    if bits == 5:
        for _ in range(3):
            advance(sums)
            tie_all(sums)
        for s in sums:
            s.go()
        second.end()
        third.end()
        second.held, third.held, first.base = tie(second.held, third.held, first.base)
        second.go()
        third.go()
        first.end()
        third.end()
        first.held, third.held = tie(first.held, third.held)
        third.go()
        second.end()
        third.end()
        tie_all([second, third])
        third.go()
        second.go()
        second.end()
        second.held, third.base = tie(second.held, third.base)
        third.end()
        tie_all([second, third])
        advance([third])
    else:
        while not all(s.done for s in sums):
            advance([s for s in sums if not s.done])
    (whole_ffout,) = first.held
    whole_in, whole_out, whole_proj = second.held
    whole_query, whole_key, whole_value, small = third.held
    lines = model_width // LANES
    loss = loss_sum / (micro_count * row_count)
    return (
        loss,
        unit_embed.reshape(1, micro_count, item_count, model_width),
        grad_states.reshape(1, micro_count, length, model_width),
        whole_query,
        whole_key,
        whole_value,
        whole_out,
        whole_in,
        whole_ffout,
        whole_proj,
        *(small[n * lines : (n + 1) * lines].reshape(-1) for n in range(3)),
        small[BIAS_AT : BIAS_AT + bucket_count, :head_count],
    )


def solution(mesh):
    return jax.shard_map(
        local,
        mesh=mesh,
        in_specs=(
            P("tower", None, "dp", None),
            P("tower", None, "dp"),
            P("tower", None, "dp"),
        )
        + (P(),) * 12,
        out_specs=(P(), P("tower", None, "dp", None), P("tower", None, "dp", None)) + (P(),) * 11,
        check_vma=False,
    )
```
